128 devices in a mesh: grp: 8 (over z, core), tok: 16 (over y, x).
Axes of the slice: x: 4, y: 4, z: 4, core: 2. Of those that a mesh axis runs over, the one named last changes fastest.
Arguments:
- guess_symbol_ids: int32 [4096], replicated, may hold values from 0 to 32767
- symbol_vector_lookup: bfloat16 [32768, 4096], P('tok', 'grp'), may hold values from -6 to 6
- prior_attention_normed: bfloat16 [256, 4096], P('tok', 'grp'), may hold values from -6 to 6
- prior_feedforward_normed: bfloat16 [256, 4096], P('tok', 'grp'), may hold values from -6 to 6
- layernorm_scales: float32 [3, 4096], replicated, may hold values from 0.25 to 1.75
- lagged_blend_ratios: float32 [7, 4096], replicated, may hold values from 0.05 to 0.95
- attention_matrices: bfloat16 [4, 4096, 4096], P(None, None, 'grp'), may hold values from -0.09375 to 0.09375
- forgetting_baseline_vector: float32 [4096], replicated, may hold values from -6 to -0.5
- forgetting_narrow_matrix: bfloat16 [4096, 128], replicated, may hold values from -0.09375 to 0.09375
- forgetting_widen_matrix: bfloat16 [128, 4096], P(None, 'grp'), may hold values from -0.5 to 0.5
- diagonal_boost: float32 [4096], replicated, may hold values from -3 to 3
- attention_result_matrix: bfloat16 [4096, 4096], P('grp', 'tok'), may hold values from -0.09375 to 0.09375
- feedforward_lookup_matrix: bfloat16 [4096, 7168], P('tok', 'grp'), may hold values from -0.09375 to 0.09375
- feedforward_content_matrix: bfloat16 [7168, 4096], P('grp', 'tok'), may hold values from -0.0625 to 0.0625
- feedforward_gating_matrix: bfloat16 [4096, 4096], P('tok', 'grp'), may hold values from -0.09375 to 0.09375
- memory_matrix_store: float32 [256, 64, 4096], P('tok', 'grp'), may hold values from -6 to 6
- query_memory_slot: int32 [128], replicated, may hold values from 0 to 255, as said below
- candidate_tally_each_query: int32 [16, 8], replicated, may hold values from 1 to 4, 16 in all within a row
- kept_guess_tally: int32 [256], P('tok'), may hold values from 0 to 16
Outputs:
- layer_out: bfloat16 [4096, 4096], P('tok', 'grp')
- shift_att_out: bfloat16 [256, 4096], P('tok', 'grp')
- shift_ffn_out: bfloat16 [256, 4096], P('tok', 'grp')
- store_out: float32 [256, 64, 4096], P('tok', 'grp')
The draws below stay inside these ranges and needn't reach their ends.
Inputs may be any that keep to these rules, and one draw needn't show every extreme that they name: `query_memory_slot`: pages of different requests differ. Page p lies on tok index p // 16, slot p % 16. The 8 requests r * 8 onward, whose branches are branches r * 16 onward, have pages on pairwise different tok indices. `candidate_tally_each_query`: row r holds the branch counts of requests r * 8 onward, in order; each row sums to 16.
All inputs are finite; a program needn't handle non-finite values.
Results may differ from the reference program's by a relative error of at most 0.02.
Values may be sent and summed in bfloat16 or wider, within the bound.
A program may use at most 192 MiB of HBM per device.

```python
import math
import jax
import jax.numpy as jnp
import numpy as np
from jax import lax

HIDDEN_BREADTH = 4096
ATTENTION_PARTS = 64
PART_BREADTH = 64
FFW = 7168
VW = 32768
DECAY_RANK = 128
GUESS_SYMBOLS = 16
BR_DEV = 16
REQ_DEV = 8
MOST_BR = 4
BRANCHES = 256
REQUESTS = 128
TOKENS = 4096
SLOTS = 16
PAGES = 256


def draw_query_memory_slot(key, part):
    groups = REQUESTS // REQ_DEV
    key_one, key_two, key_three = jax.random.split(key, 3)
    parity = jax.random.randint(key_one, (), 0, 2)
    offsets = 2 * jax.random.permutation(key_two, REQ_DEV).astype(jnp.int32) + parity
    relabel = jax.random.permutation(key_three, groups).astype(jnp.int32)
    row_ids = jnp.arange(groups, dtype=jnp.int32)[:, None]
    col_ids = jnp.arange(REQ_DEV, dtype=jnp.int32)[None, :]
    spot = (row_ids - row_ids % 2 + offsets[None, :]) % groups
    owner = relabel[spot]
    slot_ids = 2 * col_ids + row_ids % 2
    return (owner * SLOTS + slot_ids).reshape(-1).astype(jnp.int32)


def set_ends(values, own_key, low, high):
    shape = values.shape
    place = [jax.random.randint(jax.random.fold_in(own_key, axis), (), 0, shape[axis]) for axis in range(len(shape))]
    values = values.at[tuple(place)].set(low)
    longest = shape.index(max(shape))
    place[longest] = (place[longest] + 1) % shape[longest]
    return values.at[tuple(place)].set(high)


def level_of(own_key, shape, cuts, least, high):
    factor_of = 1.0
    for dim, blocks in cuts:
        heights = jax.random.uniform(jax.random.fold_in(jax.random.fold_in(own_key, 6), dim), (blocks,), jnp.float32, least / len(cuts), high / len(cuts))
        factor_of = factor_of * jnp.repeat(jnp.exp(heights), shape[dim] // blocks).reshape((-1,) + (1,) * (len(shape) - 1 - dim))
    return factor_of


def cumulative_ranks(count, slope):
    portions = [(1 << 20) // math.isqrt(grade ** slope) + 1 for grade in range(1, count + 1)]
    width = 1 + sum(portions) // (1 << 30)
    return np.cumsum(np.array([max(1, weight // width) for weight in portions]))


def ranked_ids(stream_key, shape, amount, slope):
    listing = cumulative_ranks(amount, slope)
    lot = jax.random.randint(jax.random.fold_in(stream_key, 1), shape, 0, int(listing[amount - 1]))
    grade = jnp.searchsorted(jnp.asarray(listing, jnp.int32), lot, side="right")
    return jax.random.permutation(jax.random.fold_in(stream_key, 2), amount)[grade].astype(jnp.int32)


def split_up(count, total, reach, lean):
    portions = [(1 << 20) // math.isqrt(rank ** lean) + 1 for rank in range(2, count + 1)]
    spare, holding = total - reach - (count - 1), [1] * (count - 1)
    while spare > 0:
        free = [i for i in range(count - 1) if holding[i] < reach]
        pool, budget = sum([portions[i] for i in free]), spare
        for i in free:
            more = min(reach - holding[i], max(1, budget * portions[i] // pool), spare)
            holding[i] = holding[i] + more
            spare = spare - more
    return np.array([reach] + holding)


def ragged_sizes(rng, amount, total, bound, skew):
    if amount == 2:
        one = jax.random.randint(rng, (), max(1, total - bound), min(bound, total - 1) + 1)
        return jnp.stack([one, total - one])
    sizes = jnp.asarray(split_up(amount, total, bound, skew), jnp.int32)
    couples = (amount - 1) // 2
    giver, taker = sizes[1:1 + 2 * couples:2], sizes[2:2 + 2 * couples:2]
    room = jnp.minimum(giver - 1, bound - taker)
    passed = jax.random.randint(jax.random.fold_in(rng, 1), (couples,), 0, 1 << 20) % (room + 1)
    sizes = sizes.at[1:1 + 2 * couples:2].set(giver - passed).at[2:2 + 2 * couples:2].set(taker + passed)
    return sizes[jax.random.permutation(jax.random.fold_in(rng, 2), amount)]


def scatter_about(own_key, shape, width, reach, cuts=(), held_as=jnp.bfloat16):
    entries = width * jax.random.normal(own_key, shape, jnp.float32)
    if cuts:
        entries = entries * level_of(own_key, shape, cuts, -0.22, 0.18)
    return jnp.clip(entries, -reach, reach).astype(held_as)


def setup_inputs(seed: int = 0) -> dict:
    seeds = jax.random.split(jax.random.key(seed), 20)
    guess_symbol_ids = set_ends(ranked_ids(seeds[0], (TOKENS,), VW, 2), jax.random.fold_in(seeds[0], 3), 0, VW - 1).astype(jnp.int32)
    symbol_vector_lookup = scatter_about(seeds[1], (VW, HIDDEN_BREADTH), 1.0, 6.0, ((0, 16), (1, 8)))
    prior_attention_normed = scatter_about(seeds[2], (BRANCHES, HIDDEN_BREADTH), 1.0, 6.0, ((0, 16), (1, 8)))
    prior_feedforward_normed = scatter_about(seeds[3], (BRANCHES, HIDDEN_BREADTH), 1.0, 6.0, ((0, 16), (1, 8)))
    layernorm_scales = jnp.clip(1.0 + 0.15 * jax.random.normal(seeds[4], (3, HIDDEN_BREADTH), jnp.float32), 0.25, 1.75)
    lagged_blend_ratios = jnp.clip(jax.random.uniform(seeds[5], (7, HIDDEN_BREADTH), jnp.float32, 0.05, 0.95), 0.05, 0.95)
    attention_matrices = scatter_about(seeds[6], (4, HIDDEN_BREADTH, HIDDEN_BREADTH), HIDDEN_BREADTH ** -0.5, 0.09375, ((2, 8),))
    forgetting_baseline_vector = jnp.clip(jax.random.uniform(seeds[7], (HIDDEN_BREADTH,), jnp.float32, -6.0, -0.5), -6.0, -0.5)
    forgetting_narrow_matrix = scatter_about(seeds[8], (HIDDEN_BREADTH, DECAY_RANK), HIDDEN_BREADTH ** -0.5, 0.09375)
    forgetting_widen_matrix = scatter_about(seeds[9], (DECAY_RANK, HIDDEN_BREADTH), DECAY_RANK ** -0.5, 0.5, ((1, 8),))
    diagonal_boost = scatter_about(seeds[10], (HIDDEN_BREADTH,), 0.5, 3.0, (), jnp.float32)
    attention_result_matrix = scatter_about(seeds[11], (HIDDEN_BREADTH, HIDDEN_BREADTH), HIDDEN_BREADTH ** -0.5, 0.09375, ((0, 8), (1, 16)))
    feedforward_lookup_matrix = scatter_about(seeds[12], (HIDDEN_BREADTH, FFW), HIDDEN_BREADTH ** -0.5, 0.09375, ((0, 16), (1, 8)))
    feedforward_content_matrix = scatter_about(seeds[13], (FFW, HIDDEN_BREADTH), FFW ** -0.5, 0.0625, ((0, 8), (1, 16)))
    feedforward_gating_matrix = scatter_about(seeds[14], (HIDDEN_BREADTH, HIDDEN_BREADTH), HIDDEN_BREADTH ** -0.5, 0.09375, ((0, 16), (1, 8)))
    memory_matrix_store = scatter_about(seeds[15], (PAGES, ATTENTION_PARTS, PART_BREADTH * PART_BREADTH), 1.0, 6.0, ((0, 16), (1, 8)), jnp.float32)
    query_memory_slot = draw_query_memory_slot(jax.random.fold_in(seeds[19], 71), 0)
    candidate_tally_each_query = jax.vmap(lambda own: ragged_sizes(own, REQ_DEV, BR_DEV, MOST_BR, 2))(jax.random.split(seeds[17], (REQUESTS // REQ_DEV))).reshape((REQUESTS // REQ_DEV, REQ_DEV)).astype(jnp.int32)
    kept_guess_tally = set_ends(jax.random.randint(seeds[18], (BRANCHES,), 0, GUESS_SYMBOLS + 1), jax.random.fold_in(seeds[18], 1), 0, GUESS_SYMBOLS).astype(jnp.int32)
    return dict(guess_symbol_ids=guess_symbol_ids, symbol_vector_lookup=symbol_vector_lookup, prior_attention_normed=prior_attention_normed, prior_feedforward_normed=prior_feedforward_normed, layernorm_scales=layernorm_scales, lagged_blend_ratios=lagged_blend_ratios, attention_matrices=attention_matrices, forgetting_baseline_vector=forgetting_baseline_vector, forgetting_narrow_matrix=forgetting_narrow_matrix, forgetting_widen_matrix=forgetting_widen_matrix, diagonal_boost=diagonal_boost, attention_result_matrix=attention_result_matrix, feedforward_lookup_matrix=feedforward_lookup_matrix, feedforward_content_matrix=feedforward_content_matrix, feedforward_gating_matrix=feedforward_gating_matrix, memory_matrix_store=memory_matrix_store, query_memory_slot=query_memory_slot, candidate_tally_each_query=candidate_tally_each_query, kept_guess_tally=kept_guess_tally)


EPSILON = 1e-05
HEAD_EPSILON = 0.00064

def normalize(tensor, gain_row, eps_value):
    row_mean = lax.optimization_barrier(jnp.mean(tensor, axis=-1, keepdims=True))
    centered = tensor - row_mean
    spread = lax.optimization_barrier(jnp.mean(centered * centered, axis=-1, keepdims=True))
    return centered * lax.rsqrt(spread + eps_value) * gain_row

def shifted(normed, carried):
    return jnp.concatenate([carried.astype(jnp.float32)[:, None, :], normed[:, :-1, :]], axis=1)

def mix_input(normed, before, coeff):
    return (normed + (before - normed) * coeff).reshape(-1, normed.shape[-1]).astype(jnp.bfloat16)

def memory_matrix_sweep(gating_vectors, lookup_vectors, content_vectors, forgetting_multiplier, extra_head_rows, initial_memory_matrix, accepted_count, draft_length):

    def scan_step(carry_state, inputs):
        wkv_state, chosen_candidate = carry_state
        current_receptance, current_key, current_value, decay_now, step_index = inputs
        current_token_term = lax.optimization_barrier(jnp.sum(current_receptance * extra_head_rows * current_key, axis=-1, keepdims=True)) * current_value
        head_out = jnp.einsum('bhi,bhij->bhj', current_receptance, wkv_state, precision=lax.Precision.HIGHEST) + current_token_term
        wkv_state = decay_now[..., None] * wkv_state + current_key[..., None] * current_value[..., None, :]
        chosen_candidate = jnp.where((accepted_count == step_index + 1)[:, None, None, None], wkv_state, chosen_candidate)
        return ((wkv_state, chosen_candidate), head_out)
    step_ids = jnp.arange(draft_length, dtype=jnp.int32)
    (final_state, chosen_candidate), attention_part_results = lax.scan(scan_step, (initial_memory_matrix, initial_memory_matrix), (gating_vectors, lookup_vectors, content_vectors, forgetting_multiplier, step_ids))
    return (attention_part_results, chosen_candidate)

def keep_shift(normed, carried, kept_guess_tally):
    last_index = jnp.maximum(kept_guess_tally - 1, 0).astype(jnp.int32)
    picked = jnp.take_along_axis(normed, last_index[:, None, None], axis=1)[:, 0]
    return jnp.where((kept_guess_tally > 0)[:, None], picked, carried.astype(jnp.float32)).astype(jnp.bfloat16)

def reference(guess_symbol_ids, symbol_vector_lookup, prior_attention_normed, prior_feedforward_normed, layernorm_scales, lagged_blend_ratios, attention_matrices, forgetting_baseline_vector, forgetting_narrow_matrix, forgetting_widen_matrix, diagonal_boost, attention_result_matrix, feedforward_lookup_matrix, feedforward_content_matrix, feedforward_gating_matrix, memory_matrix_store, query_memory_slot, candidate_tally_each_query, kept_guess_tally):
    embedded = jnp.take(symbol_vector_lookup, guess_symbol_ids, axis=0)
    base_values = embedded.astype(jnp.float32)
    normed = normalize(base_values, layernorm_scales[0], EPSILON).reshape(BRANCHES, GUESS_SYMBOLS, HIDDEN_BREADTH)
    before = shifted(normed, prior_attention_normed)

    def project(index, weight):
        return jnp.dot(mix_input(normed, before, lagged_blend_ratios[index]), weight, preferred_element_type=jnp.float32)
    gating_vectors = project(0, attention_matrices[0])
    lookup_vectors = project(1, attention_matrices[1])
    content_vectors = project(2, attention_matrices[2])
    gate_proj = jax.nn.silu(project(3, attention_matrices[3]))
    lowrank = jnp.tanh(project(4, forgetting_narrow_matrix)).astype(jnp.bfloat16)
    forgetting_multiplier = jnp.exp(-jnp.exp(forgetting_baseline_vector + jnp.dot(lowrank, forgetting_widen_matrix, preferred_element_type=jnp.float32)))

    def divide_among_parts(tensor):
        return tensor.reshape(BRANCHES, GUESS_SYMBOLS, ATTENTION_PARTS, PART_BREADTH).transpose(1, 0, 2, 3)
    branch_totals = candidate_tally_each_query.reshape(-1)
    request_ends = jnp.cumsum(branch_totals)
    branch_ids = jnp.arange(BRANCHES, dtype=jnp.int32)
    request_of = lax.optimization_barrier(jnp.sum((request_ends[None, :] <= branch_ids[:, None]).astype(jnp.int32), axis=1)).astype(jnp.int32)
    initial_memory_matrix = jnp.take(memory_matrix_store, jnp.take(query_memory_slot, request_of), axis=0).reshape(BRANCHES, ATTENTION_PARTS, PART_BREADTH, PART_BREADTH)
    attention_part_results, chosen_candidate = memory_matrix_sweep(divide_among_parts(gating_vectors), divide_among_parts(lookup_vectors), divide_among_parts(content_vectors), divide_among_parts(forgetting_multiplier), diagonal_boost.reshape(ATTENTION_PARTS, PART_BREADTH), initial_memory_matrix, kept_guess_tally, GUESS_SYMBOLS)
    head_normed = normalize(attention_part_results, layernorm_scales[2].reshape(ATTENTION_PARTS, PART_BREADTH), HEAD_EPSILON).transpose(1, 0, 2, 3).reshape(TOKENS, HIDDEN_BREADTH)
    attended = (head_normed * gate_proj).astype(jnp.bfloat16)
    residual = (base_values + jnp.dot(attended, attention_result_matrix, preferred_element_type=jnp.float32)).astype(jnp.bfloat16)
    residual_values = residual.astype(jnp.float32)
    normed2 = normalize(residual_values, layernorm_scales[1], EPSILON).reshape(BRANCHES, GUESS_SYMBOLS, HIDDEN_BREADTH)
    before2 = shifted(normed2, prior_feedforward_normed)
    key_in = mix_input(normed2, before2, lagged_blend_ratios[5])
    rec_in = mix_input(normed2, before2, lagged_blend_ratios[6])
    hidden = jnp.square(jax.nn.relu(jnp.dot(key_in, feedforward_lookup_matrix, preferred_element_type=jnp.float32))).astype(jnp.bfloat16)
    gate_two = jax.nn.sigmoid(jnp.dot(rec_in, feedforward_gating_matrix, preferred_element_type=jnp.float32))
    layer_out = (residual_values + gate_two * jnp.dot(hidden, feedforward_content_matrix, preferred_element_type=jnp.float32)).astype(jnp.bfloat16)
    shift_att_out = keep_shift(normed, prior_attention_normed, kept_guess_tally)
    shift_ffn_out = keep_shift(normed2, prior_feedforward_normed, kept_guess_tally)
    branch_score = kept_guess_tally * BRANCHES + (BRANCHES - 1 - branch_ids)
    member = request_of[None, :] == jnp.arange(REQUESTS, dtype=jnp.int32)[:, None]
    best_score = lax.optimization_barrier(jnp.max(jnp.where(member, branch_score[None, :], -1), axis=1))
    winner = (BRANCHES - 1 - best_score % BRANCHES).astype(jnp.int32)
    new_pages = jnp.take(chosen_candidate, winner, axis=0).reshape(REQUESTS, ATTENTION_PARTS, PART_BREADTH * PART_BREADTH)
    store_out = memory_matrix_store.at[query_memory_slot].set(new_pages)
    return (layer_out, shift_att_out, shift_ffn_out, store_out)
```

```python
import functools

import jax
import jax.numpy as jnp
from jax import lax
from jax.experimental import pallas as pl
from jax.experimental.pallas import tpu as pltpu
from jax.sharding import PartitionSpec as P

HIDDEN = 4096
HEAD = 64
DRAFT = 16
BRANCH = 16
ROWS = BRANCH * DRAFT
WIDTH = 512
TOK = 16
GRP = 8
REQ = 8
PAIRS = 4
KEYS = 896
EPSILON = 1e-05
HEAD_EPSILON = 0.00064
F32 = jnp.float32
BF16 = jnp.bfloat16
MESH = pl.DeviceIdType.MESH
ANY = pl.BlockSpec(memory_space=pl.ANY)
VMEM = pl.BlockSpec(memory_space=pltpu.VMEM)


def remote(src, dst, send, recv, device):
    return pltpu.make_async_remote_copy(
        src_ref=src, dst_ref=dst, send_sem=send, recv_sem=recv, device_id=device, device_id_type=MESH
    )


def greet(devices):
    barrier = pltpu.get_barrier_semaphore()
    for device in devices:
        pl.semaphore_signal(barrier, inc=1, device_id=device, device_id_type=MESH)
    pl.semaphore_wait(barrier, len(devices))


def grp_places():
    g = lax.axis_index("grp")
    z, core = g // 2, g % 2
    up = lax.rem(z + 1, 4) * 2 + core
    down = lax.rem(z + 3, 4) * 2 + core
    far = lax.rem(z + 2, 4) * 2 + core
    mate = z * 2 + 1 - core
    return g, up, down, far, mate


def block_of(g):
    return pl.ds(pl.multiple_of(g * WIDTH, WIDTH), WIDTH)


def flip(g):
    return g + 1 - 2 * lax.rem(g, 2)


def gather_grp(own, out, send, recv, local):
    rows = out.shape[0]
    half = rows // 2
    g, up, down, far, mate = grp_places()
    first, last, whole = pl.ds(0, half), pl.ds(half, rows - half), pl.ds(0, rows)
    at = lambda part, g_of: out.at[part, block_of(g_of)]
    keep = pltpu.make_async_copy(own, at(whole, g), local)
    keep.start()
    started = []

    def go(index, src, part, g_of, target):
        copy = remote(src, at(part, g_of), send.at[index], recv.at[index], {"grp": target})
        copy.start()
        started.append(copy)

    def came(index, part, g_of):
        remote(at(part, g_of), at(part, g_of), send.at[index], recv.at[index], {"grp": mate}).wait_recv()

    go(0, own, whole, g, up)
    go(1, own, whole, g, down)
    go(2, own, whole, g, mate)
    came(0, whole, down)
    go(3, at(first, down), first, down, up)
    go(5, at(whole, down), whole, down, mate)
    came(1, whole, up)
    go(4, at(last, up), last, up, down)
    go(6, at(whole, up), whole, up, mate)
    came(3, first, far)
    go(7, at(first, far), first, far, mate)
    came(4, last, far)
    go(8, at(last, far), last, far, mate)
    came(2, whole, mate)
    came(5, whole, flip(down))
    came(6, whole, flip(up))
    came(7, first, flip(far))
    came(8, last, flip(far))
    keep.wait()
    for copy in started:
        copy.wait_send()


def reduce_grp(part, mated, sums, halves, full, send, recv):
    g, up, down, far, mate = grp_places()
    half = ROWS // 2
    started = []

    def go(index, src, dst, target):
        copy = remote(src, dst, send.at[index], recv.at[index], {"grp": target})
        copy.start()
        started.append(copy)

    def came(index, dst):
        remote(dst, dst, send.at[index], recv.at[index], {"grp": mate}).wait_recv()

    order = (far, up, down, g)
    for k in range(4):
        go(k, part.at[:, block_of(flip(order[k]))], mated.at[k], mate)

    def own(k):
        return part[:, block_of(order[k])].astype(F32) + mated[k].astype(F32)

    came(0, mated.at[0])
    sums[0] = own(0).astype(BF16)
    go(4, sums.at[0, pl.ds(0, half)], halves.at[0], up)
    go(5, sums.at[0, pl.ds(half, half)], halves.at[1], down)
    came(1, mated.at[1])
    came(4, halves.at[0])
    sums[1, :half] = (own(1)[:half] + halves[0].astype(F32)).astype(BF16)
    sums[1, half:] = own(1)[half:].astype(BF16)
    go(6, sums.at[1], full.at[0], up)
    came(2, mated.at[2])
    came(5, halves.at[1])
    sums[2, :half] = own(2)[:half].astype(BF16)
    sums[2, half:] = (own(2)[half:] + halves[1].astype(F32)).astype(BF16)
    go(7, sums.at[2], full.at[1], down)
    came(3, mated.at[3])
    came(6, full.at[0])
    came(7, full.at[1])
    total = own(3) + full[0].astype(F32) + full[1].astype(F32)
    for copy in started:
        copy.wait_send()
    return total


REDUCE_SCRATCH = [
    pltpu.VMEM((4, ROWS, WIDTH), BF16),
    pltpu.VMEM((3, ROWS, WIDTH), BF16),
    pltpu.VMEM((2, ROWS // 2, WIDTH), BF16),
    pltpu.VMEM((2, ROWS, WIDTH), BF16),
    pltpu.SemaphoreType.DMA((8,)),
    pltpu.SemaphoreType.DMA((8,)),
]


def grp_peers():
    _, up, down, _, mate = grp_places()
    return [{"grp": up}, {"grp": down}, {"grp": mate}]


def tok_peers():
    t = lax.axis_index("tok")
    return [{"tok": lax.rem(t + k, TOK)} for k in range(1, TOK)]


def trade_start(out_pages, in_pages, send, recv, local):
    t = lax.axis_index("tok")
    keep = pltpu.make_async_copy(out_pages.at[t], in_pages.at[t], local)
    keep.start()
    for k in range(1, TOK):
        peer = lax.rem(t + k, TOK)
        remote(out_pages.at[peer], in_pages.at[t], send.at[k - 1], recv.at[k - 1], {"tok": peer}).start()
    return keep


def trade_end(out_pages, in_pages, send, recv, keep):
    t = lax.axis_index("tok")
    keep.wait()
    for k in range(1, TOK):
        peer = lax.rem(t + k, TOK)
        origin = lax.rem(t + TOK - k, TOK)
        copy = remote(out_pages.at[peer], in_pages.at[origin], send.at[k - 1], recv.at[k - 1], {"tok": peer})
        copy.wait_recv()
        copy.wait_send()


TRADE_SEMAPHORES = [
    pltpu.SemaphoreType.DMA((TOK - 1,)),
    pltpu.SemaphoreType.DMA((TOK - 1,)),
    pltpu.SemaphoreType.DMA,
]


def embed_kernel(found, priors, out_pages, whole, in_pages, own, a1h, a1s, a1f, b1h, b1s, b1f, a2, a2h, a2s, a2f, b2, b2h, b2s, b2f, xsend, xrecv, gsend, grecv, glocal, tsend, trecv, tlocal):
    t = lax.axis_index("tok")
    y, x = t // 4, lax.rem(t, 4)
    xu, xd, xf = [lax.rem(x + k, 4) for k in (1, 3, 2)]
    yu, yd, yf = [lax.rem(y + k, 4) for k in (1, 3, 2)]
    along_x = lambda x_of: {"tok": y * 4 + x_of}
    along_y = lambda y_of: {"tok": y_of * 4 + x}
    greet(tok_peers() + grp_peers())
    started = []

    def go(index, src, dst, target):
        copy = remote(src, dst, xsend.at[index], xrecv.at[index], target)
        copy.start()
        started.append(copy)

    def came(index, dst):
        remote(dst, dst, xsend.at[index], xrecv.at[index], along_x(xu)).wait_recv()

    h = WIDTH // 2
    left, right = pl.ds(0, h), pl.ds(h, h)
    low, high = pl.ds(0, 2), pl.ds(2, 2)
    go(0, found.at[low, xf, :, left], a1h.at[0], along_x(xu))
    go(1, found.at[high, xf, :, left], a1h.at[1], along_x(xd))
    go(2, found.at[yf, low, :, right], b1h.at[0], along_y(yu))
    go(3, found.at[yf, high, :, right], b1h.at[1], along_y(yd))
    keep = trade_start(out_pages, in_pages, tsend, trecv, tlocal)
    own[ROWS:] = priors[...]
    came(0, a1h.at[0])
    a1s[0, :2] = found[:2, xu, :, :h] + a1h[0]
    a1s[0, 2:] = found[2:, xu, :, :h]
    go(4, a1s.at[0], a1f.at[0], along_x(xu))
    came(1, a1h.at[1])
    a1s[1, :2] = found[:2, xd, :, :h]
    a1s[1, 2:] = found[2:, xd, :, :h] + a1h[1]
    go(5, a1s.at[1], a1f.at[1], along_x(xd))
    came(2, b1h.at[0])
    b1s[0, :2] = found[yu, :2, :, h:] + b1h[0]
    b1s[0, 2:] = found[yu, 2:, :, h:]
    go(6, b1s.at[0], b1f.at[0], along_y(yu))
    came(3, b1h.at[1])
    b1s[1, :2] = found[yd, :2, :, h:]
    b1s[1, 2:] = found[yd, 2:, :, h:] + b1h[1]
    go(7, b1s.at[1], b1f.at[1], along_y(yd))
    m = ROWS // 2
    top, bottom = pl.ds(0, m), pl.ds(m, m)
    came(4, a1f.at[0])
    came(5, a1f.at[1])
    a2[...] = found[:, x, :, :h] + a1f[0] + a1f[1]
    go(8, a2.at[yf, top], a2h.at[0], along_y(yu))
    go(9, a2.at[yf, bottom], a2h.at[1], along_y(yd))
    came(6, b1f.at[0])
    came(7, b1f.at[1])
    b2[...] = found[y, :, :, h:] + b1f[0] + b1f[1]
    go(10, b2.at[xf, top], b2h.at[0], along_x(xu))
    go(11, b2.at[xf, bottom], b2h.at[1], along_x(xd))
    came(8, a2h.at[0])
    a2s[0, :m] = a2[yu, :m] + a2h[0]
    a2s[0, m:] = a2[yu, m:]
    go(12, a2s.at[0], a2f.at[0], along_y(yu))
    came(9, a2h.at[1])
    a2s[1, :m] = a2[yd, :m]
    a2s[1, m:] = a2[yd, m:] + a2h[1]
    go(13, a2s.at[1], a2f.at[1], along_y(yd))
    came(10, b2h.at[0])
    b2s[0, :m] = b2[xu, :m] + b2h[0]
    b2s[0, m:] = b2[xu, m:]
    go(14, b2s.at[0], b2f.at[0], along_x(xu))
    came(11, b2h.at[1])
    b2s[1, :m] = b2[xd, :m]
    b2s[1, m:] = b2[xd, m:] + b2h[1]
    go(15, b2s.at[1], b2f.at[1], along_x(xd))
    came(12, a2f.at[0])
    came(13, a2f.at[1])
    own[:ROWS, :h] = a2[y] + a2f[0] + a2f[1]
    came(14, b2f.at[0])
    came(15, b2f.at[1])
    own[:ROWS, h:] = b2[x] + b2f[0] + b2f[1]
    gather_grp(own, whole, gsend, grecv, glocal)
    for copy in started:
        copy.wait_send()
    trade_end(out_pages, in_pages, tsend, trecv, keep)


def embed_exchange(found, priors, out_pages):
    rows = ROWS + 2 * BRANCH
    h, m = WIDTH // 2, ROWS // 2
    return pl.pallas_call(
        embed_kernel,
        out_shape=(
            jax.ShapeDtypeStruct((rows, HIDDEN), BF16),
            jax.ShapeDtypeStruct((TOK, REQ, HIDDEN), BF16),
        ),
        in_specs=[VMEM, VMEM, ANY],
        out_specs=(ANY, ANY),
        scratch_shapes=[
            pltpu.VMEM((rows, WIDTH), BF16),
            pltpu.VMEM((2, 2, ROWS, h), BF16),
            pltpu.VMEM((2, 4, ROWS, h), BF16),
            pltpu.VMEM((2, 4, ROWS, h), BF16),
            pltpu.VMEM((2, 2, ROWS, h), BF16),
            pltpu.VMEM((2, 4, ROWS, h), BF16),
            pltpu.VMEM((2, 4, ROWS, h), BF16),
            pltpu.VMEM((4, ROWS, h), BF16),
            pltpu.VMEM((2, m, h), BF16),
            pltpu.VMEM((2, ROWS, h), BF16),
            pltpu.VMEM((2, ROWS, h), BF16),
            pltpu.VMEM((4, ROWS, h), BF16),
            pltpu.VMEM((2, m, h), BF16),
            pltpu.VMEM((2, ROWS, h), BF16),
            pltpu.VMEM((2, ROWS, h), BF16),
            pltpu.SemaphoreType.DMA((16,)),
            pltpu.SemaphoreType.DMA((16,)),
            pltpu.SemaphoreType.DMA((9,)),
            pltpu.SemaphoreType.DMA((9,)),
            pltpu.SemaphoreType.DMA,
            *TRADE_SEMAPHORES,
        ],
        compiler_params=pltpu.CompilerParams(
            collective_id=1, has_side_effects=True, vmem_limit_bytes=40 << 20
        ),
        cost_estimate=pl.CostEstimate(flops=0, transcendentals=0, bytes_accessed=100 << 20),
        name="embed_exchange",
    )(found, priors, out_pages)


def residual_kernel(part, base, out_pages, whole, own_out, in_pages, mated, sums, halves, full, rsend, rrecv, own, gsend, grecv, glocal, tsend, trecv, tlocal):
    greet(tok_peers() + grp_peers())
    keep = trade_start(out_pages, in_pages, tsend, trecv, tlocal)
    total = reduce_grp(part, mated, sums, halves, full, rsend, rrecv)
    own[...] = (base[...].astype(F32) + total).astype(BF16)
    own_out[...] = own[...]
    gather_grp(own, whole, gsend, grecv, glocal)
    trade_end(out_pages, in_pages, tsend, trecv, keep)


def residual_exchange(part, base, out_pages):
    return pl.pallas_call(
        residual_kernel,
        out_shape=(
            jax.ShapeDtypeStruct((ROWS, HIDDEN), BF16),
            jax.ShapeDtypeStruct((ROWS, WIDTH), BF16),
            jax.ShapeDtypeStruct((TOK, REQ, HIDDEN), BF16),
        ),
        in_specs=[VMEM, VMEM, ANY],
        out_specs=(ANY, VMEM, ANY),
        scratch_shapes=[
            *REDUCE_SCRATCH,
            pltpu.VMEM((ROWS, WIDTH), BF16),
            pltpu.SemaphoreType.DMA((9,)),
            pltpu.SemaphoreType.DMA((9,)),
            pltpu.SemaphoreType.DMA,
            *TRADE_SEMAPHORES,
        ],
        compiler_params=pltpu.CompilerParams(
            collective_id=2, has_side_effects=True, vmem_limit_bytes=40 << 20
        ),
        cost_estimate=pl.CostEstimate(flops=0, transcendentals=0, bytes_accessed=80 << 20),
        name="residual_exchange",
    )(part, base, out_pages)


def final_kernel(part, base, gate, out, mated, sums, halves, full, rsend, rrecv):
    greet(grp_peers())
    total = reduce_grp(part, mated, sums, halves, full, rsend, rrecv)
    out[...] = (base[...].astype(F32) + gate[...] * total).astype(BF16)


def final_exchange(part, base, gate):
    return pl.pallas_call(
        final_kernel,
        out_shape=jax.ShapeDtypeStruct((ROWS, WIDTH), BF16),
        in_specs=[VMEM, VMEM, VMEM],
        out_specs=VMEM,
        scratch_shapes=REDUCE_SCRATCH,
        compiler_params=pltpu.CompilerParams(
            collective_id=3, has_side_effects=True, vmem_limit_bytes=40 << 20
        ),
        cost_estimate=pl.CostEstimate(flops=0, transcendentals=0, bytes_accessed=40 << 20),
        name="final_exchange",
    )(part, base, gate)


def dot(a, b):
    return jnp.dot(a, b, preferred_element_type=F32)


def row_stats(rows_of, mean, scale):
    value = rows_of.astype(F32)
    middle = jnp.mean(value, axis=-1, keepdims=True)
    centered = value - middle
    spread = jnp.mean(centered * centered, axis=-1, keepdims=True)
    mean[...] = middle
    scale[...] = lax.rsqrt(spread + EPSILON)


def normed_and_step(block, prior, mean, scale, gain):
    normed = (block.astype(F32) - mean) * scale * gain
    row = lax.broadcasted_iota(jnp.int32, (ROWS, WIDTH), 0)
    spread = (
        lax.broadcasted_iota(jnp.int32, (ROWS, BRANCH), 0) // DRAFT
        == lax.broadcasted_iota(jnp.int32, (ROWS, BRANCH), 1)
    )
    carried = dot(spread.astype(BF16), prior)
    before = jnp.where(lax.rem(row, DRAFT) == 0, carried, pltpu.roll(normed, 1, axis=0))
    return normed, before - normed


def kept_row(normed, prior, kept_column):
    column = lax.broadcasted_iota(jnp.int32, (BRANCH, ROWS), 1)
    branch = lax.broadcasted_iota(jnp.int32, (BRANCH, ROWS), 0)
    pick = (column == branch * DRAFT + kept_column - 1) & (kept_column > 0)
    picked = dot(pick.astype(BF16), normed.astype(BF16))
    return jnp.where(kept_column > 0, picked, prior.astype(F32)).astype(BF16)


def head_ones(size):
    return (
        lax.broadcasted_iota(jnp.int32, (size, size), 0) // HEAD
        == lax.broadcasted_iota(jnp.int32, (size, size), 1) // HEAD
    ).astype(BF16)


def per_head(value):
    ones = head_ones(256)
    return jnp.concatenate([dot(value[:, :256], ones), dot(value[:, 256:], ones)], axis=1)


def per_head_fine(value):
    top = value.astype(BF16)
    rest = (value - top.astype(F32)).astype(BF16)
    return per_head(top) + per_head(rest)


def attention_kernel(
    place, request_of, winner, kept,
    xw, gain1, blend, weights, narrow, widen, baseline, boost, gain2, kept_column, pages,
    attended, chosen, shift,
    mean, scale, acc, low, r_s, k_s, v_s, w_s, y_s, p_s,
):
    step = pl.program_id(0)

    @pl.when(step == 0)
    def _():
        row_stats(xw[:ROWS], mean, scale)
        acc[...] = jnp.zeros_like(acc)
        low[...] = jnp.zeros_like(low)

    columns = pl.ds(pl.multiple_of(step * WIDTH, WIDTH), WIDTH)
    prior = xw[ROWS : ROWS + BRANCH, columns]
    normed, delta = normed_and_step(xw[:ROWS, columns], prior, mean[...], scale[...], gain1[0:1])

    @pl.when(step == place[0])
    def _():
        shift[...] = kept_row(normed, prior, kept_column[...])

    for c in range(4):
        acc[c] += dot((normed + delta * blend[c : c + 1]).astype(BF16), weights[c])
    low[...] += dot((normed + delta * blend[4:5]).astype(BF16), narrow[...])

    @pl.when(step == GRP - 1)
    def _():
        lowrank = jnp.tanh(low[...]).astype(BF16)
        w_s[...] = jnp.exp(-jnp.exp(baseline[...] + dot(lowrank, widen[...])))
        r_s[...] = acc[0]
        k_s[...] = acc[1]
        v_s[...] = acc[2]
        shape3 = (BRANCH, DRAFT, WIDTH)
        r3, k3 = r_s[...].reshape(shape3), k_s[...].reshape(shape3)
        v3, w3 = v_s[...].reshape(shape3), w_s[...].reshape(shape3)
        position = lax.broadcasted_iota(jnp.int32, shape3, 1)
        y_s[...] = per_head_fine(r_s[...] * boost[...] * k_s[...]) * v_s[...]
        p_s[...] = jnp.ones_like(p_s)
        for s in range(DRAFT - 2, -1, -1):
            decay = jnp.where(position > s + 1, p_s[...].reshape(shape3) * w3[:, s + 1 : s + 2], 1.0)
            p_s[...] = decay.reshape(ROWS, WIDTH)
            term = jnp.where(position > s, r3 * decay * k3[:, s : s + 1], 0.0)
            score = per_head(term.reshape(ROWS, WIDTH).astype(BF16)).reshape(shape3)
            y_s[...] += (score * v3[:, s : s + 1]).reshape(ROWS, WIDTH)
        decay = jnp.where(position > 0, p_s[...].reshape(shape3) * w3[:, 0:1], 1.0)
        p_s[...] = r_s[...] * decay.reshape(ROWS, WIDTH)
        for b in range(BRANCH):
            rows = pl.ds(b * DRAFT, DRAFT)
            for pair in range(PAIRS):
                lanes = pl.ds(pair * 128, 128)
                y_s[rows, lanes] += dot(p_s[rows, lanes].astype(BF16), pages[request_of[b], pair])
        y = y_s[...]
        centered = y - per_head_fine(y) * (1.0 / HEAD)
        spread = per_head_fine(centered * centered) * (1.0 / HEAD)
        gate = acc[3]
        gate = gate * jax.nn.sigmoid(gate)
        attended[...] = (centered * lax.rsqrt(spread + HEAD_EPSILON) * gain2[...] * gate).astype(BF16)
        eye = (
            lax.broadcasted_iota(jnp.int32, (128, 128), 0)
            == lax.broadcasted_iota(jnp.int32, (128, 128), 1)
        )
        spot = lax.broadcasted_iota(jnp.int32, (DRAFT, WIDTH), 0)
        for q in range(REQ):
            b = winner[q]
            count = kept[b]
            rows = pl.ds(pl.multiple_of(b * DRAFT, DRAFT), DRAFT)
            live = spot < count
            tail = jnp.where(live, w_s[rows], 1.0)
            for hop in (1, 2, 4, 8):
                later = pltpu.roll(tail, DRAFT - hop, axis=0)
                tail = tail * jnp.where(spot < DRAFT - hop, later, 1.0)
            after = jnp.where(spot < DRAFT - 1, pltpu.roll(tail, DRAFT - 1, axis=0), 1.0)
            keys = jnp.where(live, k_s[rows], 0.0) * after
            values = v_s[rows].astype(BF16)
            for pair in range(PAIRS):
                lanes = slice(pair * 128, pair * 128 + 128)
                fade = jnp.where(eye, tail[0:1, lanes], 0.0)
                left = jnp.concatenate([keys[:, lanes], fade], axis=0).astype(BF16)
                right = jnp.concatenate([values[:, lanes], pages[q, pair]], axis=0)
                chosen[q, pair] = lax.dot_general(
                    left, right, (((0,), (0,)), ((), ())), preferred_element_type=F32
                ).astype(BF16)


def attention(place, request_of, winner, kept, xw, scales, blends, weights, narrow, widen, baseline, boost, pages):
    rows = xw.shape[0]
    full = lambda *shape: pl.BlockSpec(shape, lambda k, *_: (0,) * len(shape))
    mine = pl.BlockSpec((1, WIDTH), lambda k, at, *_: (0, at[0]))
    return pl.pallas_call(
        attention_kernel,
        out_shape=(
            jax.ShapeDtypeStruct((ROWS, WIDTH), BF16),
            jax.ShapeDtypeStruct((REQ, PAIRS, 128, 128), BF16),
            jax.ShapeDtypeStruct((BRANCH, WIDTH), BF16),
        ),
        grid_spec=pltpu.PrefetchScalarGridSpec(
            num_scalar_prefetch=4,
            grid=(GRP,),
            in_specs=[
                full(rows, HIDDEN),
                pl.BlockSpec((3, WIDTH), lambda k, *_: (0, k)),
                pl.BlockSpec((7, WIDTH), lambda k, *_: (0, k)),
                pl.BlockSpec((4, WIDTH, WIDTH), lambda k, *_: (0, k, 0)),
                pl.BlockSpec((WIDTH, 128), lambda k, *_: (k, 0)),
                full(128, WIDTH),
                mine,
                mine,
                mine,
                full(BRANCH, 1),
                full(REQ, PAIRS, 128, 128),
            ],
            out_specs=(
                full(ROWS, WIDTH),
                full(REQ, PAIRS, 128, 128),
                full(BRANCH, WIDTH),
            ),
            scratch_shapes=[
                pltpu.VMEM((ROWS, 1), F32),
                pltpu.VMEM((ROWS, 1), F32),
                pltpu.VMEM((4, ROWS, WIDTH), F32),
                pltpu.VMEM((ROWS, 128), F32),
            ]
            + [pltpu.VMEM((ROWS, WIDTH), F32)] * 6,
        ),
        compiler_params=pltpu.CompilerParams(vmem_limit_bytes=52 << 20),
        cost_estimate=pl.CostEstimate(flops=6 << 30, transcendentals=1 << 20, bytes_accessed=24 << 20),
        name="attention",
    )(
        place, request_of, winner, kept,
        xw, scales, blends, weights, narrow, widen,
        baseline.reshape(1, HIDDEN), boost.reshape(1, HIDDEN), scales[2:3],
        kept.reshape(BRANCH, 1), pages,
    )


def feedforward_kernel(place, rw, prior_ref, gain, blend, keyed, content, kept_column, part, gate, shift, mean, scale, acc):
    step = pl.program_id(0)

    @pl.when(step == 0)
    def _():
        row_stats(rw[...], mean, scale)
        acc[...] = jnp.zeros_like(acc)

    columns = pl.ds(pl.multiple_of(step * WIDTH, WIDTH), WIDTH)
    prior = prior_ref[...]
    normed, delta = normed_and_step(rw[:, columns], prior, mean[...], scale[...], gain[1:2])

    @pl.when(step == place[0])
    def _():
        shift[...] = kept_row(normed, prior, kept_column[...])

    acc[:, :KEYS] += dot((normed + delta * blend[5:6]).astype(BF16), keyed[:, :KEYS])
    acc[:, KEYS:] += dot((normed + delta * blend[6:7]).astype(BF16), keyed[:, KEYS:])

    @pl.when(step == GRP - 1)
    def _():
        gate[...] = jax.nn.sigmoid(acc[:, KEYS:])
        hidden = jnp.square(jnp.maximum(acc[:, :KEYS], 0.0)).astype(BF16)
        for g in range(GRP):
            lanes = slice(g * WIDTH, g * WIDTH + WIDTH)
            part[:, lanes] = dot(hidden, content[:, lanes]).astype(BF16)


def feedforward(place, rw, prior, scales, blends, keyed, content, kept):
    full = lambda *shape: pl.BlockSpec(shape, lambda k, *_: (0,) * len(shape))
    return pl.pallas_call(
        feedforward_kernel,
        out_shape=(
            jax.ShapeDtypeStruct((ROWS, HIDDEN), BF16),
            jax.ShapeDtypeStruct((ROWS, WIDTH), F32),
            jax.ShapeDtypeStruct((BRANCH, WIDTH), BF16),
        ),
        grid_spec=pltpu.PrefetchScalarGridSpec(
            num_scalar_prefetch=1,
            grid=(GRP,),
            in_specs=[
                full(ROWS, HIDDEN),
                pl.BlockSpec((BRANCH, WIDTH), lambda k, *_: (0, k)),
                pl.BlockSpec((3, WIDTH), lambda k, *_: (0, k)),
                pl.BlockSpec((7, WIDTH), lambda k, *_: (0, k)),
                pl.BlockSpec((WIDTH, KEYS + WIDTH), lambda k, *_: (k, 0)),
                full(KEYS, HIDDEN),
                full(BRANCH, 1),
            ],
            out_specs=(full(ROWS, HIDDEN), full(ROWS, WIDTH), full(BRANCH, WIDTH)),
            scratch_shapes=[
                pltpu.VMEM((ROWS, 1), F32),
                pltpu.VMEM((ROWS, 1), F32),
                pltpu.VMEM((ROWS, KEYS + WIDTH), F32),
            ],
        ),
        compiler_params=pltpu.CompilerParams(vmem_limit_bytes=52 << 20),
        cost_estimate=pl.CostEstimate(flops=5 << 30, transcendentals=1 << 18, bytes_accessed=24 << 20),
        name="feedforward",
    )(place, rw, prior, scales, blends, keyed, content, kept.reshape(BRANCH, 1))


def body(
    guess_symbol_ids,
    symbol_vector_lookup,
    prior_attention_normed,
    prior_feedforward_normed,
    layernorm_scales,
    lagged_blend_ratios,
    attention_matrices,
    forgetting_baseline_vector,
    forgetting_narrow_matrix,
    forgetting_widen_matrix,
    diagonal_boost,
    attention_result_matrix,
    feedforward_lookup_matrix,
    feedforward_content_matrix,
    feedforward_gating_matrix,
    memory_matrix_store,
    query_memory_slot,
    candidate_tally_each_query,
    kept_guess_tally,
):
    tok_at = lax.axis_index("tok")
    grp_at = lax.axis_index("grp")
    place = grp_at.reshape(1)
    vocab_rows = symbol_vector_lookup.shape[0]
    slot_count = memory_matrix_store.shape[0]

    result_matrix = lax.all_gather(attention_result_matrix, "tok", axis=1, tiled=True)
    keyed = lax.all_gather(
        jnp.concatenate([feedforward_lookup_matrix, feedforward_gating_matrix], axis=1),
        "tok",
        axis=0,
        tiled=True,
    )
    content = lax.all_gather(feedforward_content_matrix, "tok", axis=1, tiled=True)

    wanted = guess_symbol_ids - tok_at * vocab_rows
    inside = (wanted >= 0) & (wanted < vocab_rows)
    found = jnp.take(symbol_vector_lookup, jnp.clip(wanted, 0, vocab_rows - 1), axis=0)
    found = jnp.where(inside[:, None], found, jnp.zeros((), BF16)).reshape(4, 4, ROWS, WIDTH)
    priors = jnp.concatenate([prior_attention_normed, prior_feedforward_normed], axis=0)

    owners = (query_memory_slot // slot_count).reshape(TOK, REQ)
    places = (query_memory_slot % slot_count).reshape(TOK, REQ)
    owned_here = owners == tok_at
    send_slot = jnp.sum(jnp.where(owned_here, places, 0), axis=1)
    sending = jnp.any(owned_here, axis=1)
    outgoing = jnp.where(
        sending[:, None, None], jnp.take(memory_matrix_store, send_slot, axis=0), 0.0
    ).astype(BF16)

    whole, incoming = embed_exchange(found, priors, outgoing)

    my_owners = lax.dynamic_index_in_dim(owners, tok_at, 0, keepdims=False)
    my_counts = lax.dynamic_index_in_dim(candidate_tally_each_query, tok_at, 0, keepdims=False)
    local_ids = jnp.arange(BRANCH, dtype=jnp.int32)
    request_ends = jnp.cumsum(my_counts)
    request_of = jnp.sum((request_ends[None, :] <= local_ids[:, None]).astype(jnp.int32), axis=1)
    branch_score = kept_guess_tally * BRANCH + (BRANCH - 1 - local_ids)
    member = request_of[None, :] == jnp.arange(REQ, dtype=jnp.int32)[:, None]
    best_score = jnp.max(jnp.where(member, branch_score[None, :], -1), axis=1)
    winner = BRANCH - 1 - best_score % BRANCH

    diagonal = (
        lax.broadcasted_iota(jnp.int32, (128, 128), 0) // HEAD
        == lax.broadcasted_iota(jnp.int32, (128, 128), 1) // HEAD
    )
    my_pages = jnp.take(incoming, my_owners, axis=0).reshape(REQ, PAIRS, 128, HEAD)
    pages = jnp.where(diagonal, jnp.concatenate([my_pages, my_pages], axis=-1), jnp.zeros((), BF16))

    attended, chosen, shift_att_out = attention(
        place, request_of, winner, kept_guess_tally,
        whole, layernorm_scales, lagged_blend_ratios, attention_matrices,
        forgetting_narrow_matrix, forgetting_widen_matrix,
        forgetting_baseline_vector, diagonal_boost, pages,
    )
    partial_att = dot(attended, result_matrix).astype(BF16)

    half = lax.broadcasted_iota(jnp.int32, (128, HEAD), 0) < HEAD
    new_pages = jnp.where(half, chosen[..., :HEAD], chosen[..., HEAD:]).reshape(REQ, REQ, HIDDEN)
    targets = my_owners[None, :] == jnp.arange(TOK, dtype=jnp.int32)[:, None]
    pick_index = jnp.sum(
        jnp.where(targets, jnp.arange(REQ, dtype=jnp.int32)[None, :], 0), axis=1
    )
    outgoing_back = jnp.take(new_pages, pick_index, axis=0)

    own_x = lax.dynamic_slice(whole, (0, grp_at * WIDTH), (ROWS, WIDTH))
    residual_whole, residual, returned = residual_exchange(partial_att, own_x, outgoing_back)

    partial_ffn, gate, shift_ffn_out = feedforward(
        place, residual_whole, whole[ROWS + BRANCH :], layernorm_scales, lagged_blend_ratios,
        keyed, content, kept_guess_tally,
    )
    layer_out = final_exchange(partial_ffn, residual, gate)

    hit = (send_slot[None, :] == jnp.arange(slot_count, dtype=jnp.int32)[:, None]) & sending[None, :]
    source = jnp.sum(jnp.where(hit, jnp.arange(TOK, dtype=jnp.int32)[None, :], 0), axis=1)
    store_out = jnp.where(
        jnp.any(hit, axis=1)[:, None, None],
        jnp.take(returned, source, axis=0).astype(F32),
        memory_matrix_store,
    )
    return (layer_out, shift_att_out, shift_ffn_out, store_out)


def solution(mesh):
    in_specs = (
        P(),
        P("tok", "grp"),
        P("tok", "grp"),
        P("tok", "grp"),
        P(),
        P(),
        P(None, None, "grp"),
        P(),
        P(),
        P(None, "grp"),
        P(),
        P("grp", "tok"),
        P("tok", "grp"),
        P("grp", "tok"),
        P("tok", "grp"),
        P("tok", "grp", None),
        P(),
        P(),
        P("tok"),
    )
    out_specs = (P("tok", "grp"), P("tok", "grp"), P("tok", "grp"), P("tok", "grp", None))
    return jax.shard_map(body, mesh=mesh, in_specs=in_specs, out_specs=out_specs, check_vma=False)
```

```python
import functools

import jax
import jax.numpy as jnp
from jax import lax
from jax.experimental import pallas as pl
from jax.experimental.pallas import tpu as pltpu
from jax.sharding import PartitionSpec as P

HIDDEN = 4096
HEAD = 64
DRAFT = 16
BRANCH = 16
ROWS = BRANCH * DRAFT
WIDTH = 512
TOK = 16
GRP = 8
REQ = 8
PAIRS = 4
KEYS = 896
SPACE = 48
EPSILON = 1e-05
HEAD_EPSILON = 0.00064
F32 = jnp.float32
BF16 = jnp.bfloat16
MESH = pl.DeviceIdType.MESH
ANY = pl.BlockSpec(memory_space=pl.ANY)
VMEM = pl.BlockSpec(memory_space=pltpu.VMEM)


def remote(src, dst, send, recv, device):
    return pltpu.make_async_remote_copy(
        src_ref=src, dst_ref=dst, send_sem=send, recv_sem=recv, device_id=device, device_id_type=MESH
    )


def greet(devices):
    barrier = pltpu.get_barrier_semaphore()
    for device in devices:
        pl.semaphore_signal(barrier, inc=1, device_id=device, device_id_type=MESH)
    pl.semaphore_wait(barrier, len(devices))


def grp_places():
    g = lax.axis_index("grp")
    z, core = g // 2, g % 2
    up = lax.rem(z + 1, 4) * 2 + core
    down = lax.rem(z + 3, 4) * 2 + core
    far = lax.rem(z + 2, 4) * 2 + core
    mate = z * 2 + 1 - core
    return g, up, down, far, mate


def block_of(g):
    return pl.ds(pl.multiple_of(g * WIDTH, WIDTH), WIDTH)


def flip(g):
    return g + 1 - 2 * lax.rem(g, 2)


def gather_grp(own, out, send, recv, local, between=()):
    between = list(between)

    def aside():
        if between:
            between.pop(0)()

    rows = out.shape[0]
    half = rows // 2
    g, up, down, far, mate = grp_places()
    first, last, whole = pl.ds(0, half), pl.ds(half, rows - half), pl.ds(0, rows)
    at = lambda part, g_of: out.at[part, block_of(g_of)]
    keep = pltpu.make_async_copy(own, at(whole, g), local)
    keep.start()
    started = []

    def go(index, src, part, g_of, target):
        copy = remote(src, at(part, g_of), send.at[index], recv.at[index], {"grp": target})
        copy.start()
        started.append(copy)

    def came(index, part, g_of):
        remote(at(part, g_of), at(part, g_of), send.at[index], recv.at[index], {"grp": mate}).wait_recv()

    go(0, own, whole, g, up)
    go(1, own, whole, g, down)
    go(2, own, whole, g, mate)
    aside()
    came(0, whole, down)
    go(3, at(first, down), first, down, up)
    go(5, at(whole, down), whole, down, mate)
    came(1, whole, up)
    go(4, at(last, up), last, up, down)
    go(6, at(whole, up), whole, up, mate)
    aside()
    came(3, first, far)
    go(7, at(first, far), first, far, mate)
    came(4, last, far)
    go(8, at(last, far), last, far, mate)
    came(2, whole, mate)
    came(5, whole, flip(down))
    came(6, whole, flip(up))
    came(7, first, flip(far))
    came(8, last, flip(far))
    while between:
        aside()
    keep.wait()
    for copy in started:
        copy.wait_send()


def reduce_grp(part, mated, sums, halves, full, send, recv, meanwhile=lambda: None):
    g, up, down, far, mate = grp_places()
    half = ROWS // 2
    started = []

    def go(index, src, dst, target):
        copy = remote(src, dst, send.at[index], recv.at[index], {"grp": target})
        copy.start()
        started.append(copy)

    def came(index, dst):
        remote(dst, dst, send.at[index], recv.at[index], {"grp": mate}).wait_recv()

    order = (far, up, down, g)
    for k in range(4):
        go(k, part.at[:, block_of(flip(order[k]))], mated.at[k], mate)

    def own(k):
        return part[:, block_of(order[k])].astype(F32) + mated[k].astype(F32)

    came(0, mated.at[0])
    sums[0] = own(0).astype(BF16)
    go(4, sums.at[0, pl.ds(0, half)], halves.at[0], up)
    go(5, sums.at[0, pl.ds(half, half)], halves.at[1], down)
    came(1, mated.at[1])
    came(4, halves.at[0])
    sums[1, :half] = (own(1)[:half] + halves[0].astype(F32)).astype(BF16)
    sums[1, half:] = own(1)[half:].astype(BF16)
    go(6, sums.at[1], full.at[0], up)
    came(2, mated.at[2])
    came(5, halves.at[1])
    sums[2, :half] = own(2)[:half].astype(BF16)
    sums[2, half:] = (own(2)[half:] + halves[1].astype(F32)).astype(BF16)
    go(7, sums.at[2], full.at[1], down)
    meanwhile()
    came(3, mated.at[3])
    came(6, full.at[0])
    came(7, full.at[1])
    total = own(3) + full[0].astype(F32) + full[1].astype(F32)
    for copy in started:
        copy.wait_send()
    return total


REDUCE_SCRATCH = [
    pltpu.VMEM((4, ROWS, WIDTH), BF16),
    pltpu.VMEM((3, ROWS, WIDTH), BF16),
    pltpu.VMEM((2, ROWS // 2, WIDTH), BF16),
    pltpu.VMEM((2, ROWS, WIDTH), BF16),
    pltpu.SemaphoreType.DMA((8,)),
    pltpu.SemaphoreType.DMA((8,)),
]


def gather_tok(own, out, first_rows, last_rows, send, recv, local):
    t = lax.axis_index("tok")
    y, x = t // 4, lax.rem(t, 4)
    xu, xd, xf = [lax.rem(x + k, 4) for k in (1, 3, 2)]
    yu, yd, yf = [lax.rem(y + k, 4) for k in (1, 3, 2)]
    along_x = lambda x_of: {"tok": y * 4 + x_of}
    along_y = lambda y_of: {"tok": y_of * 4 + x}
    cols = lambda x_of: pl.ds(pl.multiple_of(x_of * 256, 256), 256)
    one = lambda rows, y_of, x_of: out.at[y_of, rows, cols(x_of)]
    wide = lambda rows, y_of: out.at[y_of, rows]
    tall = lambda rows, x_of: out.at[:, rows, cols(x_of)]
    f0, f1 = first_rows, last_rows
    fa, fb = [pl.ds(f0.start + k * (f0.size // 2), f0.size // 2) for k in (0, 1)]
    la, lb = [pl.ds(f1.start + k * (f1.size // 2), f1.size // 2) for k in (0, 1)]
    started = []

    def go(index, src, dst, target):
        copy = remote(src, dst, send.at[index], recv.at[index], target)
        copy.start()
        started.append(copy)

    def came(index, dst):
        remote(dst, dst, send.at[index], recv.at[index], along_x(xu)).wait_recv()

    keep = pltpu.make_async_copy(own, one(pl.ds(0, own.shape[0]), y, x), local)

    def begin():
        keep.start()
        go(0, own.at[f0], one(f0, y, x), along_x(xu))
        go(1, own.at[f0], one(f0, y, x), along_x(xd))
        go(2, own.at[f1], one(f1, y, x), along_y(yu))
        go(3, own.at[f1], one(f1, y, x), along_y(yd))

    def relay():
        came(0, one(f0, y, xd))
        go(4, one(fa, y, xd), one(fa, y, xd), along_x(xu))
        came(2, one(f1, yd, x))
        go(6, one(la, yd, x), one(la, yd, x), along_y(yu))
        came(1, one(f0, y, xu))
        go(5, one(fb, y, xu), one(fb, y, xu), along_x(xd))
        came(3, one(f1, yu, x))
        go(7, one(lb, yu, x), one(lb, yu, x), along_y(yd))

    def turn():
        keep.wait()
        came(4, one(fa, y, xf))
        came(5, one(fb, y, xf))
        go(8, wide(f0, y), wide(f0, y), along_y(yu))
        go(9, wide(f0, y), wide(f0, y), along_y(yd))
        came(6, one(la, yf, x))
        came(7, one(lb, yf, x))
        go(10, tall(f1, x), tall(f1, x), along_x(xu))
        go(11, tall(f1, x), tall(f1, x), along_x(xd))

    def last():
        came(8, wide(f0, yd))
        go(12, wide(fa, yd), wide(fa, yd), along_y(yu))
        came(10, tall(f1, xd))
        go(14, tall(la, xd), tall(la, xd), along_x(xu))
        came(9, wide(f0, yu))
        go(13, wide(fb, yu), wide(fb, yu), along_y(yd))
        came(11, tall(f1, xu))
        go(15, tall(lb, xu), tall(lb, xu), along_x(xd))

    def end():
        came(12, wide(fa, yf))
        came(13, wide(fb, yf))
        came(14, tall(la, xf))
        came(15, tall(lb, xf))
        for copy in started:
            copy.wait_send()

    return begin, relay, turn, last, end


def grp_peers():
    _, up, down, _, mate = grp_places()
    return [{"grp": up}, {"grp": down}, {"grp": mate}]


def tok_peers():
    t = lax.axis_index("tok")
    return [{"tok": lax.rem(t + k, TOK)} for k in range(1, TOK)]


def page_masks():
    even = lax.rem(lax.broadcasted_iota(jnp.int32, (8, 128), 0), 2) == 0
    left = lax.broadcasted_iota(jnp.int32, (8, 128), 1) < HEAD
    return even, left


def pair_page(page, put):
    even, left = page_masks()
    for block in range(4):
        rows = [[] for _ in range(PAIRS)]
        for group in (2 * block, 2 * block + 1):
            pieces = []
            for m in range(4 * group, 4 * group + 4):
                here = page[:, m * 128 : m * 128 + 128]
                swapped = pltpu.roll(here, HEAD, axis=1)
                pieces += [jnp.where(even, here, swapped), jnp.where(even, swapped, here)]
            turned = jnp.swapaxes(jnp.stack(pieces), 0, 1)
            for pair in range(PAIRS):
                rows[pair].append(jnp.where(left, turned[2 * pair], turned[2 * pair + 1]))
        for pair in range(PAIRS):
            put(pair, 16 * block, jnp.concatenate(rows[pair], axis=0))


def flat_page(page, put):
    even, left = page_masks()
    for group in range(8):
        rows = [page[pair, 8 * group : 8 * group + 8] for pair in range(PAIRS)]
        turned = jnp.swapaxes(jnp.stack([rows[h // 2] for h in range(8)]), 0, 1)
        for m in range(4):
            first, second = turned[2 * m], turned[2 * m + 1]
            swapped_first = pltpu.roll(first, HEAD, axis=1)
            swapped_second = pltpu.roll(second, HEAD, axis=1)
            put(
                (4 * group + m) * 128,
                jnp.where(
                    left,
                    jnp.where(even, first, swapped_first),
                    jnp.where(even, swapped_second, second),
                ),
            )


def trade_start(out_pages, in_pages, send, recv, local):
    t = lax.axis_index("tok")
    keep = pltpu.make_async_copy(out_pages.at[t], in_pages.at[t], local)
    keep.start()
    for k in range(1, TOK):
        peer = lax.rem(t + k, TOK)
        remote(out_pages.at[peer], in_pages.at[t], send.at[k - 1], recv.at[k - 1], {"tok": peer}).start()
    return keep


def trade_end(out_pages, in_pages, send, recv, keep):
    t = lax.axis_index("tok")
    keep.wait()
    for k in range(1, TOK):
        peer = lax.rem(t + k, TOK)
        origin = lax.rem(t + TOK - k, TOK)
        copy = remote(out_pages.at[peer], in_pages.at[origin], send.at[k - 1], recv.at[k - 1], {"tok": peer})
        copy.wait_recv()
        copy.wait_send()


TRADE_SEMAPHORES = [
    pltpu.SemaphoreType.DMA((TOK - 1,)),
    pltpu.SemaphoreType.DMA((TOK - 1,)),
    pltpu.SemaphoreType.DMA,
]


def dense_rows(found, own, begin, a1h, a1s, a1f, b1h, b1s, b1f, a2, a2h, a2s, a2f, b2, b2h, b2s, b2f, xsend, xrecv):
    t = lax.axis_index("tok")
    y, x = t // 4, lax.rem(t, 4)
    xu, xd, xf = [lax.rem(x + k, 4) for k in (1, 3, 2)]
    yu, yd, yf = [lax.rem(y + k, 4) for k in (1, 3, 2)]
    along_x = lambda x_of: {"tok": y * 4 + x_of}
    along_y = lambda y_of: {"tok": y_of * 4 + x}
    started = []

    def go(index, src, dst, target):
        copy = remote(src, dst, xsend.at[index], xrecv.at[index], target)
        copy.start()
        started.append(copy)

    def came(index, dst):
        remote(dst, dst, xsend.at[index], xrecv.at[index], along_x(xu)).wait_recv()

    h = WIDTH // 2
    left, right = pl.ds(0, h), pl.ds(h, h)
    low, high = pl.ds(0, 2), pl.ds(2, 2)
    go(0, found.at[low, xf, :, left], a1h.at[0], along_x(xu))
    go(1, found.at[high, xf, :, left], a1h.at[1], along_x(xd))
    go(2, found.at[yf, low, :, right], b1h.at[0], along_y(yu))
    go(3, found.at[yf, high, :, right], b1h.at[1], along_y(yd))
    begin()
    came(0, a1h.at[0])
    a1s[0, :2] = found[:2, xu, :, :h] + a1h[0]
    a1s[0, 2:] = found[2:, xu, :, :h]
    go(4, a1s.at[0], a1f.at[0], along_x(xu))
    came(1, a1h.at[1])
    a1s[1, :2] = found[:2, xd, :, :h]
    a1s[1, 2:] = found[2:, xd, :, :h] + a1h[1]
    go(5, a1s.at[1], a1f.at[1], along_x(xd))
    came(2, b1h.at[0])
    b1s[0, :2] = found[yu, :2, :, h:] + b1h[0]
    b1s[0, 2:] = found[yu, 2:, :, h:]
    go(6, b1s.at[0], b1f.at[0], along_y(yu))
    came(3, b1h.at[1])
    b1s[1, :2] = found[yd, :2, :, h:]
    b1s[1, 2:] = found[yd, 2:, :, h:] + b1h[1]
    go(7, b1s.at[1], b1f.at[1], along_y(yd))
    m = ROWS // 2
    top, bottom = pl.ds(0, m), pl.ds(m, m)
    came(4, a1f.at[0])
    came(5, a1f.at[1])
    a2[...] = found[:, x, :, :h] + a1f[0] + a1f[1]
    go(8, a2.at[yf, top], a2h.at[0], along_y(yu))
    go(9, a2.at[yf, bottom], a2h.at[1], along_y(yd))
    came(6, b1f.at[0])
    came(7, b1f.at[1])
    b2[...] = found[y, :, :, h:] + b1f[0] + b1f[1]
    go(10, b2.at[xf, top], b2h.at[0], along_x(xu))
    go(11, b2.at[xf, bottom], b2h.at[1], along_x(xd))
    came(8, a2h.at[0])
    a2s[0, :m] = a2[yu, :m] + a2h[0]
    a2s[0, m:] = a2[yu, m:]
    go(12, a2s.at[0], a2f.at[0], along_y(yu))
    came(9, a2h.at[1])
    a2s[1, :m] = a2[yd, :m]
    a2s[1, m:] = a2[yd, m:] + a2h[1]
    go(13, a2s.at[1], a2f.at[1], along_y(yd))
    came(10, b2h.at[0])
    b2s[0, :m] = b2[xu, :m] + b2h[0]
    b2s[0, m:] = b2[xu, m:]
    go(14, b2s.at[0], b2f.at[0], along_x(xu))
    came(11, b2h.at[1])
    b2s[1, :m] = b2[xd, :m]
    b2s[1, m:] = b2[xd, m:] + b2h[1]
    go(15, b2s.at[1], b2f.at[1], along_x(xd))
    came(12, a2f.at[0])
    came(13, a2f.at[1])
    own[:ROWS, :h] = a2[y] + a2f[0] + a2f[1]
    came(14, b2f.at[0])
    came(15, b2f.at[1])
    own[:ROWS, h:] = b2[x] + b2f[0] + b2f[1]
    for copy in started:
        copy.wait_send()


def sparse_rows(packed, spot, own, begin, parcels, psend, precv, plocal):
    t = lax.axis_index("tok")
    keep = pltpu.make_async_copy(packed.at[t], parcels.at[t], plocal)
    keep.start()
    copies = []
    for k in range(1, TOK):
        peer = lax.rem(t + k, TOK)
        copy = remote(packed.at[peer], parcels.at[t], psend.at[k - 1], precv.at[k - 1], {"tok": peer})
        copy.start()
        copies.append(copy)
    begin()
    slots = lax.broadcasted_iota(jnp.int32, (ROWS, TOK * SPACE), 1)
    pick = (slots == spot[...]).astype(BF16)
    keep.wait()
    for k in range(1, TOK):
        origin = lax.rem(t + TOK - k, TOK)
        remote(packed.at[t], parcels.at[origin], psend.at[k - 1], precv.at[k - 1], {"tok": origin}).wait_recv()
    own[:ROWS] = dot(pick, parcels[...].reshape(TOK * SPACE, WIDTH)).astype(BF16)
    for copy in copies:
        copy.wait_send()


def embed_kernel(sparse, count, *refs):
    slots, store, *refs = refs
    inputs, refs = refs[:count], refs[count:]
    priors, result, whole, in_pages, results, own, gsend, grecv, glocal, out_pages, tsend, trecv, tlocal, wsend, wrecv, wlocal, *rest = refs
    greet(tok_peers() + grp_peers())
    steps = gather_tok(result, results, pl.ds(0, 256), pl.ds(256, 256), wsend, wrecv, wlocal)
    keeps = []

    def begin():
        steps[0]()
        own[ROWS:] = priors[...]

        @pl.loop(0, TOK)
        def _(peer):
            page = store[slots[peer]]

            def put(pair, row, value):
                out_pages[peer, pair, pl.ds(row, 16)] = value.astype(BF16)

            pair_page(page, put)

        keeps.append(trade_start(out_pages, in_pages, tsend, trecv, tlocal))

    (sparse_rows if sparse else dense_rows)(*inputs, own, begin, *rest)
    gather_grp(own, whole, gsend, grecv, glocal, steps[1:4])
    steps[4]()
    trade_end(out_pages, in_pages, tsend, trecv, keeps[0])


def embed_exchange(sparse, slots, store, inputs, priors, result):
    rows = ROWS + 2 * BRANCH
    h, m = WIDTH // 2, ROWS // 2
    if sparse:
        scratch = [
            pltpu.VMEM((TOK, SPACE, WIDTH), BF16),
            pltpu.SemaphoreType.DMA((TOK - 1,)),
            pltpu.SemaphoreType.DMA((TOK - 1,)),
            pltpu.SemaphoreType.DMA,
        ]
    else:
        scratch = [
            pltpu.VMEM((2, 2, ROWS, h), BF16),
            pltpu.VMEM((2, 4, ROWS, h), BF16),
            pltpu.VMEM((2, 4, ROWS, h), BF16),
            pltpu.VMEM((2, 2, ROWS, h), BF16),
            pltpu.VMEM((2, 4, ROWS, h), BF16),
            pltpu.VMEM((2, 4, ROWS, h), BF16),
            pltpu.VMEM((4, ROWS, h), BF16),
            pltpu.VMEM((2, m, h), BF16),
            pltpu.VMEM((2, ROWS, h), BF16),
            pltpu.VMEM((2, ROWS, h), BF16),
            pltpu.VMEM((4, ROWS, h), BF16),
            pltpu.VMEM((2, m, h), BF16),
            pltpu.VMEM((2, ROWS, h), BF16),
            pltpu.VMEM((2, ROWS, h), BF16),
            pltpu.SemaphoreType.DMA((16,)),
            pltpu.SemaphoreType.DMA((16,)),
        ]
    return pl.pallas_call(
        functools.partial(embed_kernel, sparse, len(inputs)),
        out_shape=(
            jax.ShapeDtypeStruct((rows, HIDDEN), BF16),
            jax.ShapeDtypeStruct((TOK, PAIRS, HEAD, 128), BF16),
            jax.ShapeDtypeStruct((4, WIDTH, 1024), BF16),
        ),
        in_specs=[pl.BlockSpec(memory_space=pltpu.SMEM)] + [VMEM] * (len(inputs) + 2) + [ANY],
        out_specs=(ANY, ANY, ANY),
        scratch_shapes=[
            pltpu.VMEM((rows, WIDTH), BF16),
            pltpu.SemaphoreType.DMA((9,)),
            pltpu.SemaphoreType.DMA((9,)),
            pltpu.SemaphoreType.DMA,
            pltpu.VMEM((TOK, PAIRS, HEAD, 128), BF16),
            *TRADE_SEMAPHORES,
            pltpu.SemaphoreType.DMA((16,)),
            pltpu.SemaphoreType.DMA((16,)),
            pltpu.SemaphoreType.DMA,
            *scratch,
        ],
        compiler_params=pltpu.CompilerParams(
            collective_id=1 if sparse else 4, has_side_effects=True, vmem_limit_bytes=40 << 20
        ),
        cost_estimate=pl.CostEstimate(flops=0, transcendentals=0, bytes_accessed=100 << 20),
        name="embed_sparse" if sparse else "embed_dense",
    )(slots, store, *inputs, priors, result)


def pack_kernel(place, ids, table, packed, spot, most, slot_s):
    t_at = place[0]
    shape = (ROWS, ROWS)
    sub = lax.broadcasted_iota(jnp.int32, shape, 0)
    lane = lax.broadcasted_iota(jnp.int32, shape, 1)
    vocab_rows = table.shape[0]
    base = t_at * vocab_rows

    def column(row):
        return jnp.sum(jnp.where(sub == lane, jnp.broadcast_to(row, shape), 0), axis=1, keepdims=True)

    def ranks(row):
        col = column(row)
        same = col == row
        first_col = 1 - jnp.max(jnp.where(same & (lane < sub), 1, 0), axis=1, keepdims=True)
        first_row = 1 - jnp.max(jnp.where(same & (sub < lane), 1, 0), axis=0, keepdims=True)
        start = row - lax.rem(row, vocab_rows)
        ahead = (col < row) & (col >= start)
        rank = jnp.sum(jnp.where(ahead, first_col, 0), axis=0, keepdims=True)
        return first_row, start, rank

    def one(t, top):
        row = ids[pl.ds(t, 1), :]
        first_row, start, rank = ranks(row)
        mine = (first_row > 0) & (start == base)
        slot = lax.broadcasted_iota(jnp.int32, (SPACE, ROWS), 0)
        hit = (slot == rank) & mine
        slot_s[pl.ds(pl.multiple_of(t * SPACE, SPACE), SPACE)] = (
            jnp.sum(jnp.where(hit, row - base + 1, 0), axis=1, keepdims=True) - 1
        )

        @pl.when(t == t_at)
        def _():
            owner = start // vocab_rows
            spot[...] = column(owner * SPACE + rank)

        return jnp.maximum(top, rank)

    top = lax.fori_loop(0, TOK, one, jnp.zeros((1, ROWS), jnp.int32))
    most[...] = jnp.broadcast_to(jnp.max(top, axis=1, keepdims=True) + 1, (8, 128))
    step = 256
    for k in range(TOK * SPACE // step):
        rows = pl.ds(k * step, step)
        pick = (
            lax.broadcasted_iota(jnp.int32, (step, vocab_rows), 1) == slot_s[rows]
        ).astype(BF16)
        packed[rows] = dot(pick, table[...]).astype(BF16)


def pack(place, ids, table):
    return pl.pallas_call(
        pack_kernel,
        out_shape=(
            jax.ShapeDtypeStruct((TOK * SPACE, WIDTH), BF16),
            jax.ShapeDtypeStruct((ROWS, 1), jnp.int32),
            jax.ShapeDtypeStruct((8, 128), jnp.int32),
        ),
        in_specs=[pl.BlockSpec(memory_space=pltpu.SMEM), VMEM, VMEM],
        out_specs=(VMEM, VMEM, VMEM),
        scratch_shapes=[pltpu.VMEM((TOK * SPACE, 1), jnp.int32)],
        compiler_params=pltpu.CompilerParams(vmem_limit_bytes=32 << 20),
        cost_estimate=pl.CostEstimate(flops=2 << 30, transcendentals=0, bytes_accessed=4 << 20),
        name="pack",
    )(place, ids, table)


def residual_kernel(part, base, out_pages, whole, own_out, in_pages, mated, sums, halves, full, rsend, rrecv, own, gsend, grecv, glocal, tsend, trecv, tlocal):
    greet(tok_peers() + grp_peers())
    keep = trade_start(out_pages, in_pages, tsend, trecv, tlocal)
    total = reduce_grp(part, mated, sums, halves, full, rsend, rrecv)
    own[...] = (base[...].astype(F32) + total).astype(BF16)
    own_out[...] = own[...]
    gather_grp(own, whole, gsend, grecv, glocal)
    trade_end(out_pages, in_pages, tsend, trecv, keep)


def residual_exchange(part, base, out_pages):
    return pl.pallas_call(
        residual_kernel,
        out_shape=(
            jax.ShapeDtypeStruct((ROWS, HIDDEN), BF16),
            jax.ShapeDtypeStruct((ROWS, WIDTH), BF16),
            jax.ShapeDtypeStruct((TOK, PAIRS, HEAD, 128), BF16),
        ),
        in_specs=[VMEM, VMEM, ANY],
        out_specs=(ANY, VMEM, ANY),
        scratch_shapes=[
            *REDUCE_SCRATCH,
            pltpu.VMEM((ROWS, WIDTH), BF16),
            pltpu.SemaphoreType.DMA((9,)),
            pltpu.SemaphoreType.DMA((9,)),
            pltpu.SemaphoreType.DMA,
            *TRADE_SEMAPHORES,
        ],
        compiler_params=pltpu.CompilerParams(
            collective_id=2, has_side_effects=True, vmem_limit_bytes=40 << 20
        ),
        cost_estimate=pl.CostEstimate(flops=0, transcendentals=0, bytes_accessed=80 << 20),
        name="residual_exchange",
    )(part, base, out_pages)


def final_kernel(source, hit, part, base, gate, returned, store, out, store_out, mated, sums, halves, full, rsend, rrecv):
    greet(grp_peers())

    def pages():
        @pl.loop(0, TOK)
        def _(slot):
            page = returned[source[slot]].astype(F32)
            taken = hit[slot] > 0

            def put(column, value):
                columns = pl.ds(column, 128)
                store_out[slot, :, columns] = jnp.where(taken, value, store[slot, :, columns])

            flat_page(page, put)

    total = reduce_grp(part, mated, sums, halves, full, rsend, rrecv, pages)
    out[...] = (base[...].astype(F32) + gate[...] * total).astype(BF16)


def final_exchange(source, hit, part, base, gate, returned, store):
    smem = pl.BlockSpec(memory_space=pltpu.SMEM)
    return pl.pallas_call(
        final_kernel,
        out_shape=(
            jax.ShapeDtypeStruct((ROWS, WIDTH), BF16),
            jax.ShapeDtypeStruct(store.shape, F32),
        ),
        in_specs=[smem, smem, VMEM, VMEM, VMEM, VMEM, VMEM],
        out_specs=(VMEM, VMEM),
        scratch_shapes=REDUCE_SCRATCH,
        compiler_params=pltpu.CompilerParams(
            collective_id=3, has_side_effects=True, vmem_limit_bytes=40 << 20
        ),
        cost_estimate=pl.CostEstimate(flops=0, transcendentals=0, bytes_accessed=40 << 20),
        name="final_exchange",
    )(source, hit, part, base, gate, returned, store)


def dot(a, b):
    return jnp.dot(a, b, preferred_element_type=F32)


def row_stats(rows_of, mean, scale):
    value = rows_of.astype(F32)
    middle = jnp.mean(value, axis=-1, keepdims=True)
    centered = value - middle
    spread = jnp.mean(centered * centered, axis=-1, keepdims=True)
    mean[...] = middle
    scale[...] = lax.rsqrt(spread + EPSILON)


def normed_and_step(block, prior, mean, scale, gain):
    normed = (block.astype(F32) - mean) * scale * gain
    row = lax.broadcasted_iota(jnp.int32, (ROWS, WIDTH), 0)
    spread = (
        lax.broadcasted_iota(jnp.int32, (ROWS, BRANCH), 0) // DRAFT
        == lax.broadcasted_iota(jnp.int32, (ROWS, BRANCH), 1)
    )
    carried = dot(spread.astype(BF16), prior)
    before = jnp.where(lax.rem(row, DRAFT) == 0, carried, pltpu.roll(normed, 1, axis=0))
    return normed, before - normed


def kept_row(normed, prior, kept_column):
    column = lax.broadcasted_iota(jnp.int32, (BRANCH, ROWS), 1)
    branch = lax.broadcasted_iota(jnp.int32, (BRANCH, ROWS), 0)
    pick = (column == branch * DRAFT + kept_column - 1) & (kept_column > 0)
    picked = dot(pick.astype(BF16), normed.astype(BF16))
    return jnp.where(kept_column > 0, picked, prior.astype(F32)).astype(BF16)


def head_ones(size):
    return (
        lax.broadcasted_iota(jnp.int32, (size, size), 0) // HEAD
        == lax.broadcasted_iota(jnp.int32, (size, size), 1) // HEAD
    ).astype(BF16)


def per_head(value):
    ones = head_ones(256)
    return jnp.concatenate([dot(value[:, :256], ones), dot(value[:, 256:], ones)], axis=1)


def per_head_fine(value):
    top = value.astype(BF16)
    rest = (value - top.astype(F32)).astype(BF16)
    return per_head(top) + per_head(rest)


def two_heads(page):
    side = lax.broadcasted_iota(jnp.int32, (HEAD, 128), 1) < HEAD
    none = jnp.zeros_like(page)
    return jnp.concatenate([jnp.where(side, page, none), jnp.where(side, none, page)], axis=0)


def attention_kernel(
    place, owner_of, request_of, winner, kept,
    xw, gain1, blend, weights, narrow, widen, baseline, boost, gain2, kept_column, pages, results,
    part, chosen, shift,
    result_s, result_sem, mean, scale, acc, low, r_s, k_s, v_s, w_s, y_s, p_s,
):
    step = pl.program_id(0)

    fetch = pltpu.make_async_copy(results, result_s, result_sem)

    @pl.when(step == 0)
    def _():
        fetch.start()
        row_stats(xw[:ROWS], mean, scale)
        acc[...] = jnp.zeros_like(acc)
        low[...] = jnp.zeros_like(low)

    columns = pl.ds(pl.multiple_of(step * WIDTH, WIDTH), WIDTH)
    prior = xw[ROWS : ROWS + BRANCH, columns]
    normed, delta = normed_and_step(xw[:ROWS, columns], prior, mean[...], scale[...], gain1[0:1])

    @pl.when(step == place[0])
    def _():
        shift[...] = kept_row(normed, prior, kept_column[...])

    for c in range(4):
        acc[c] += dot((normed + delta * blend[c : c + 1]).astype(BF16), weights[c])
    low[...] += dot((normed + delta * blend[4:5]).astype(BF16), narrow[...])

    @pl.when(step == GRP - 1)
    def _():
        lowrank = jnp.tanh(low[...]).astype(BF16)
        w_s[...] = jnp.exp(-jnp.exp(baseline[...] + dot(lowrank, widen[...])))
        r_s[...] = acc[0]
        k_s[...] = acc[1]
        v_s[...] = acc[2]
        shape3 = (BRANCH, DRAFT, WIDTH)
        r3, k3 = r_s[...].reshape(shape3), k_s[...].reshape(shape3)
        v3, w3 = v_s[...].reshape(shape3), w_s[...].reshape(shape3)
        position = lax.broadcasted_iota(jnp.int32, shape3, 1)
        y_s[...] = per_head_fine(r_s[...] * boost[...] * k_s[...]) * v_s[...]
        p_s[...] = jnp.ones_like(p_s)
        for s in range(DRAFT - 2, -1, -1):
            decay = jnp.where(position > s + 1, p_s[...].reshape(shape3) * w3[:, s + 1 : s + 2], 1.0)
            p_s[...] = decay.reshape(ROWS, WIDTH)
            term = jnp.where(position > s, r3 * decay * k3[:, s : s + 1], 0.0)
            score = per_head(term.reshape(ROWS, WIDTH).astype(BF16)).reshape(shape3)
            y_s[...] += (score * v3[:, s : s + 1]).reshape(ROWS, WIDTH)
        decay = jnp.where(position > 0, p_s[...].reshape(shape3) * w3[:, 0:1], 1.0)
        p_s[...] = r_s[...] * decay.reshape(ROWS, WIDTH)
        for b in range(BRANCH):
            rows = pl.ds(b * DRAFT, DRAFT)
            for pair in range(PAIRS):
                lanes = pl.ds(pair * 128, 128)
                y_s[rows, lanes] += dot(p_s[rows, lanes].astype(BF16), two_heads(pages[owner_of[request_of[b]], pair]))
        y = y_s[...]
        centered = y - per_head_fine(y) * (1.0 / HEAD)
        spread = per_head_fine(centered * centered) * (1.0 / HEAD)
        gate = acc[3]
        gate = gate * jax.nn.sigmoid(gate)
        attended = (centered * lax.rsqrt(spread + HEAD_EPSILON) * gain2[...] * gate).astype(BF16)
        fetch.wait()
        for y_of in range(4):
            part[:, y_of * 1024 : y_of * 1024 + 1024] = dot(attended, result_s[y_of]).astype(BF16)
        eye = (
            lax.broadcasted_iota(jnp.int32, (128, 128), 0)
            == lax.broadcasted_iota(jnp.int32, (128, 128), 1)
        )
        spot = lax.broadcasted_iota(jnp.int32, (DRAFT, WIDTH), 0)
        for q in range(REQ):
            b = winner[q]
            count = kept[b]
            rows = pl.ds(pl.multiple_of(b * DRAFT, DRAFT), DRAFT)
            live = spot < count
            tail = jnp.where(live, w_s[rows], 1.0)
            for hop in (1, 2, 4, 8):
                later = pltpu.roll(tail, DRAFT - hop, axis=0)
                tail = tail * jnp.where(spot < DRAFT - hop, later, 1.0)
            after = jnp.where(spot < DRAFT - 1, pltpu.roll(tail, DRAFT - 1, axis=0), 1.0)
            keys = jnp.where(live, k_s[rows], 0.0) * after
            values = v_s[rows].astype(BF16)
            for pair in range(PAIRS):
                lanes = slice(pair * 128, pair * 128 + 128)
                fade = jnp.where(eye, tail[0:1, lanes], 0.0)
                left = jnp.concatenate([keys[:, lanes], fade], axis=0).astype(BF16)
                right = jnp.concatenate([values[:, lanes], two_heads(pages[owner_of[q], pair])], axis=0)
                both = lax.dot_general(
                    left, right, (((0,), (0,)), ((), ())), preferred_element_type=F32
                )
                side = lax.broadcasted_iota(jnp.int32, (HEAD, 128), 1) < HEAD
                chosen[q, pair] = jnp.where(side, both[:HEAD], both[HEAD:]).astype(BF16)


def attention(place, owner_of, request_of, winner, kept, xw, scales, blends, weights, narrow, widen, baseline, boost, pages, results):
    rows = xw.shape[0]
    full = lambda *shape: pl.BlockSpec(shape, lambda k, *_: (0,) * len(shape))
    mine = pl.BlockSpec((1, WIDTH), lambda k, at, *_: (0, at[0]))
    return pl.pallas_call(
        attention_kernel,
        out_shape=(
            jax.ShapeDtypeStruct((ROWS, HIDDEN), BF16),
            jax.ShapeDtypeStruct((REQ, PAIRS, HEAD, 128), BF16),
            jax.ShapeDtypeStruct((BRANCH, WIDTH), BF16),
        ),
        grid_spec=pltpu.PrefetchScalarGridSpec(
            num_scalar_prefetch=5,
            grid=(GRP,),
            in_specs=[
                full(rows, HIDDEN),
                pl.BlockSpec((3, WIDTH), lambda k, *_: (0, k)),
                pl.BlockSpec((7, WIDTH), lambda k, *_: (0, k)),
                pl.BlockSpec((4, WIDTH, WIDTH), lambda k, *_: (0, k, 0)),
                pl.BlockSpec((WIDTH, 128), lambda k, *_: (k, 0)),
                full(128, WIDTH),
                mine,
                mine,
                mine,
                full(BRANCH, 1),
                full(TOK, PAIRS, HEAD, 128),
                ANY,
            ],
            out_specs=(
                full(ROWS, HIDDEN),
                full(REQ, PAIRS, HEAD, 128),
                full(BRANCH, WIDTH),
            ),
            scratch_shapes=[
                pltpu.VMEM((4, WIDTH, 1024), BF16),
                pltpu.SemaphoreType.DMA,
                pltpu.VMEM((ROWS, 1), F32),
                pltpu.VMEM((ROWS, 1), F32),
                pltpu.VMEM((4, ROWS, WIDTH), F32),
                pltpu.VMEM((ROWS, 128), F32),
            ]
            + [pltpu.VMEM((ROWS, WIDTH), F32)] * 6,
        ),
        compiler_params=pltpu.CompilerParams(vmem_limit_bytes=52 << 20),
        cost_estimate=pl.CostEstimate(flops=6 << 30, transcendentals=1 << 20, bytes_accessed=24 << 20),
        name="attention",
    )(
        place, owner_of, request_of, winner, kept,
        xw, scales, blends, weights, narrow, widen,
        baseline.reshape(1, HIDDEN), boost.reshape(1, HIDDEN), scales[2:3],
        kept.reshape(BRANCH, 1), pages, results,
    )


def feedforward_kernel(place, rw, prior_ref, gain, blend, weights, kept_column, part, gate, shift, mean, scale, acc, content):
    step = pl.program_id(0)

    @pl.when(step == 0)
    def _():
        row_stats(rw[...], mean, scale)
        acc[...] = jnp.zeros_like(acc)

    columns = pl.ds(pl.multiple_of(step * WIDTH, WIDTH), WIDTH)
    prior = prior_ref[...]
    normed, delta = normed_and_step(rw[:, columns], prior, mean[...], scale[...], gain[1:2])

    @pl.when(step == place[0])
    def _():
        shift[...] = kept_row(normed, prior, kept_column[...])

    acc[:, :KEYS] += dot((normed + delta * blend[5:6]).astype(BF16), weights[:, KEYS : 2 * KEYS])
    acc[:, KEYS:] += dot((normed + delta * blend[6:7]).astype(BF16), weights[:, 2 * KEYS :])
    content[columns] = weights[:, :KEYS]

    @pl.when(step == GRP - 1)
    def _():
        gate[...] = jax.nn.sigmoid(acc[:, KEYS:])
        hidden = jnp.square(jnp.maximum(acc[:, :KEYS], 0.0)).astype(BF16)
        for g in range(GRP):
            lanes = slice(g * WIDTH, g * WIDTH + WIDTH)
            part[:, lanes] = lax.dot_general(
                hidden, content[lanes], (((1,), (1,)), ((), ())), preferred_element_type=F32
            ).astype(BF16)


def feedforward(place, rw, prior, scales, blends, weights, kept):
    full = lambda *shape: pl.BlockSpec(shape, lambda k, *_: (0,) * len(shape))
    return pl.pallas_call(
        feedforward_kernel,
        out_shape=(
            jax.ShapeDtypeStruct((ROWS, HIDDEN), BF16),
            jax.ShapeDtypeStruct((ROWS, WIDTH), F32),
            jax.ShapeDtypeStruct((BRANCH, WIDTH), BF16),
        ),
        grid_spec=pltpu.PrefetchScalarGridSpec(
            num_scalar_prefetch=1,
            grid=(GRP,),
            in_specs=[
                full(ROWS, HIDDEN),
                pl.BlockSpec((BRANCH, WIDTH), lambda k, *_: (0, k)),
                pl.BlockSpec((3, WIDTH), lambda k, *_: (0, k)),
                pl.BlockSpec((7, WIDTH), lambda k, *_: (0, k)),
                pl.BlockSpec((WIDTH, 2 * KEYS + WIDTH), lambda k, *_: (k, 0)),
                full(BRANCH, 1),
            ],
            out_specs=(full(ROWS, HIDDEN), full(ROWS, WIDTH), full(BRANCH, WIDTH)),
            scratch_shapes=[
                pltpu.VMEM((ROWS, 1), F32),
                pltpu.VMEM((ROWS, 1), F32),
                pltpu.VMEM((ROWS, KEYS + WIDTH), F32),
                pltpu.VMEM((HIDDEN, KEYS), BF16),
            ],
        ),
        compiler_params=pltpu.CompilerParams(vmem_limit_bytes=52 << 20),
        cost_estimate=pl.CostEstimate(flops=5 << 30, transcendentals=1 << 18, bytes_accessed=24 << 20),
        name="feedforward",
    )(place, rw, prior, scales, blends, weights, kept.reshape(BRANCH, 1))


def body(
    guess_symbol_ids,
    symbol_vector_lookup,
    prior_attention_normed,
    prior_feedforward_normed,
    layernorm_scales,
    lagged_blend_ratios,
    attention_matrices,
    forgetting_baseline_vector,
    forgetting_narrow_matrix,
    forgetting_widen_matrix,
    diagonal_boost,
    attention_result_matrix,
    feedforward_lookup_matrix,
    feedforward_content_matrix,
    feedforward_gating_matrix,
    memory_matrix_store,
    query_memory_slot,
    candidate_tally_each_query,
    kept_guess_tally,
):
    tok_at = lax.axis_index("tok")
    grp_at = lax.axis_index("grp")
    place = grp_at.reshape(1)
    vocab_rows = symbol_vector_lookup.shape[0]
    slot_count = memory_matrix_store.shape[0]

    weights = lax.all_gather(
        jnp.concatenate(
            [feedforward_content_matrix.T, feedforward_lookup_matrix, feedforward_gating_matrix], axis=1
        ),
        "tok",
        axis=0,
        tiled=True,
    )
    priors = jnp.concatenate([prior_attention_normed, prior_feedforward_normed], axis=0)

    owners = (query_memory_slot // slot_count).reshape(TOK, REQ)
    places = (query_memory_slot % slot_count).reshape(TOK, REQ)
    owned_here = owners == tok_at
    send_slot = jnp.sum(jnp.where(owned_here, places, 0), axis=1)
    sending = jnp.any(owned_here, axis=1)
    packed, spot, most = pack(
        tok_at.reshape(1), guess_symbol_ids.reshape(TOK, ROWS), symbol_vector_lookup
    )

    def sparse(_):
        return embed_exchange(
            True, send_slot, memory_matrix_store, (packed.reshape(TOK, SPACE, WIDTH), spot), priors,
            attention_result_matrix,
        )

    def dense(_):
        wanted = guess_symbol_ids - tok_at * vocab_rows
        inside = (wanted >= 0) & (wanted < vocab_rows)
        found = jnp.take(symbol_vector_lookup, jnp.clip(wanted, 0, vocab_rows - 1), axis=0)
        found = jnp.where(inside[:, None], found, jnp.zeros((), BF16)).reshape(4, 4, ROWS, WIDTH)
        return embed_exchange(
            False, send_slot, memory_matrix_store, (found,), priors, attention_result_matrix
        )

    whole, pages, results = lax.cond(most[0, 0] <= SPACE, sparse, dense, 0)

    my_owners = lax.dynamic_index_in_dim(owners, tok_at, 0, keepdims=False)
    my_counts = lax.dynamic_index_in_dim(candidate_tally_each_query, tok_at, 0, keepdims=False)
    local_ids = jnp.arange(BRANCH, dtype=jnp.int32)
    request_ends = jnp.cumsum(my_counts)
    request_of = jnp.sum((request_ends[None, :] <= local_ids[:, None]).astype(jnp.int32), axis=1)
    branch_score = kept_guess_tally * BRANCH + (BRANCH - 1 - local_ids)
    member = request_of[None, :] == jnp.arange(REQ, dtype=jnp.int32)[:, None]
    best_score = jnp.max(jnp.where(member, branch_score[None, :], -1), axis=1)
    winner = BRANCH - 1 - best_score % BRANCH

    partial_att, new_pages, shift_att_out = attention(
        place, my_owners, request_of, winner, kept_guess_tally,
        whole, layernorm_scales, lagged_blend_ratios, attention_matrices,
        forgetting_narrow_matrix, forgetting_widen_matrix,
        forgetting_baseline_vector, diagonal_boost, pages, results,
    )

    targets = my_owners[None, :] == jnp.arange(TOK, dtype=jnp.int32)[:, None]
    pick_index = jnp.sum(
        jnp.where(targets, jnp.arange(REQ, dtype=jnp.int32)[None, :], 0), axis=1
    )
    outgoing_back = jnp.take(new_pages, pick_index, axis=0)

    own_x = lax.dynamic_slice(whole, (0, grp_at * WIDTH), (ROWS, WIDTH))
    residual_whole, residual, returned = residual_exchange(partial_att, own_x, outgoing_back)

    partial_ffn, gate, shift_ffn_out = feedforward(
        place, residual_whole, whole[ROWS + BRANCH :], layernorm_scales, lagged_blend_ratios,
        weights, kept_guess_tally,
    )
    hit = (send_slot[None, :] == jnp.arange(slot_count, dtype=jnp.int32)[:, None]) & sending[None, :]
    source = jnp.sum(jnp.where(hit, jnp.arange(TOK, dtype=jnp.int32)[None, :], 0), axis=1)
    layer_out, store_out = final_exchange(
        source, jnp.any(hit, axis=1).astype(jnp.int32), partial_ffn, residual, gate, returned,
        memory_matrix_store,
    )
    return (layer_out, shift_att_out, shift_ffn_out, store_out)


def solution(mesh):
    in_specs = (
        P(),
        P("tok", "grp"),
        P("tok", "grp"),
        P("tok", "grp"),
        P(),
        P(),
        P(None, None, "grp"),
        P(),
        P(),
        P(None, "grp"),
        P(),
        P("grp", "tok"),
        P("tok", "grp"),
        P("grp", "tok"),
        P("tok", "grp"),
        P("tok", "grp", None),
        P(),
        P(),
        P("tok"),
    )
    out_specs = (P("tok", "grp"), P("tok", "grp"), P("tok", "grp"), P("tok", "grp", None))
    return jax.shard_map(body, mesh=mesh, in_specs=in_specs, out_specs=out_specs, check_vma=False)
```

```python
import functools

import jax
import jax.numpy as jnp
from jax import lax
from jax.experimental import pallas as pl
from jax.experimental.pallas import tpu as pltpu
from jax.sharding import PartitionSpec as P

HIDDEN = 4096
HEAD = 64
DRAFT = 16
BRANCH = 16
ROWS = BRANCH * DRAFT
WIDTH = 512
TOK = 16
GRP = 8
REQ = 8
PAIRS = 4
KEYS = 896
SPACE = 48
EPSILON = 1e-05
HEAD_EPSILON = 0.00064
F32 = jnp.float32
BF16 = jnp.bfloat16
MESH = pl.DeviceIdType.MESH
ANY = pl.BlockSpec(memory_space=pl.ANY)
VMEM = pl.BlockSpec(memory_space=pltpu.VMEM)


def remote(src, dst, send, recv, device):
    return pltpu.make_async_remote_copy(
        src_ref=src, dst_ref=dst, send_sem=send, recv_sem=recv, device_id=device, device_id_type=MESH
    )


def greet(devices):
    barrier = pltpu.get_barrier_semaphore()
    for device in devices:
        pl.semaphore_signal(barrier, inc=1, device_id=device, device_id_type=MESH)
    pl.semaphore_wait(barrier, len(devices))


def grp_places():
    g = lax.axis_index("grp")
    z, core = g // 2, g % 2
    up = lax.rem(z + 1, 4) * 2 + core
    down = lax.rem(z + 3, 4) * 2 + core
    far = lax.rem(z + 2, 4) * 2 + core
    mate = z * 2 + 1 - core
    return g, up, down, far, mate


def block_of(g):
    return pl.ds(pl.multiple_of(g * WIDTH, WIDTH), WIDTH)


def flip(g):
    return g + 1 - 2 * lax.rem(g, 2)


def gather_grp(own, out, send, recv, local, between=()):
    between = list(between)

    def aside():
        if between:
            between.pop(0)()

    rows = out.shape[0]
    half = rows // 2
    g, up, down, far, mate = grp_places()
    first, last, whole = pl.ds(0, half), pl.ds(half, rows - half), pl.ds(0, rows)
    at = lambda part, g_of: out.at[part, block_of(g_of)]
    keep = pltpu.make_async_copy(own, at(whole, g), local)
    keep.start()
    started = []

    def go(index, src, part, g_of, target):
        copy = remote(src, at(part, g_of), send.at[index], recv.at[index], {"grp": target})
        copy.start()
        started.append(copy)

    def came(index, part, g_of):
        remote(at(part, g_of), at(part, g_of), send.at[index], recv.at[index], {"grp": mate}).wait_recv()

    go(0, own, whole, g, up)
    go(1, own, whole, g, down)
    go(2, own, whole, g, mate)
    aside()
    came(0, whole, down)
    go(3, at(first, down), first, down, up)
    go(5, at(whole, down), whole, down, mate)
    came(1, whole, up)
    go(4, at(last, up), last, up, down)
    go(6, at(whole, up), whole, up, mate)
    aside()
    came(3, first, far)
    go(7, at(first, far), first, far, mate)
    came(4, last, far)
    go(8, at(last, far), last, far, mate)
    came(2, whole, mate)
    came(5, whole, flip(down))
    came(6, whole, flip(up))
    came(7, first, flip(far))
    came(8, last, flip(far))
    while between:
        aside()
    keep.wait()
    for copy in started:
        copy.wait_send()


def reduce_grp(part, mated, sums, halves, full, send, recv, meanwhile=lambda: None):
    g, up, down, far, mate = grp_places()
    half = ROWS // 2
    started = []

    def go(index, src, dst, target):
        copy = remote(src, dst, send.at[index], recv.at[index], {"grp": target})
        copy.start()
        started.append(copy)

    def came(index, dst):
        remote(dst, dst, send.at[index], recv.at[index], {"grp": mate}).wait_recv()

    order = (far, up, down, g)
    for k in range(4):
        go(k, part.at[:, block_of(flip(order[k]))], mated.at[k], mate)

    def own(k):
        return part[:, block_of(order[k])].astype(F32) + mated[k].astype(F32)

    came(0, mated.at[0])
    sums[0] = own(0).astype(BF16)
    go(4, sums.at[0, pl.ds(0, half)], halves.at[0], up)
    go(5, sums.at[0, pl.ds(half, half)], halves.at[1], down)
    came(1, mated.at[1])
    came(4, halves.at[0])
    sums[1, :half] = (own(1)[:half] + halves[0].astype(F32)).astype(BF16)
    sums[1, half:] = own(1)[half:].astype(BF16)
    go(6, sums.at[1], full.at[0], up)
    came(2, mated.at[2])
    came(5, halves.at[1])
    sums[2, :half] = own(2)[:half].astype(BF16)
    sums[2, half:] = (own(2)[half:] + halves[1].astype(F32)).astype(BF16)
    go(7, sums.at[2], full.at[1], down)
    meanwhile()
    came(3, mated.at[3])
    came(6, full.at[0])
    came(7, full.at[1])
    total = own(3) + full[0].astype(F32) + full[1].astype(F32)
    for copy in started:
        copy.wait_send()
    return total


REDUCE_SCRATCH = [
    pltpu.VMEM((4, ROWS, WIDTH), BF16),
    pltpu.VMEM((3, ROWS, WIDTH), BF16),
    pltpu.VMEM((2, ROWS // 2, WIDTH), BF16),
    pltpu.VMEM((2, ROWS, WIDTH), BF16),
    pltpu.SemaphoreType.DMA((8,)),
    pltpu.SemaphoreType.DMA((8,)),
]


def result_views(out):
    cols = lambda x_of: pl.ds(pl.multiple_of(x_of * 256, 256), 256)
    return (
        lambda rows, y_of, x_of: out.at[y_of, rows, cols(x_of)],
        lambda rows, y_of: out.at[y_of, rows],
        lambda rows, x_of: out.at[:, rows, cols(x_of)],
    )


def stack_views(out):
    return (
        lambda rows, y_of, x_of: out.at[y_of, x_of, rows],
        lambda rows, y_of: out.at[y_of, :, rows],
        lambda rows, x_of: out.at[:, x_of, rows],
    )


def gather_tok(own, views, send, recv, local):
    t = lax.axis_index("tok")
    y, x = t // 4, lax.rem(t, 4)
    xu, xd, xf = [lax.rem(x + k, 4) for k in (1, 3, 2)]
    yu, yd, yf = [lax.rem(y + k, 4) for k in (1, 3, 2)]
    along_x = lambda x_of: {"tok": y * 4 + x_of}
    along_y = lambda y_of: {"tok": y_of * 4 + x}
    one, wide, tall = views
    count = own.shape[0]
    f0, f1 = pl.ds(0, count // 2), pl.ds(count // 2, count // 2)
    fa, fb = [pl.ds(f0.start + k * (f0.size // 2), f0.size // 2) for k in (0, 1)]
    la, lb = [pl.ds(f1.start + k * (f1.size // 2), f1.size // 2) for k in (0, 1)]
    started = []

    def go(index, src, dst, target):
        copy = remote(src, dst, send.at[index], recv.at[index], target)
        copy.start()
        started.append(copy)

    def came(index, dst):
        remote(dst, dst, send.at[index], recv.at[index], along_x(xu)).wait_recv()

    keep = pltpu.make_async_copy(own, one(pl.ds(0, count), y, x), local)

    def begin():
        keep.start()
        go(0, own.at[f0], one(f0, y, x), along_x(xu))
        go(1, own.at[f0], one(f0, y, x), along_x(xd))
        go(2, own.at[f1], one(f1, y, x), along_y(yu))
        go(3, own.at[f1], one(f1, y, x), along_y(yd))

    def relay():
        came(0, one(f0, y, xd))
        go(4, one(fa, y, xd), one(fa, y, xd), along_x(xu))
        came(2, one(f1, yd, x))
        go(6, one(la, yd, x), one(la, yd, x), along_y(yu))
        came(1, one(f0, y, xu))
        go(5, one(fb, y, xu), one(fb, y, xu), along_x(xd))
        came(3, one(f1, yu, x))
        go(7, one(lb, yu, x), one(lb, yu, x), along_y(yd))

    def turn():
        keep.wait()
        came(4, one(fa, y, xf))
        came(5, one(fb, y, xf))
        go(8, wide(f0, y), wide(f0, y), along_y(yu))
        go(9, wide(f0, y), wide(f0, y), along_y(yd))
        came(6, one(la, yf, x))
        came(7, one(lb, yf, x))
        go(10, tall(f1, x), tall(f1, x), along_x(xu))
        go(11, tall(f1, x), tall(f1, x), along_x(xd))

    def last():
        came(8, wide(f0, yd))
        go(12, wide(fa, yd), wide(fa, yd), along_y(yu))
        came(10, tall(f1, xd))
        go(14, tall(la, xd), tall(la, xd), along_x(xu))
        came(9, wide(f0, yu))
        go(13, wide(fb, yu), wide(fb, yu), along_y(yd))
        came(11, tall(f1, xu))
        go(15, tall(lb, xu), tall(lb, xu), along_x(xd))

    def end():
        came(12, wide(fa, yf))
        came(13, wide(fb, yf))
        came(14, tall(la, xf))
        came(15, tall(lb, xf))
        for copy in started:
            copy.wait_send()

    return begin, relay, turn, last, end


def grp_peers():
    _, up, down, _, mate = grp_places()
    return [{"grp": up}, {"grp": down}, {"grp": mate}]


def tok_peers():
    t = lax.axis_index("tok")
    return [{"tok": lax.rem(t + k, TOK)} for k in range(1, TOK)]


def page_masks():
    even = lax.rem(lax.broadcasted_iota(jnp.int32, (8, 128), 0), 2) == 0
    left = lax.broadcasted_iota(jnp.int32, (8, 128), 1) < HEAD
    return even, left


def pair_page(page, put):
    even, left = page_masks()
    for block in range(4):
        rows = [[] for _ in range(PAIRS)]
        for group in (2 * block, 2 * block + 1):
            pieces = []
            for m in range(4 * group, 4 * group + 4):
                here = page[:, m * 128 : m * 128 + 128]
                swapped = pltpu.roll(here, HEAD, axis=1)
                pieces += [jnp.where(even, here, swapped), jnp.where(even, swapped, here)]
            turned = jnp.swapaxes(jnp.stack(pieces), 0, 1)
            for pair in range(PAIRS):
                rows[pair].append(jnp.where(left, turned[2 * pair], turned[2 * pair + 1]))
        for pair in range(PAIRS):
            put(pair, 16 * block, jnp.concatenate(rows[pair], axis=0))


def flat_page(page, put):
    even, left = page_masks()
    for group in range(8):
        rows = [page[pair, 8 * group : 8 * group + 8] for pair in range(PAIRS)]
        turned = jnp.swapaxes(jnp.stack([rows[h // 2] for h in range(8)]), 0, 1)
        for m in range(4):
            first, second = turned[2 * m], turned[2 * m + 1]
            swapped_first = pltpu.roll(first, HEAD, axis=1)
            swapped_second = pltpu.roll(second, HEAD, axis=1)
            put(
                (4 * group + m) * 128,
                jnp.where(
                    left,
                    jnp.where(even, first, swapped_first),
                    jnp.where(even, swapped_second, second),
                ),
            )


def trade_start(out_pages, in_pages, send, recv, local):
    t = lax.axis_index("tok")
    keep = pltpu.make_async_copy(out_pages.at[t], in_pages.at[t], local)
    keep.start()
    for k in range(1, TOK):
        peer = lax.rem(t + k, TOK)
        remote(out_pages.at[peer], in_pages.at[t], send.at[k - 1], recv.at[k - 1], {"tok": peer}).start()
    return keep


def trade_end(out_pages, in_pages, send, recv, keep):
    t = lax.axis_index("tok")
    keep.wait()
    for k in range(1, TOK):
        peer = lax.rem(t + k, TOK)
        origin = lax.rem(t + TOK - k, TOK)
        copy = remote(out_pages.at[peer], in_pages.at[origin], send.at[k - 1], recv.at[k - 1], {"tok": peer})
        copy.wait_recv()
        copy.wait_send()


TRADE_SEMAPHORES = [
    pltpu.SemaphoreType.DMA((TOK - 1,)),
    pltpu.SemaphoreType.DMA((TOK - 1,)),
    pltpu.SemaphoreType.DMA,
]


def dense_rows(found, own, begin, a1h, a1s, a1f, b1h, b1s, b1f, a2, a2h, a2s, a2f, b2, b2h, b2s, b2f, xsend, xrecv):
    t = lax.axis_index("tok")
    y, x = t // 4, lax.rem(t, 4)
    xu, xd, xf = [lax.rem(x + k, 4) for k in (1, 3, 2)]
    yu, yd, yf = [lax.rem(y + k, 4) for k in (1, 3, 2)]
    along_x = lambda x_of: {"tok": y * 4 + x_of}
    along_y = lambda y_of: {"tok": y_of * 4 + x}
    started = []

    def go(index, src, dst, target):
        copy = remote(src, dst, xsend.at[index], xrecv.at[index], target)
        copy.start()
        started.append(copy)

    def came(index, dst):
        remote(dst, dst, xsend.at[index], xrecv.at[index], along_x(xu)).wait_recv()

    h = WIDTH // 2
    left, right = pl.ds(0, h), pl.ds(h, h)
    low, high = pl.ds(0, 2), pl.ds(2, 2)
    go(0, found.at[low, xf, :, left], a1h.at[0], along_x(xu))
    go(1, found.at[high, xf, :, left], a1h.at[1], along_x(xd))
    go(2, found.at[yf, low, :, right], b1h.at[0], along_y(yu))
    go(3, found.at[yf, high, :, right], b1h.at[1], along_y(yd))
    begin()
    came(0, a1h.at[0])
    a1s[0, :2] = found[:2, xu, :, :h] + a1h[0]
    a1s[0, 2:] = found[2:, xu, :, :h]
    go(4, a1s.at[0], a1f.at[0], along_x(xu))
    came(1, a1h.at[1])
    a1s[1, :2] = found[:2, xd, :, :h]
    a1s[1, 2:] = found[2:, xd, :, :h] + a1h[1]
    go(5, a1s.at[1], a1f.at[1], along_x(xd))
    came(2, b1h.at[0])
    b1s[0, :2] = found[yu, :2, :, h:] + b1h[0]
    b1s[0, 2:] = found[yu, 2:, :, h:]
    go(6, b1s.at[0], b1f.at[0], along_y(yu))
    came(3, b1h.at[1])
    b1s[1, :2] = found[yd, :2, :, h:]
    b1s[1, 2:] = found[yd, 2:, :, h:] + b1h[1]
    go(7, b1s.at[1], b1f.at[1], along_y(yd))
    m = ROWS // 2
    top, bottom = pl.ds(0, m), pl.ds(m, m)
    came(4, a1f.at[0])
    came(5, a1f.at[1])
    a2[...] = found[:, x, :, :h] + a1f[0] + a1f[1]
    go(8, a2.at[yf, top], a2h.at[0], along_y(yu))
    go(9, a2.at[yf, bottom], a2h.at[1], along_y(yd))
    came(6, b1f.at[0])
    came(7, b1f.at[1])
    b2[...] = found[y, :, :, h:] + b1f[0] + b1f[1]
    go(10, b2.at[xf, top], b2h.at[0], along_x(xu))
    go(11, b2.at[xf, bottom], b2h.at[1], along_x(xd))
    came(8, a2h.at[0])
    a2s[0, :m] = a2[yu, :m] + a2h[0]
    a2s[0, m:] = a2[yu, m:]
    go(12, a2s.at[0], a2f.at[0], along_y(yu))
    came(9, a2h.at[1])
    a2s[1, :m] = a2[yd, :m]
    a2s[1, m:] = a2[yd, m:] + a2h[1]
    go(13, a2s.at[1], a2f.at[1], along_y(yd))
    came(10, b2h.at[0])
    b2s[0, :m] = b2[xu, :m] + b2h[0]
    b2s[0, m:] = b2[xu, m:]
    go(14, b2s.at[0], b2f.at[0], along_x(xu))
    came(11, b2h.at[1])
    b2s[1, :m] = b2[xd, :m]
    b2s[1, m:] = b2[xd, m:] + b2h[1]
    go(15, b2s.at[1], b2f.at[1], along_x(xd))
    came(12, a2f.at[0])
    came(13, a2f.at[1])
    own[:ROWS, :h] = a2[y] + a2f[0] + a2f[1]
    came(14, b2f.at[0])
    came(15, b2f.at[1])
    own[:ROWS, h:] = b2[x] + b2f[0] + b2f[1]
    for copy in started:
        copy.wait_send()


def dense_kernel(found, own, *rest):
    greet(tok_peers())
    dense_rows(found, own, lambda: None, *rest)


def dense_exchange(found):
    h, m = WIDTH // 2, ROWS // 2
    return pl.pallas_call(
        dense_kernel,
        out_shape=jax.ShapeDtypeStruct((ROWS, WIDTH), BF16),
        in_specs=[VMEM],
        out_specs=VMEM,
        scratch_shapes=[
            pltpu.VMEM((2, 2, ROWS, h), BF16),
            pltpu.VMEM((2, 4, ROWS, h), BF16),
            pltpu.VMEM((2, 4, ROWS, h), BF16),
            pltpu.VMEM((2, 2, ROWS, h), BF16),
            pltpu.VMEM((2, 4, ROWS, h), BF16),
            pltpu.VMEM((2, 4, ROWS, h), BF16),
            pltpu.VMEM((4, ROWS, h), BF16),
            pltpu.VMEM((2, m, h), BF16),
            pltpu.VMEM((2, ROWS, h), BF16),
            pltpu.VMEM((2, ROWS, h), BF16),
            pltpu.VMEM((4, ROWS, h), BF16),
            pltpu.VMEM((2, m, h), BF16),
            pltpu.VMEM((2, ROWS, h), BF16),
            pltpu.VMEM((2, ROWS, h), BF16),
            pltpu.SemaphoreType.DMA((16,)),
            pltpu.SemaphoreType.DMA((16,)),
        ],
        compiler_params=pltpu.CompilerParams(
            collective_id=1, has_side_effects=True, vmem_limit_bytes=40 << 20
        ),
        name="dense_exchange",
    )(found)


def pack_kernel(place, ids, table, packed, spot, most, slot_s):
    t_at = place[0]
    shape = (ROWS, ROWS)
    sub = lax.broadcasted_iota(jnp.int32, shape, 0)
    lane = lax.broadcasted_iota(jnp.int32, shape, 1)
    vocab_rows = table.shape[0]
    base = t_at * vocab_rows

    def column(row):
        return jnp.sum(jnp.where(sub == lane, jnp.broadcast_to(row, shape), 0), axis=1, keepdims=True)

    def ranks(row):
        col = column(row)
        same = col == row
        first_col = 1 - jnp.max(jnp.where(same & (lane < sub), 1, 0), axis=1, keepdims=True)
        first_row = 1 - jnp.max(jnp.where(same & (sub < lane), 1, 0), axis=0, keepdims=True)
        start = row - lax.rem(row, vocab_rows)
        ahead = (col < row) & (col >= start)
        rank = jnp.sum(jnp.where(ahead, first_col, 0), axis=0, keepdims=True)
        return first_row, start, rank

    def one(t, top):
        row = ids[pl.ds(t, 1), :]
        first_row, start, rank = ranks(row)
        mine = (first_row > 0) & (start == base)
        slot = lax.broadcasted_iota(jnp.int32, (SPACE, ROWS), 0)
        hit = (slot == rank) & mine
        slot_s[pl.ds(pl.multiple_of(t * SPACE, SPACE), SPACE)] = (
            jnp.sum(jnp.where(hit, row - base + 1, 0), axis=1, keepdims=True) - 1
        )

        @pl.when(t == t_at)
        def _():
            owner = start // vocab_rows
            spot[...] = column(owner * SPACE + rank)

        return jnp.maximum(top, rank)

    top = lax.fori_loop(0, TOK, one, jnp.zeros((1, ROWS), jnp.int32))
    most[...] = jnp.broadcast_to(jnp.max(top, axis=1, keepdims=True) + 1, (8, 128))
    step = 256
    for k in range(TOK * SPACE // step):
        rows = pl.ds(k * step, step)
        pick = (
            lax.broadcasted_iota(jnp.int32, (step, vocab_rows), 1) == slot_s[rows]
        ).astype(BF16)
        packed[rows] = dot(pick, table[...]).astype(BF16)


def pack(place, ids, table):
    return pl.pallas_call(
        pack_kernel,
        out_shape=(
            jax.ShapeDtypeStruct((TOK * SPACE, WIDTH), BF16),
            jax.ShapeDtypeStruct((ROWS, 1), jnp.int32),
            jax.ShapeDtypeStruct((8, 128), jnp.int32),
        ),
        in_specs=[pl.BlockSpec(memory_space=pltpu.SMEM), VMEM, VMEM],
        out_specs=(VMEM, VMEM, VMEM),
        scratch_shapes=[pltpu.VMEM((TOK * SPACE, 1), jnp.int32)],
        compiler_params=pltpu.CompilerParams(vmem_limit_bytes=32 << 20),
        cost_estimate=pl.CostEstimate(flops=2 << 30, transcendentals=0, bytes_accessed=4 << 20),
        name="pack",
    )(place, ids, table)


def dot(a, b):
    return jnp.dot(a, b, preferred_element_type=F32)


def normed_and_step(block, prior, mean, scale, gain):
    normed = (block.astype(F32) - mean) * scale * gain
    row = lax.broadcasted_iota(jnp.int32, (ROWS, WIDTH), 0)
    spread = (
        lax.broadcasted_iota(jnp.int32, (ROWS, BRANCH), 0) // DRAFT
        == lax.broadcasted_iota(jnp.int32, (ROWS, BRANCH), 1)
    )
    carried = dot(spread.astype(BF16), prior)
    before = jnp.where(lax.rem(row, DRAFT) == 0, carried, pltpu.roll(normed, 1, axis=0))
    return normed, before - normed


def kept_row(normed, prior, kept_column):
    column = lax.broadcasted_iota(jnp.int32, (BRANCH, ROWS), 1)
    branch = lax.broadcasted_iota(jnp.int32, (BRANCH, ROWS), 0)
    pick = (column == branch * DRAFT + kept_column - 1) & (kept_column > 0)
    picked = dot(pick.astype(BF16), normed.astype(BF16))
    return jnp.where(kept_column > 0, picked, prior.astype(F32)).astype(BF16)


def head_ones(size):
    return (
        lax.broadcasted_iota(jnp.int32, (size, size), 0) // HEAD
        == lax.broadcasted_iota(jnp.int32, (size, size), 1) // HEAD
    ).astype(BF16)


def per_head(value):
    ones = head_ones(256)
    return jnp.concatenate([dot(value[:, :256], ones), dot(value[:, 256:], ones)], axis=1)


def per_head_fine(value):
    top = value.astype(BF16)
    rest = (value - top.astype(F32)).astype(BF16)
    return per_head(top) + per_head(rest)


def two_heads(page):
    side = lax.broadcasted_iota(jnp.int32, (HEAD, 128), 1) < HEAD
    none = jnp.zeros_like(page)
    return jnp.concatenate([jnp.where(side, page, none), jnp.where(side, none, page)], axis=0)


META = ("slots", TOK), ("owner_of", REQ), ("page_of", BRANCH), ("winner", REQ), ("kept", REQ), ("pick", TOK), ("source", TOK), ("hit", TOK), ("dense", 1)


def starts():
    at, result = 0, {}
    for name, count in META:
        result[name] = at
        at += count
    return result


def row_stats(value_ref, mean, scale):
    step = 64

    @pl.loop(0, ROWS // step)
    def _(k):
        rows = pl.ds(pl.multiple_of(k * step, step), step)
        value = value_ref[rows].astype(F32)
        middle = jnp.mean(value, axis=-1, keepdims=True)
        centered = value - middle
        spread = jnp.mean(centered * centered, axis=-1, keepdims=True)
        mean[rows] = middle
        scale[rows] = lax.rsqrt(spread + EPSILON)


def layer_kernel(
    meta, store, packed, spot, dense_own, priors, scales, blends, narrow, widen, baseline, boost, kept_column,
    attention_w, result_w, lookup_w, gating_w, content_w,
    out, shift_att, shift_ffn, store_out,
    whole, residuals, results, lookups, gatings, contents, wbuf, part,
    mated, sums, halves, full, rsend, rrecv,
    own, residual, parcels, psend, precv, plocal, gsend, grecv, glocal,
    out_pages, in_pages, tsend, trecv, tlocal, made, returned, bsend, brecv, blocal,
    acc, low, w_s, y_s, p_s, ffn, mean, scale, wsend, wrecv, wlocal, wsem,
):
    base = starts()
    word = lambda name, index: meta[base[name] + index]
    t, g = lax.axis_index("tok"), lax.axis_index("grp")
    mine = block_of(g)
    greet(tok_peers() + grp_peers())

    def load(k):
        rows = pl.ds(pl.multiple_of(k * WIDTH, WIDTH), WIDTH)
        slot = lax.rem(k, 2)
        return pltpu.make_async_copy(attention_w.at[:, rows], wbuf.at[slot], wsem.at[slot])

    keep = pltpu.make_async_copy(packed.at[t], parcels.at[t], plocal)
    keep.start()
    copies = []
    for k in range(1, TOK):
        peer = lax.rem(t + k, TOK)
        copy = remote(packed.at[peer], parcels.at[t], psend.at[k - 1], precv.at[k - 1], {"tok": peer})
        copy.start()
        copies.append(copy)
    load(0).start()
    load(1).start()
    res, look, gat, con = [
        gather_tok(w, views(all_of), wsend.at[k], wrecv.at[k], wlocal.at[k])
        for k, (w, views, all_of) in enumerate(
            (
                (result_w, result_views, results),
                (lookup_w, stack_views, lookups),
                (gating_w, stack_views, gatings),
                (content_w, result_views, contents),
            )
        )
    ]
    res[0]()

    @pl.loop(0, TOK)
    def _(peer):
        page = store[word("slots", peer)]

        def put(pair, row, value):
            out_pages[peer, pair, pl.ds(row, 16)] = value.astype(BF16)

        pair_page(page, put)

    trade = trade_start(out_pages, in_pages, tsend, trecv, tlocal)
    look[0]()
    own[ROWS:] = priors[...]
    slots = lax.broadcasted_iota(jnp.int32, (ROWS, TOK * SPACE), 1)
    choice = (slots == spot[...]).astype(BF16)
    keep.wait()
    for k in range(1, TOK):
        origin = lax.rem(t + TOK - k, TOK)
        remote(packed.at[t], parcels.at[origin], psend.at[k - 1], precv.at[k - 1], {"tok": origin}).wait_recv()
    picked = dot(choice, parcels[...].reshape(TOK * SPACE, WIDTH)).astype(BF16)
    own[:ROWS] = jnp.where(word("dense", 0) > 0, dense_own[...], picked)
    gather_grp(own, whole, gsend, grecv, glocal, [res[1], look[1]])
    for copy in copies:
        copy.wait_send()

    row_stats(whole, mean, scale)
    acc[...] = jnp.zeros_like(acc)
    low[...] = jnp.zeros_like(low)
    res[2]()
    gat[0]()

    shape3 = (BRANCH, DRAFT, WIDTH)
    flat = lambda value: value.reshape(ROWS, WIDTH)

    def mix(k):
        load(k).wait()
        columns = block_of(k)
        weights = wbuf.at[lax.rem(k, 2)]
        prior = whole[ROWS : ROWS + BRANCH, columns]
        normed, delta = normed_and_step(whole[:ROWS, columns], prior, mean[...], scale[...], scales[0:1, columns])

        @pl.when(k == g)
        def _():
            shift_att[...] = kept_row(normed, prior, kept_column[...])

        blend = blends[:, columns]
        for c in range(4):
            acc[c] += dot((normed + delta * blend[c : c + 1]).astype(BF16), weights[c]).reshape(shape3)
        low[...] += dot((normed + delta * blend[4:5]).astype(BF16), narrow[columns])

        @pl.when(k < GRP - 2)
        def _():
            load(k + 2).start()

    pl.loop(0, 4)(mix)
    look[2]()
    res[3]()
    pl.loop(4, 8)(mix)
    gat[1]()
    trade_end(out_pages, in_pages, tsend, trecv, trade)

    lowrank = jnp.tanh(low[...]).astype(BF16)
    w_s[...] = jnp.exp(-jnp.exp(baseline[:, mine] + dot(lowrank, widen[...]))).reshape(shape3)
    position = lax.broadcasted_iota(jnp.int32, shape3, 1)
    r3, k3, v3, w3 = acc[0], acc[1], acc[2], w_s[...]
    y_s[...] = per_head_fine(flat(r3) * boost[:, mine] * flat(k3)) * flat(v3)
    p_s[...] = jnp.ones_like(p_s)
    for s in range(DRAFT - 2, -1, -1):
        decay = jnp.where(position > s + 1, p_s[...].reshape(shape3) * w3[:, s + 1 : s + 2], 1.0)
        p_s[...] = decay.reshape(ROWS, WIDTH)
        term = jnp.where(position > s, r3 * decay * k3[:, s : s + 1], 0.0)
        score = per_head(term.reshape(ROWS, WIDTH).astype(BF16)).reshape(shape3)
        y_s[...] += (score * v3[:, s : s + 1]).reshape(ROWS, WIDTH)
    decay = jnp.where(position > 0, p_s[...].reshape(shape3) * w3[:, 0:1], 1.0)
    p_s[...] = flat(r3 * decay)

    @pl.loop(0, BRANCH)
    def _(b):
        rows = pl.ds(pl.multiple_of(b * DRAFT, DRAFT), DRAFT)
        page = in_pages[word("page_of", b)]
        for pair in range(PAIRS):
            lanes = pl.ds(pair * 128, 128)
            y_s[rows, lanes] += dot(p_s[rows, lanes].astype(BF16), two_heads(page[pair]))

    con[0]()
    value = y_s[...]
    centered = value - per_head_fine(value) * (1.0 / HEAD)
    spread = per_head_fine(centered * centered) * (1.0 / HEAD)
    gate = flat(acc[3])
    gate = gate * jax.nn.sigmoid(gate)
    attended = (centered * lax.rsqrt(spread + HEAD_EPSILON) * scales[2:3, mine] * gate).astype(BF16)
    res[4]()
    for y_of in range(4):
        part[:, y_of * 1024 : y_of * 1024 + 1024] = dot(attended, results[y_of]).astype(BF16)

    def states():
        eye = (
            lax.broadcasted_iota(jnp.int32, (128, 128), 0)
            == lax.broadcasted_iota(jnp.int32, (128, 128), 1)
        )
        spot16 = lax.broadcasted_iota(jnp.int32, (DRAFT, WIDTH), 0)
        side = lax.broadcasted_iota(jnp.int32, (HEAD, 128), 1) < HEAD

        @pl.loop(0, REQ)
        def _(q):
            b = word("winner", q)
            count = word("kept", q)
            live = spot16 < count
            tail = jnp.where(live, w_s[b], 1.0)
            for hop in (1, 2, 4, 8):
                later = pltpu.roll(tail, DRAFT - hop, axis=0)
                tail = tail * jnp.where(spot16 < DRAFT - hop, later, 1.0)
            after = jnp.where(spot16 < DRAFT - 1, pltpu.roll(tail, DRAFT - 1, axis=0), 1.0)
            keys = jnp.where(live, acc[1, b], 0.0) * after
            values = acc[2, b].astype(BF16)
            page = in_pages[word("owner_of", q)]
            for pair in range(PAIRS):
                lanes = slice(pair * 128, pair * 128 + 128)
                fade = jnp.where(eye, tail[0:1, lanes], 0.0)
                left = jnp.concatenate([keys[:, lanes], fade], axis=0).astype(BF16)
                right = jnp.concatenate([values[:, lanes], two_heads(page[pair])], axis=0)
                both = lax.dot_general(left, right, (((0,), (0,)), ((), ())), preferred_element_type=F32)
                made[q, pair] = jnp.where(side, both[:HEAD], both[HEAD:]).astype(BF16)

        @pl.loop(0, TOK)
        def _(peer):
            out_pages[peer] = made[word("pick", peer)]

        trades.append(trade_start(out_pages, returned, bsend, brecv, blocal))

    trades = []
    total = reduce_grp(part, mated, sums, halves, full, rsend, rrecv, states)
    residual[...] = (own[:ROWS].astype(F32) + total).astype(BF16)
    gather_grp(residual, residuals, gsend, grecv, glocal, [look[3], gat[2]])
    row_stats(residuals, mean, scale)
    con[1]()
    gat[3]()

    ffn[...] = jnp.zeros_like(ffn)
    look[4]()
    con[2]()
    gat[4]()

    @pl.loop(0, GRP)
    def _(k):
        columns = block_of(k)
        prior = whole[ROWS + BRANCH :, columns]
        normed, delta = normed_and_step(residuals[:, columns], prior, mean[...], scale[...], scales[1:2, columns])

        @pl.when(k == g)
        def _():
            shift_ffn[...] = kept_row(normed, prior, kept_column[...])

        blend = blends[:, columns]
        y_of, x_of = k // 2, pl.ds(lax.rem(k, 2) * 2, 2)
        ffn[:, :KEYS] += dot(
            (normed + delta * blend[5:6]).astype(BF16), lookups[y_of, x_of].reshape(WIDTH, KEYS)
        )
        ffn[:, KEYS:] += dot(
            (normed + delta * blend[6:7]).astype(BF16), gatings[y_of, x_of].reshape(WIDTH, WIDTH)
        )

    trade_end(out_pages, returned, bsend, brecv, trades[0])
    hidden = jnp.square(jnp.maximum(ffn[:, :KEYS], 0.0)).astype(BF16)
    con[3]()
    con[4]()
    for y_of in range(4):
        part[:, y_of * 1024 : y_of * 1024 + 1024] = dot(hidden, contents[y_of]).astype(BF16)

    def pages():
        @pl.loop(0, TOK)
        def _(slot):
            page = returned[word("source", slot)].astype(F32)
            taken = word("hit", slot) > 0

            def put(column, value):
                columns = pl.ds(column, 128)
                store_out[slot, :, columns] = jnp.where(taken, value, store[slot, :, columns])

            flat_page(page, put)

    total = reduce_grp(part, mated, sums, halves, full, rsend, rrecv, pages)
    out[...] = (residual[...].astype(F32) + jax.nn.sigmoid(ffn[:, KEYS:]) * total).astype(BF16)


def layer(meta, store, packed, spot, dense_own, priors, scales, blends, narrow, widen, baseline, boost, kept_column, *weights):
    rows = ROWS + 2 * BRANCH
    wide = lambda *shape: pltpu.VMEM(shape, BF16)
    fine = lambda *shape: pltpu.VMEM(shape, F32)
    dma = lambda *shape: pltpu.SemaphoreType.DMA(shape)
    return pl.pallas_call(
        layer_kernel,
        out_shape=(
            jax.ShapeDtypeStruct((ROWS, WIDTH), BF16),
            jax.ShapeDtypeStruct((BRANCH, WIDTH), BF16),
            jax.ShapeDtypeStruct((BRANCH, WIDTH), BF16),
            jax.ShapeDtypeStruct(store.shape, F32),
        ),
        in_specs=[pl.BlockSpec(memory_space=pltpu.SMEM)] + [VMEM] * 12 + [ANY] * 5,
        out_specs=(VMEM, VMEM, VMEM, VMEM),
        scratch_shapes=[
            wide(rows, HIDDEN),
            wide(ROWS, HIDDEN),
            wide(4, WIDTH, 1024),
            wide(4, 4, 256, KEYS),
            wide(4, 4, 256, WIDTH),
            wide(4, KEYS, 1024),
            wide(2, 4, WIDTH, WIDTH),
            wide(ROWS, HIDDEN),
            *REDUCE_SCRATCH,
            wide(rows, WIDTH),
            wide(ROWS, WIDTH),
            wide(TOK, SPACE, WIDTH),
            dma(TOK - 1),
            dma(TOK - 1),
            pltpu.SemaphoreType.DMA,
            dma(9),
            dma(9),
            pltpu.SemaphoreType.DMA,
            wide(TOK, PAIRS, HEAD, 128),
            wide(TOK, PAIRS, HEAD, 128),
            *TRADE_SEMAPHORES,
            wide(REQ, PAIRS, HEAD, 128),
            wide(TOK, PAIRS, HEAD, 128),
            *TRADE_SEMAPHORES,
            fine(4, BRANCH, DRAFT, WIDTH),
            fine(ROWS, 128),
            fine(BRANCH, DRAFT, WIDTH),
            fine(ROWS, WIDTH),
            fine(ROWS, WIDTH),
            fine(ROWS, KEYS + WIDTH),
            fine(ROWS, 1),
            fine(ROWS, 1),
            dma(4, 16),
            dma(4, 16),
            dma(4),
            dma(2),
        ],
        compiler_params=pltpu.CompilerParams(
            collective_id=2, has_side_effects=True, vmem_limit_bytes=60 << 20
        ),
        cost_estimate=pl.CostEstimate(flops=12 << 30, transcendentals=1 << 20, bytes_accessed=60 << 20),
        name="layer",
    )(meta, store, packed, spot, dense_own, priors, scales, blends, narrow, widen, baseline, boost, kept_column, *weights)


def body(
    guess_symbol_ids,
    symbol_vector_lookup,
    prior_attention_normed,
    prior_feedforward_normed,
    layernorm_scales,
    lagged_blend_ratios,
    attention_matrices,
    forgetting_baseline_vector,
    forgetting_narrow_matrix,
    forgetting_widen_matrix,
    diagonal_boost,
    attention_result_matrix,
    feedforward_lookup_matrix,
    feedforward_content_matrix,
    feedforward_gating_matrix,
    memory_matrix_store,
    query_memory_slot,
    candidate_tally_each_query,
    kept_guess_tally,
):
    tok_at = lax.axis_index("tok")
    vocab_rows = symbol_vector_lookup.shape[0]
    slot_count = memory_matrix_store.shape[0]

    priors = jnp.concatenate([prior_attention_normed, prior_feedforward_normed], axis=0)

    owners = (query_memory_slot // slot_count).reshape(TOK, REQ)
    places = (query_memory_slot % slot_count).reshape(TOK, REQ)
    owned_here = owners == tok_at
    send_slot = jnp.sum(jnp.where(owned_here, places, 0), axis=1)
    sending = jnp.any(owned_here, axis=1)
    packed, spot, most = pack(
        tok_at.reshape(1), guess_symbol_ids.reshape(TOK, ROWS), symbol_vector_lookup
    )

    crowded = most[0, 0] > SPACE

    def dense(_):
        wanted = guess_symbol_ids - tok_at * vocab_rows
        inside = (wanted >= 0) & (wanted < vocab_rows)
        found = jnp.take(symbol_vector_lookup, jnp.clip(wanted, 0, vocab_rows - 1), axis=0)
        found = jnp.where(inside[:, None], found, jnp.zeros((), BF16)).reshape(4, 4, ROWS, WIDTH)
        return dense_exchange(found)

    dense_own = lax.cond(crowded, dense, lambda _: jnp.zeros((ROWS, WIDTH), BF16), 0)

    my_owners = lax.dynamic_index_in_dim(owners, tok_at, 0, keepdims=False)
    my_counts = lax.dynamic_index_in_dim(candidate_tally_each_query, tok_at, 0, keepdims=False)
    local_ids = jnp.arange(BRANCH, dtype=jnp.int32)
    request_ends = jnp.cumsum(my_counts)
    request_of = jnp.sum((request_ends[None, :] <= local_ids[:, None]).astype(jnp.int32), axis=1)
    branch_score = kept_guess_tally * BRANCH + (BRANCH - 1 - local_ids)
    member = request_of[None, :] == jnp.arange(REQ, dtype=jnp.int32)[:, None]
    best_score = jnp.max(jnp.where(member, branch_score[None, :], -1), axis=1)
    winner = BRANCH - 1 - best_score % BRANCH

    targets = my_owners[None, :] == jnp.arange(TOK, dtype=jnp.int32)[:, None]
    pick_index = jnp.sum(
        jnp.where(targets, jnp.arange(REQ, dtype=jnp.int32)[None, :], 0), axis=1
    )
    hit = (send_slot[None, :] == jnp.arange(slot_count, dtype=jnp.int32)[:, None]) & sending[None, :]
    source = jnp.sum(jnp.where(hit, jnp.arange(TOK, dtype=jnp.int32)[None, :], 0), axis=1)
    meta = jnp.concatenate(
        [
            send_slot, my_owners, my_owners[request_of], winner, kept_guess_tally[winner], pick_index, source,
            jnp.any(hit, axis=1).astype(jnp.int32), crowded.astype(jnp.int32).reshape(1),
        ]
    )
    layer_out, shift_att_out, shift_ffn_out, store_out = layer(
        meta, memory_matrix_store, packed.reshape(TOK, SPACE, WIDTH), spot, dense_own, priors,
        layernorm_scales, lagged_blend_ratios, forgetting_narrow_matrix, forgetting_widen_matrix,
        forgetting_baseline_vector.reshape(1, HIDDEN), diagonal_boost.reshape(1, HIDDEN),
        kept_guess_tally.reshape(BRANCH, 1), attention_matrices, attention_result_matrix,
        feedforward_lookup_matrix, feedforward_gating_matrix, feedforward_content_matrix,
    )
    return (layer_out, shift_att_out, shift_ffn_out, store_out)


def solution(mesh):
    in_specs = (
        P(),
        P("tok", "grp"),
        P("tok", "grp"),
        P("tok", "grp"),
        P(),
        P(),
        P(None, None, "grp"),
        P(),
        P(),
        P(None, "grp"),
        P(),
        P("grp", "tok"),
        P("tok", "grp"),
        P("grp", "tok"),
        P("tok", "grp"),
        P("tok", "grp", None),
        P(),
        P(),
        P("tok"),
    )
    out_specs = (P("tok", "grp"), P("tok", "grp"), P("tok", "grp"), P("tok", "grp", None))
    return jax.shard_map(body, mesh=mesh, in_specs=in_specs, out_specs=out_specs, check_vma=False)
```

```python
import functools

import jax
import jax.numpy as jnp
from jax import lax
from jax.experimental import pallas as pl
from jax.experimental.pallas import tpu as pltpu
from jax.sharding import PartitionSpec as P

HIDDEN = 4096
HEAD = 64
DRAFT = 16
BRANCH = 16
ROWS = BRANCH * DRAFT
WIDTH = 512
TOK = 16
GRP = 8
REQ = 8
PAIRS = 4
KEYS = 896
SPACE = 32
EPSILON = 1e-05
HEAD_EPSILON = 0.00064
F32 = jnp.float32
BF16 = jnp.bfloat16
MESH = pl.DeviceIdType.MESH
ANY = pl.BlockSpec(memory_space=pl.ANY)
VMEM = pl.BlockSpec(memory_space=pltpu.VMEM)


def remote(src, dst, send, recv, device):
    return pltpu.make_async_remote_copy(
        src_ref=src, dst_ref=dst, send_sem=send, recv_sem=recv, device_id=device, device_id_type=MESH
    )


def greet(devices):
    barrier = pltpu.get_barrier_semaphore()
    for device in devices:
        pl.semaphore_signal(barrier, inc=1, device_id=device, device_id_type=MESH)
    pl.semaphore_wait(barrier, len(devices))


def grp_places():
    g = lax.axis_index("grp")
    z, core = g // 2, g % 2
    up = lax.rem(z + 1, 4) * 2 + core
    down = lax.rem(z + 3, 4) * 2 + core
    far = lax.rem(z + 2, 4) * 2 + core
    mate = z * 2 + 1 - core
    return g, up, down, far, mate


def block_of(g):
    return pl.ds(pl.multiple_of(g * WIDTH, WIDTH), WIDTH)


def flip(g):
    return g + 1 - 2 * lax.rem(g, 2)


def gather_grp(own, out, send, recv, local, between=()):
    between = list(between)

    def aside():
        if between:
            between.pop(0)()

    rows = out.shape[0]
    half = rows // 2
    g, up, down, far, mate = grp_places()
    first, last, whole = pl.ds(0, half), pl.ds(half, rows - half), pl.ds(0, rows)
    at = lambda part, g_of: out.at[part, block_of(g_of)]
    keep = pltpu.make_async_copy(own, at(whole, g), local)
    keep.start()
    started = []

    def go(index, src, part, g_of, target):
        copy = remote(src, at(part, g_of), send.at[index], recv.at[index], {"grp": target})
        copy.start()
        started.append(copy)

    def came(index, part, g_of):
        remote(at(part, g_of), at(part, g_of), send.at[index], recv.at[index], {"grp": mate}).wait_recv()

    go(0, own, whole, g, up)
    go(1, own, whole, g, down)
    go(2, own, whole, g, mate)
    aside()
    came(0, whole, down)
    go(3, at(first, down), first, down, up)
    go(5, at(whole, down), whole, down, mate)
    came(1, whole, up)
    go(4, at(last, up), last, up, down)
    go(6, at(whole, up), whole, up, mate)
    aside()
    came(3, first, far)
    go(7, at(first, far), first, far, mate)
    came(4, last, far)
    go(8, at(last, far), last, far, mate)
    came(2, whole, mate)
    came(5, whole, flip(down))
    came(6, whole, flip(up))
    came(7, first, flip(far))
    came(8, last, flip(far))
    while between:
        aside()
    keep.wait()
    for copy in started:
        copy.wait_send()


def reduce_grp(part, mated, sums, halves, full, send, recv, meanwhile=lambda: None):
    g, up, down, far, mate = grp_places()
    half = ROWS // 2
    started = []

    def go(index, src, dst, target):
        copy = remote(src, dst, send.at[index], recv.at[index], {"grp": target})
        copy.start()
        started.append(copy)

    def came(index, dst):
        remote(dst, dst, send.at[index], recv.at[index], {"grp": mate}).wait_recv()

    order = (far, up, down, g)
    for k in range(4):
        go(k, part.at[:, block_of(flip(order[k]))], mated.at[k], mate)

    def own(k):
        return part[:, block_of(order[k])].astype(F32) + mated[k].astype(F32)

    came(0, mated.at[0])
    sums[0] = own(0).astype(BF16)
    go(4, sums.at[0, pl.ds(0, half)], halves.at[0], up)
    go(5, sums.at[0, pl.ds(half, half)], halves.at[1], down)
    came(1, mated.at[1])
    came(4, halves.at[0])
    sums[1, :half] = (own(1)[:half] + halves[0].astype(F32)).astype(BF16)
    sums[1, half:] = own(1)[half:].astype(BF16)
    go(6, sums.at[1], full.at[0], up)
    came(2, mated.at[2])
    came(5, halves.at[1])
    sums[2, :half] = own(2)[:half].astype(BF16)
    sums[2, half:] = (own(2)[half:] + halves[1].astype(F32)).astype(BF16)
    go(7, sums.at[2], full.at[1], down)
    meanwhile()
    came(3, mated.at[3])
    came(6, full.at[0])
    came(7, full.at[1])
    total = own(3) + full[0].astype(F32) + full[1].astype(F32)
    for copy in started:
        copy.wait_send()
    return total


REDUCE_SCRATCH = [
    pltpu.VMEM((4, ROWS, WIDTH), BF16),
    pltpu.VMEM((3, ROWS, WIDTH), BF16),
    pltpu.VMEM((2, ROWS // 2, WIDTH), BF16),
    pltpu.VMEM((2, ROWS, WIDTH), BF16),
    pltpu.SemaphoreType.DMA((8,)),
    pltpu.SemaphoreType.DMA((8,)),
]


def result_views(out):
    cols = lambda x_of: pl.ds(pl.multiple_of(x_of * 256, 256), 256)
    return (
        lambda rows, y_of, x_of: out.at[y_of, rows, cols(x_of)],
        lambda rows, y_of: out.at[y_of, rows],
        lambda rows, x_of: out.at[:, rows, cols(x_of)],
    )


def stack_views(out):
    return (
        lambda rows, y_of, x_of: out.at[y_of, x_of, rows],
        lambda rows, y_of: out.at[y_of, :, rows],
        lambda rows, x_of: out.at[:, x_of, rows],
    )


def gather_tok(own, views, send, recv, local):
    t = lax.axis_index("tok")
    y, x = t // 4, lax.rem(t, 4)
    xu, xd, xf = [lax.rem(x + k, 4) for k in (1, 3, 2)]
    yu, yd, yf = [lax.rem(y + k, 4) for k in (1, 3, 2)]
    along_x = lambda x_of: {"tok": y * 4 + x_of}
    along_y = lambda y_of: {"tok": y_of * 4 + x}
    one, wide, tall = views
    count = own.shape[0]
    f0, f1 = pl.ds(0, count // 2), pl.ds(count // 2, count // 2)
    fa, fb = [pl.ds(f0.start + k * (f0.size // 2), f0.size // 2) for k in (0, 1)]
    la, lb = [pl.ds(f1.start + k * (f1.size // 2), f1.size // 2) for k in (0, 1)]
    started = []

    def go(index, src, dst, target):
        copy = remote(src, dst, send.at[index], recv.at[index], target)
        copy.start()
        started.append(copy)

    def came(index, dst):
        remote(dst, dst, send.at[index], recv.at[index], along_x(xu)).wait_recv()

    keep = pltpu.make_async_copy(own, one(pl.ds(0, count), y, x), local)

    def begin():
        keep.start()
        go(0, own.at[f0], one(f0, y, x), along_x(xu))
        go(1, own.at[f0], one(f0, y, x), along_x(xd))
        go(2, own.at[f1], one(f1, y, x), along_y(yu))
        go(3, own.at[f1], one(f1, y, x), along_y(yd))

    def relay():
        came(0, one(f0, y, xd))
        go(4, one(fa, y, xd), one(fa, y, xd), along_x(xu))
        came(2, one(f1, yd, x))
        go(6, one(la, yd, x), one(la, yd, x), along_y(yu))
        came(1, one(f0, y, xu))
        go(5, one(fb, y, xu), one(fb, y, xu), along_x(xd))
        came(3, one(f1, yu, x))
        go(7, one(lb, yu, x), one(lb, yu, x), along_y(yd))

    def turn():
        keep.wait()
        came(4, one(fa, y, xf))
        came(5, one(fb, y, xf))
        go(8, wide(f0, y), wide(f0, y), along_y(yu))
        go(9, wide(f0, y), wide(f0, y), along_y(yd))
        came(6, one(la, yf, x))
        came(7, one(lb, yf, x))
        go(10, tall(f1, x), tall(f1, x), along_x(xu))
        go(11, tall(f1, x), tall(f1, x), along_x(xd))

    def last():
        came(8, wide(f0, yd))
        go(12, wide(fa, yd), wide(fa, yd), along_y(yu))
        came(10, tall(f1, xd))
        go(14, tall(la, xd), tall(la, xd), along_x(xu))
        came(9, wide(f0, yu))
        go(13, wide(fb, yu), wide(fb, yu), along_y(yd))
        came(11, tall(f1, xu))
        go(15, tall(lb, xu), tall(lb, xu), along_x(xd))

    def end():
        came(12, wide(fa, yf))
        came(13, wide(fb, yf))
        came(14, tall(la, xf))
        came(15, tall(lb, xf))
        for copy in started:
            copy.wait_send()

    return begin, relay, turn, last, end


def grp_peers():
    _, up, down, _, mate = grp_places()
    return [{"grp": up}, {"grp": down}, {"grp": mate}]


def tok_peers():
    t = lax.axis_index("tok")
    return [{"tok": lax.rem(t + k, TOK)} for k in range(1, TOK)]


def page_masks():
    even = lax.rem(lax.broadcasted_iota(jnp.int32, (8, 128), 0), 2) == 0
    left = lax.broadcasted_iota(jnp.int32, (8, 128), 1) < HEAD
    return even, left


def pair_page(page, put):
    even, left = page_masks()
    for block in range(4):
        rows = [[] for _ in range(PAIRS)]
        for group in (2 * block, 2 * block + 1):
            pieces = []
            for m in range(4 * group, 4 * group + 4):
                here = page[:, m * 128 : m * 128 + 128]
                swapped = pltpu.roll(here, HEAD, axis=1)
                pieces += [jnp.where(even, here, swapped), jnp.where(even, swapped, here)]
            turned = jnp.swapaxes(jnp.stack(pieces), 0, 1)
            for pair in range(PAIRS):
                rows[pair].append(jnp.where(left, turned[2 * pair], turned[2 * pair + 1]))
        for pair in range(PAIRS):
            put(pair, 16 * block, jnp.concatenate(rows[pair], axis=0))


def flat_page(page, put):
    even, left = page_masks()
    for group in range(8):
        rows = [page[pair, 8 * group : 8 * group + 8] for pair in range(PAIRS)]
        turned = jnp.swapaxes(jnp.stack([rows[h // 2] for h in range(8)]), 0, 1)
        for m in range(4):
            first, second = turned[2 * m], turned[2 * m + 1]
            swapped_first = pltpu.roll(first, HEAD, axis=1)
            swapped_second = pltpu.roll(second, HEAD, axis=1)
            put(
                (4 * group + m) * 128,
                jnp.where(
                    left,
                    jnp.where(even, first, swapped_first),
                    jnp.where(even, swapped_second, second),
                ),
            )


def trade_start(out_pages, in_pages, send, recv, local):
    t = lax.axis_index("tok")
    keep = pltpu.make_async_copy(out_pages.at[t], in_pages.at[t], local)
    keep.start()
    for k in range(1, TOK):
        peer = lax.rem(t + k, TOK)
        remote(out_pages.at[peer], in_pages.at[t], send.at[k - 1], recv.at[k - 1], {"tok": peer}).start()
    return keep


def trade_end(out_pages, in_pages, send, recv, keep):
    t = lax.axis_index("tok")
    keep.wait()
    for k in range(1, TOK):
        peer = lax.rem(t + k, TOK)
        origin = lax.rem(t + TOK - k, TOK)
        copy = remote(out_pages.at[peer], in_pages.at[origin], send.at[k - 1], recv.at[k - 1], {"tok": peer})
        copy.wait_recv()
        copy.wait_send()


TRADE_SEMAPHORES = [
    pltpu.SemaphoreType.DMA((TOK - 1,)),
    pltpu.SemaphoreType.DMA((TOK - 1,)),
    pltpu.SemaphoreType.DMA,
]


def dense_rows(found, own, begin, a1h, a1s, a1f, b1h, b1s, b1f, a2, a2h, a2s, a2f, b2, b2h, b2s, b2f, xsend, xrecv):
    t = lax.axis_index("tok")
    y, x = t // 4, lax.rem(t, 4)
    xu, xd, xf = [lax.rem(x + k, 4) for k in (1, 3, 2)]
    yu, yd, yf = [lax.rem(y + k, 4) for k in (1, 3, 2)]
    along_x = lambda x_of: {"tok": y * 4 + x_of}
    along_y = lambda y_of: {"tok": y_of * 4 + x}
    started = []

    def go(index, src, dst, target):
        copy = remote(src, dst, xsend.at[index], xrecv.at[index], target)
        copy.start()
        started.append(copy)

    def came(index, dst):
        remote(dst, dst, xsend.at[index], xrecv.at[index], along_x(xu)).wait_recv()

    h = WIDTH // 2
    left, right = pl.ds(0, h), pl.ds(h, h)
    low, high = pl.ds(0, 2), pl.ds(2, 2)
    go(0, found.at[low, xf, :, left], a1h.at[0], along_x(xu))
    go(1, found.at[high, xf, :, left], a1h.at[1], along_x(xd))
    go(2, found.at[yf, low, :, right], b1h.at[0], along_y(yu))
    go(3, found.at[yf, high, :, right], b1h.at[1], along_y(yd))
    begin()
    came(0, a1h.at[0])
    a1s[0, :2] = found[:2, xu, :, :h] + a1h[0]
    a1s[0, 2:] = found[2:, xu, :, :h]
    go(4, a1s.at[0], a1f.at[0], along_x(xu))
    came(1, a1h.at[1])
    a1s[1, :2] = found[:2, xd, :, :h]
    a1s[1, 2:] = found[2:, xd, :, :h] + a1h[1]
    go(5, a1s.at[1], a1f.at[1], along_x(xd))
    came(2, b1h.at[0])
    b1s[0, :2] = found[yu, :2, :, h:] + b1h[0]
    b1s[0, 2:] = found[yu, 2:, :, h:]
    go(6, b1s.at[0], b1f.at[0], along_y(yu))
    came(3, b1h.at[1])
    b1s[1, :2] = found[yd, :2, :, h:]
    b1s[1, 2:] = found[yd, 2:, :, h:] + b1h[1]
    go(7, b1s.at[1], b1f.at[1], along_y(yd))
    m = ROWS // 2
    top, bottom = pl.ds(0, m), pl.ds(m, m)
    came(4, a1f.at[0])
    came(5, a1f.at[1])
    a2[...] = found[:, x, :, :h] + a1f[0] + a1f[1]
    go(8, a2.at[yf, top], a2h.at[0], along_y(yu))
    go(9, a2.at[yf, bottom], a2h.at[1], along_y(yd))
    came(6, b1f.at[0])
    came(7, b1f.at[1])
    b2[...] = found[y, :, :, h:] + b1f[0] + b1f[1]
    go(10, b2.at[xf, top], b2h.at[0], along_x(xu))
    go(11, b2.at[xf, bottom], b2h.at[1], along_x(xd))
    came(8, a2h.at[0])
    a2s[0, :m] = a2[yu, :m] + a2h[0]
    a2s[0, m:] = a2[yu, m:]
    go(12, a2s.at[0], a2f.at[0], along_y(yu))
    came(9, a2h.at[1])
    a2s[1, :m] = a2[yd, :m]
    a2s[1, m:] = a2[yd, m:] + a2h[1]
    go(13, a2s.at[1], a2f.at[1], along_y(yd))
    came(10, b2h.at[0])
    b2s[0, :m] = b2[xu, :m] + b2h[0]
    b2s[0, m:] = b2[xu, m:]
    go(14, b2s.at[0], b2f.at[0], along_x(xu))
    came(11, b2h.at[1])
    b2s[1, :m] = b2[xd, :m]
    b2s[1, m:] = b2[xd, m:] + b2h[1]
    go(15, b2s.at[1], b2f.at[1], along_x(xd))
    came(12, a2f.at[0])
    came(13, a2f.at[1])
    own[:ROWS, :h] = a2[y] + a2f[0] + a2f[1]
    came(14, b2f.at[0])
    came(15, b2f.at[1])
    own[:ROWS, h:] = b2[x] + b2f[0] + b2f[1]
    for copy in started:
        copy.wait_send()


def dense_kernel(found, own, *rest):
    greet(tok_peers())
    dense_rows(found, own, lambda: None, *rest)


def dense_exchange(found):
    h, m = WIDTH // 2, ROWS // 2
    return pl.pallas_call(
        dense_kernel,
        out_shape=jax.ShapeDtypeStruct((ROWS, WIDTH), BF16),
        in_specs=[VMEM],
        out_specs=VMEM,
        scratch_shapes=[
            pltpu.VMEM((2, 2, ROWS, h), BF16),
            pltpu.VMEM((2, 4, ROWS, h), BF16),
            pltpu.VMEM((2, 4, ROWS, h), BF16),
            pltpu.VMEM((2, 2, ROWS, h), BF16),
            pltpu.VMEM((2, 4, ROWS, h), BF16),
            pltpu.VMEM((2, 4, ROWS, h), BF16),
            pltpu.VMEM((4, ROWS, h), BF16),
            pltpu.VMEM((2, m, h), BF16),
            pltpu.VMEM((2, ROWS, h), BF16),
            pltpu.VMEM((2, ROWS, h), BF16),
            pltpu.VMEM((4, ROWS, h), BF16),
            pltpu.VMEM((2, m, h), BF16),
            pltpu.VMEM((2, ROWS, h), BF16),
            pltpu.VMEM((2, ROWS, h), BF16),
            pltpu.SemaphoreType.DMA((16,)),
            pltpu.SemaphoreType.DMA((16,)),
        ],
        compiler_params=pltpu.CompilerParams(
            collective_id=1, has_side_effects=True, vmem_limit_bytes=40 << 20
        ),
        name="dense_exchange",
    )(found)


def pack_rows(ids, table, packed, spot_row, slot_s):
    t_at = lax.axis_index("tok")
    shape = (ROWS, ROWS)
    sub = lax.broadcasted_iota(jnp.int32, shape, 0)
    lane = lax.broadcasted_iota(jnp.int32, shape, 1)
    vocab_rows = table.shape[0]
    base = (t_at * vocab_rows).astype(F32)
    symbols = ids[...]
    owners = symbols // vocab_rows
    values = symbols.astype(F32)
    begins = (owners * vocab_rows).astype(F32)
    columns = jnp.transpose(values)
    slot = lax.broadcasted_iota(jnp.int32, (SPACE, ROWS), 0).astype(F32)
    ones = jnp.ones((8, ROWS), BF16)
    yes = lambda mask: jnp.where(mask, 1.0, 0.0).astype(BF16)
    for t in range(TOK):
        row, begin = values[t : t + 1], begins[t : t + 1]
        col = jnp.broadcast_to(columns[:, t : t + 1], shape)
        earlier = dot(ones, yes((col == row) & (sub < lane)))
        first = jnp.where(earlier < 0.5, 1.0, 0.0)
        rank = dot(first.astype(BF16), yes((col < row) & (col >= begin)))[0:1]
        mine = (first[0:1] > 0.5) & (begin == base)
        found = jnp.where((slot == rank) & mine, row - base + 1.0, 0.0)
        slot_s[t * SPACE : t * SPACE + SPACE] = jnp.sum(found, axis=1, keepdims=True) - 1.0

        @pl.when(t_at == t)
        def _():
            spot_row[...] = jnp.broadcast_to(begin * (SPACE / vocab_rows) + rank, (8, ROWS))

    step = 256
    for k in range(TOK * SPACE // step):
        rows = pl.ds(k * step, step)
        numbers = lax.broadcasted_iota(jnp.int32, (step, vocab_rows), 1).astype(F32)
        value = dot(yes(numbers == slot_s[rows]), table[...]).astype(BF16)
        many = step // SPACE
        packed[k * many : k * many + many] = value.reshape(many, SPACE, WIDTH)
    return jnp.transpose(spot_row[...])[:, 0:1]


def finish_kernel(source, hit, made_out, made_att, made_ffn, returned, store, out, shift_att, shift_ffn, store_out):
    step = pl.program_id(0)

    @pl.when(step == 0)
    def _():
        out[...] = made_out[...]
        shift_att[...] = made_att[...]
        shift_ffn[...] = made_ffn[...]

    for k in range(4):
        slot = step * 4 + k
        page = returned[source[slot]].astype(F32)
        taken = hit[slot] > 0

        def put(column, value):
            columns = slice(column, column + 128)
            store_out[k, :, columns] = jnp.where(taken, value, store[k, :, columns])

        flat_page(page, put)


def finish(source, hit, made_out, made_att, made_ffn, returned, store):
    full = lambda *shape: pl.BlockSpec(shape, lambda k, *_: (0,) * len(shape))
    slots = pl.BlockSpec((4, REQ, HIDDEN), lambda k, *_: (k, 0, 0))
    return pl.pallas_call(
        finish_kernel,
        out_shape=tuple(jax.ShapeDtypeStruct(v.shape, v.dtype) for v in (made_out, made_att, made_ffn, store)),
        grid_spec=pltpu.PrefetchScalarGridSpec(
            num_scalar_prefetch=2,
            grid=(4,),
            in_specs=[
                full(ROWS, WIDTH), full(BRANCH, WIDTH), full(BRANCH, WIDTH),
                full(TOK, PAIRS, HEAD, 128), slots,
            ],
            out_specs=(full(ROWS, WIDTH), full(BRANCH, WIDTH), full(BRANCH, WIDTH), slots),
        ),
        name="finish",
    )(source, hit, made_out, made_att, made_ffn, returned, store)


def dot(a, b):
    return jnp.dot(a, b, preferred_element_type=F32)


def normed_and_step(block, prior, mean, scale, gain):
    normed = (block.astype(F32) - mean) * scale * gain
    row = lax.broadcasted_iota(jnp.int32, (ROWS, WIDTH), 0)
    spread = (
        lax.broadcasted_iota(jnp.int32, (ROWS, BRANCH), 0) // DRAFT
        == lax.broadcasted_iota(jnp.int32, (ROWS, BRANCH), 1)
    )
    carried = dot(spread.astype(BF16), prior)
    before = jnp.where(lax.rem(row, DRAFT) == 0, carried, pltpu.roll(normed, 1, axis=0))
    return normed, before - normed


def kept_row(normed, prior, kept_column):
    column = lax.broadcasted_iota(jnp.int32, (BRANCH, ROWS), 1)
    branch = lax.broadcasted_iota(jnp.int32, (BRANCH, ROWS), 0)
    pick = (column == branch * DRAFT + kept_column - 1) & (kept_column > 0)
    picked = dot(pick.astype(BF16), normed.astype(BF16))
    return jnp.where(kept_column > 0, picked, prior.astype(F32)).astype(BF16)


def head_ones(size):
    return (
        lax.broadcasted_iota(jnp.int32, (size, size), 0) // HEAD
        == lax.broadcasted_iota(jnp.int32, (size, size), 1) // HEAD
    ).astype(BF16)


def per_head(value):
    ones = head_ones(256)
    return jnp.concatenate([dot(value[:, :256], ones), dot(value[:, 256:], ones)], axis=1)


def per_head_fine(value):
    top = value.astype(BF16)
    rest = (value - top.astype(F32)).astype(BF16)
    return per_head(top) + per_head(rest)


def two_heads(page):
    side = lax.broadcasted_iota(jnp.int32, (HEAD, 128), 1) < HEAD
    none = jnp.zeros_like(page)
    return jnp.concatenate([jnp.where(side, page, none), jnp.where(side, none, page)], axis=0)


META = ("slots", TOK), ("owner_of", REQ), ("page_of", BRANCH), ("winner", REQ), ("kept", REQ), ("pick", TOK), ("dense", 1)


def starts():
    at, result = 0, {}
    for name, count in META:
        result[name] = at
        at += count
    return result


def row_stats(value_ref, mean, scale):
    step = 64

    @pl.loop(0, ROWS // step)
    def _(k):
        rows = pl.ds(pl.multiple_of(k * step, step), step)
        value = value_ref[rows].astype(F32)
        middle = jnp.mean(value, axis=-1, keepdims=True)
        centered = value - middle
        spread = jnp.mean(centered * centered, axis=-1, keepdims=True)
        mean[rows] = middle
        scale[rows] = lax.rsqrt(spread + EPSILON)


def layer_kernel(
    meta, ids, dense_own, priors, scales, blends, narrow, widen, baseline, boost, kept_column,
    store_w, table_w, attention_w, result_w, lookup_w, gating_w, content_w,
    out, shift_att, shift_ffn, returned,
    store, table, packed, spot_row, slot_s, lsem,
    whole, residuals, results, lookups, gatings, contents, wbuf, part,
    mated, sums, halves, full, rsend, rrecv,
    own, residual, parcels, psend, precv, plocal, gsend, grecv, glocal,
    out_pages, in_pages, tsend, trecv, tlocal, made, bsend, brecv, blocal,
    acc, low, w_s, y_s, p_s, ffn, mean, scale, wsend, wrecv, wlocal, wsem,
):
    base = starts()
    word = lambda name, index: meta[base[name] + index]
    t, g = lax.axis_index("tok"), lax.axis_index("grp")
    mine = block_of(g)
    bring_table = pltpu.make_async_copy(table_w, table, lsem.at[0])
    bring_store = pltpu.make_async_copy(store_w, store, lsem.at[1])
    bring_table.start()
    bring_store.start()
    greet(tok_peers() + grp_peers())

    def load(k):
        rows = pl.ds(pl.multiple_of(k * WIDTH, WIDTH), WIDTH)
        slot = lax.rem(k, 2)
        return pltpu.make_async_copy(attention_w.at[:, rows], wbuf.at[slot], wsem.at[slot])

    res, look, gat, con = [
        gather_tok(w, views(all_of), wsend.at[k], wrecv.at[k], wlocal.at[k])
        for k, (w, views, all_of) in enumerate(
            (
                (result_w, result_views, results),
                (lookup_w, stack_views, lookups),
                (gating_w, stack_views, gatings),
                (content_w, result_views, contents),
            )
        )
    ]
    res[0]()
    look[0]()
    load(0).start()
    load(1).start()
    bring_table.wait()
    spot = pack_rows(ids, table, packed, spot_row, slot_s)
    keep = pltpu.make_async_copy(packed.at[t], parcels.at[t], plocal)
    keep.start()
    copies = []
    for k in range(1, TOK):
        peer = lax.rem(t + k, TOK)
        copy = remote(packed.at[peer], parcels.at[t], psend.at[k - 1], precv.at[k - 1], {"tok": peer})
        copy.start()
        copies.append(copy)
    con[0]()
    gat[0]()
    bring_store.wait()

    @pl.loop(0, TOK)
    def _(peer):
        page = store[word("slots", peer)]

        def put(pair, row, value):
            out_pages[peer, pair, pl.ds(row, 16)] = value.astype(BF16)

        pair_page(page, put)

    res[1]()
    look[1]()
    own[ROWS:] = priors[...]
    slots = lax.broadcasted_iota(jnp.int32, (ROWS, TOK * SPACE), 1)
    choice = (slots == spot.astype(jnp.int32)).astype(BF16)
    keep.wait()
    for k in range(1, TOK):
        origin = lax.rem(t + TOK - k, TOK)
        remote(packed.at[t], parcels.at[origin], psend.at[k - 1], precv.at[k - 1], {"tok": origin}).wait_recv()
    picked = dot(choice, parcels[...].reshape(TOK * SPACE, WIDTH)).astype(BF16)
    own[:ROWS] = jnp.where(word("dense", 0) > 0, dense_own[...], picked)
    trades = []

    def bring():
        res[2]()
        trades.append(trade_start(out_pages, in_pages, tsend, trecv, tlocal))

    gather_grp(own, whole, gsend, grecv, glocal, [bring, look[2]])
    for copy in copies:
        copy.wait_send()

    row_stats(whole, mean, scale)
    acc[...] = jnp.zeros_like(acc)
    low[...] = jnp.zeros_like(low)
    shape3 = (BRANCH, DRAFT, WIDTH)
    flat = lambda value: value.reshape(ROWS, WIDTH)

    def mix(k):
        load(k).wait()
        columns = block_of(k)
        weights = wbuf.at[lax.rem(k, 2)]
        prior = whole[ROWS : ROWS + BRANCH, columns]
        normed, delta = normed_and_step(whole[:ROWS, columns], prior, mean[...], scale[...], scales[0:1, columns])

        @pl.when(k == g)
        def _():
            shift_att[...] = kept_row(normed, prior, kept_column[...])

        blend = blends[:, columns]
        for c in range(4):
            acc[c] += dot((normed + delta * blend[c : c + 1]).astype(BF16), weights[c]).reshape(shape3)
        low[...] += dot((normed + delta * blend[4:5]).astype(BF16), narrow[columns])

        @pl.when(k < GRP - 2)
        def _():
            load(k + 2).start()

    pl.loop(0, 4)(mix)
    res[3]()
    pl.loop(4, 8)(mix)
    trade_end(out_pages, in_pages, tsend, trecv, trades[0])

    lowrank = jnp.tanh(low[...]).astype(BF16)
    w_s[...] = jnp.exp(-jnp.exp(baseline[:, mine] + dot(lowrank, widen[...]))).reshape(shape3)
    position = lax.broadcasted_iota(jnp.int32, shape3, 1)
    r3, k3, v3, w3 = acc[0], acc[1], acc[2], w_s[...]
    y_s[...] = per_head_fine(flat(r3) * boost[:, mine] * flat(k3)) * flat(v3)
    p_s[...] = jnp.ones_like(p_s)
    for s in range(DRAFT - 2, -1, -1):
        decay = jnp.where(position > s + 1, p_s[...].reshape(shape3) * w3[:, s + 1 : s + 2], 1.0)
        p_s[...] = decay.reshape(ROWS, WIDTH)
        term = jnp.where(position > s, r3 * decay * k3[:, s : s + 1], 0.0)
        score = per_head(term.reshape(ROWS, WIDTH).astype(BF16)).reshape(shape3)
        y_s[...] += (score * v3[:, s : s + 1]).reshape(ROWS, WIDTH)
    decay = jnp.where(position > 0, p_s[...].reshape(shape3) * w3[:, 0:1], 1.0)
    p_s[...] = flat(r3 * decay)

    @pl.loop(0, BRANCH)
    def _(b):
        rows = pl.ds(pl.multiple_of(b * DRAFT, DRAFT), DRAFT)
        page = in_pages[word("page_of", b)]
        for pair in range(PAIRS):
            lanes = pl.ds(pair * 128, 128)
            y_s[rows, lanes] += dot(p_s[rows, lanes].astype(BF16), two_heads(page[pair]))

    look[3]()
    value = y_s[...]
    centered = value - per_head_fine(value) * (1.0 / HEAD)
    spread = per_head_fine(centered * centered) * (1.0 / HEAD)
    gate = flat(acc[3])
    gate = gate * jax.nn.sigmoid(gate)
    attended = (centered * lax.rsqrt(spread + HEAD_EPSILON) * scales[2:3, mine] * gate).astype(BF16)
    res[4]()
    for y_of in range(4):
        part[:, y_of * 1024 : y_of * 1024 + 1024] = dot(attended, results[y_of]).astype(BF16)

    def states():
        con[2]()
        eye = (
            lax.broadcasted_iota(jnp.int32, (128, 128), 0)
            == lax.broadcasted_iota(jnp.int32, (128, 128), 1)
        )
        spot16 = lax.broadcasted_iota(jnp.int32, (DRAFT, WIDTH), 0)
        side = lax.broadcasted_iota(jnp.int32, (HEAD, 128), 1) < HEAD

        @pl.loop(0, REQ)
        def _(q):
            b = word("winner", q)
            count = word("kept", q)
            live = spot16 < count
            tail = jnp.where(live, w_s[b], 1.0)
            for hop in (1, 2, 4, 8):
                later = pltpu.roll(tail, DRAFT - hop, axis=0)
                tail = tail * jnp.where(spot16 < DRAFT - hop, later, 1.0)
            after = jnp.where(spot16 < DRAFT - 1, pltpu.roll(tail, DRAFT - 1, axis=0), 1.0)
            keys = jnp.where(live, acc[1, b], 0.0) * after
            values = acc[2, b].astype(BF16)
            page = in_pages[word("owner_of", q)]
            for pair in range(PAIRS):
                lanes = slice(pair * 128, pair * 128 + 128)
                fade = jnp.where(eye, tail[0:1, lanes], 0.0)
                left = jnp.concatenate([keys[:, lanes], fade], axis=0).astype(BF16)
                right = jnp.concatenate([values[:, lanes], two_heads(page[pair])], axis=0)
                both = lax.dot_general(left, right, (((0,), (0,)), ((), ())), preferred_element_type=F32)
                made[q, pair] = jnp.where(side, both[:HEAD], both[HEAD:]).astype(BF16)

        @pl.loop(0, TOK)
        def _(peer):
            out_pages[peer] = made[word("pick", peer)]

        trades.append(trade_start(out_pages, returned, bsend, brecv, blocal))

    con[1]()
    total = reduce_grp(part, mated, sums, halves, full, rsend, rrecv, states)
    residual[...] = (own[:ROWS].astype(F32) + total).astype(BF16)
    gather_grp(residual, residuals, gsend, grecv, glocal, [look[4], con[3]])
    row_stats(residuals, mean, scale)
    gat[1]()

    ffn[...] = jnp.zeros_like(ffn)
    gat[2]()

    @pl.loop(0, GRP)
    def _(k):
        columns = block_of(k)
        prior = whole[ROWS + BRANCH :, columns]
        normed, delta = normed_and_step(residuals[:, columns], prior, mean[...], scale[...], scales[1:2, columns])

        @pl.when(k == g)
        def _():
            shift_ffn[...] = kept_row(normed, prior, kept_column[...])

        blend = blends[:, columns]
        y_of, x_of = k // 2, pl.ds(lax.rem(k, 2) * 2, 2)
        ffn[...] += dot(
            (normed + delta * blend[5:6]).astype(BF16), lookups[y_of, x_of].reshape(WIDTH, KEYS)
        )
        residuals[:, columns] = (normed + delta * blend[6:7]).astype(BF16)

    hidden = jnp.square(jnp.maximum(ffn[...], 0.0)).astype(BF16)
    con[4]()
    for y_of in range(4):
        part[:, y_of * 1024 : y_of * 1024 + 1024] = dot(hidden, contents[y_of]).astype(BF16)

    def pages():
        gat[3]()
        trade_end(out_pages, returned, bsend, brecv, trades[1])

    total = reduce_grp(part, mated, sums, halves, full, rsend, rrecv, pages)
    gat[4]()
    received = jnp.zeros((ROWS, WIDTH), F32)
    for k in range(GRP):
        received += dot(
            residuals[:, k * WIDTH : k * WIDTH + WIDTH],
            gatings[k // 2, k % 2 * 2 : k % 2 * 2 + 2].reshape(WIDTH, WIDTH),
        )
    out[...] = (residual[...].astype(F32) + jax.nn.sigmoid(received) * total).astype(BF16)


def layer(meta, ids, dense_own, priors, scales, blends, narrow, widen, baseline, boost, kept_column, *weights):
    rows = ROWS + 2 * BRANCH
    wide = lambda *shape: pltpu.VMEM(shape, BF16)
    fine = lambda *shape: pltpu.VMEM(shape, F32)
    dma = lambda *shape: pltpu.SemaphoreType.DMA(shape)
    return pl.pallas_call(
        layer_kernel,
        out_shape=(
            jax.ShapeDtypeStruct((ROWS, WIDTH), BF16),
            jax.ShapeDtypeStruct((BRANCH, WIDTH), BF16),
            jax.ShapeDtypeStruct((BRANCH, WIDTH), BF16),
            jax.ShapeDtypeStruct((TOK, PAIRS, HEAD, 128), BF16),
        ),
        in_specs=[pl.BlockSpec(memory_space=pltpu.SMEM)] + [VMEM] * 10 + [ANY] * 7,
        out_specs=(VMEM, VMEM, VMEM, VMEM),
        scratch_shapes=[
            fine(*weights[0].shape),
            wide(*weights[1].shape),
            wide(TOK, SPACE, WIDTH),
            fine(8, ROWS),
            fine(TOK * SPACE, 1),
            dma(2),
            wide(rows, HIDDEN),
            wide(ROWS, HIDDEN),
            wide(4, WIDTH, 1024),
            wide(4, 4, 256, KEYS),
            wide(4, 4, 256, WIDTH),
            wide(4, KEYS, 1024),
            wide(2, 4, WIDTH, WIDTH),
            wide(ROWS, HIDDEN),
            *REDUCE_SCRATCH,
            wide(rows, WIDTH),
            wide(ROWS, WIDTH),
            wide(TOK, SPACE, WIDTH),
            dma(TOK - 1),
            dma(TOK - 1),
            pltpu.SemaphoreType.DMA,
            dma(9),
            dma(9),
            pltpu.SemaphoreType.DMA,
            wide(TOK, PAIRS, HEAD, 128),
            wide(TOK, PAIRS, HEAD, 128),
            *TRADE_SEMAPHORES,
            wide(REQ, PAIRS, HEAD, 128),
            *TRADE_SEMAPHORES,
            fine(4, BRANCH, DRAFT, WIDTH),
            fine(ROWS, 128),
            fine(BRANCH, DRAFT, WIDTH),
            fine(ROWS, WIDTH),
            fine(ROWS, WIDTH),
            fine(ROWS, KEYS),
            fine(ROWS, 1),
            fine(ROWS, 1),
            dma(4, 16),
            dma(4, 16),
            dma(4),
            dma(2),
        ],
        compiler_params=pltpu.CompilerParams(
            collective_id=2, has_side_effects=True, vmem_limit_bytes=60 << 20
        ),
        cost_estimate=pl.CostEstimate(flops=12 << 30, transcendentals=1 << 20, bytes_accessed=60 << 20),
        name="layer",
    )(meta, ids, dense_own, priors, scales, blends, narrow, widen, baseline, boost, kept_column, *weights)


def body(
    guess_symbol_ids,
    symbol_vector_lookup,
    prior_attention_normed,
    prior_feedforward_normed,
    layernorm_scales,
    lagged_blend_ratios,
    attention_matrices,
    forgetting_baseline_vector,
    forgetting_narrow_matrix,
    forgetting_widen_matrix,
    diagonal_boost,
    attention_result_matrix,
    feedforward_lookup_matrix,
    feedforward_content_matrix,
    feedforward_gating_matrix,
    memory_matrix_store,
    query_memory_slot,
    candidate_tally_each_query,
    kept_guess_tally,
):
    tok_at = lax.axis_index("tok")
    vocab_rows = symbol_vector_lookup.shape[0]
    slot_count = memory_matrix_store.shape[0]

    priors = jnp.concatenate([prior_attention_normed, prior_feedforward_normed], axis=0)

    owners = (query_memory_slot // slot_count).reshape(TOK, REQ)
    places = (query_memory_slot % slot_count).reshape(TOK, REQ)
    owned_here = owners == tok_at
    send_slot = jnp.sum(jnp.where(owned_here, places, 0), axis=1)
    sending = jnp.any(owned_here, axis=1)
    ids = guess_symbol_ids.reshape(TOK, ROWS)
    order = jnp.arange(ROWS, dtype=jnp.int32)
    again = (ids[:, :, None] == ids[:, None, :]) & (order[:, None] > order[None, :])
    first = ~jnp.any(again, axis=2)
    shard = (ids // vocab_rows)[:, None, :] == jnp.arange(TOK, dtype=jnp.int32)[None, :, None]
    need = jnp.sum((shard & first[:, None, :]).astype(jnp.int32), axis=2)
    crowded = jnp.max(need) > SPACE

    def dense(_):
        wanted = guess_symbol_ids - tok_at * vocab_rows
        inside = (wanted >= 0) & (wanted < vocab_rows)
        found = jnp.take(symbol_vector_lookup, jnp.clip(wanted, 0, vocab_rows - 1), axis=0)
        found = jnp.where(inside[:, None], found, jnp.zeros((), BF16)).reshape(4, 4, ROWS, WIDTH)
        return dense_exchange(found)

    dense_own = lax.cond(crowded, dense, lambda _: jnp.zeros((ROWS, WIDTH), BF16), 0)

    my_owners = lax.dynamic_index_in_dim(owners, tok_at, 0, keepdims=False)
    my_counts = lax.dynamic_index_in_dim(candidate_tally_each_query, tok_at, 0, keepdims=False)
    local_ids = jnp.arange(BRANCH, dtype=jnp.int32)
    request_ends = jnp.cumsum(my_counts)
    request_of = jnp.sum((request_ends[None, :] <= local_ids[:, None]).astype(jnp.int32), axis=1)
    branch_score = kept_guess_tally * BRANCH + (BRANCH - 1 - local_ids)
    member = request_of[None, :] == jnp.arange(REQ, dtype=jnp.int32)[:, None]
    best_score = jnp.max(jnp.where(member, branch_score[None, :], -1), axis=1)
    winner = BRANCH - 1 - best_score % BRANCH

    targets = my_owners[None, :] == jnp.arange(TOK, dtype=jnp.int32)[:, None]
    pick_index = jnp.sum(
        jnp.where(targets, jnp.arange(REQ, dtype=jnp.int32)[None, :], 0), axis=1
    )
    hit = (send_slot[None, :] == jnp.arange(slot_count, dtype=jnp.int32)[:, None]) & sending[None, :]
    source = jnp.sum(jnp.where(hit, jnp.arange(TOK, dtype=jnp.int32)[None, :], 0), axis=1)
    meta = jnp.concatenate(
        [
            send_slot, my_owners, my_owners[request_of], winner, kept_guess_tally[winner], pick_index,
            crowded.astype(jnp.int32).reshape(1),
        ]
    )
    made_out, made_att, made_ffn, returned = layer(
        meta, ids, dense_own, priors,
        layernorm_scales, lagged_blend_ratios, forgetting_narrow_matrix, forgetting_widen_matrix,
        forgetting_baseline_vector.reshape(1, HIDDEN), diagonal_boost.reshape(1, HIDDEN),
        kept_guess_tally.reshape(BRANCH, 1), memory_matrix_store, symbol_vector_lookup, attention_matrices, attention_result_matrix,
        feedforward_lookup_matrix, feedforward_gating_matrix, feedforward_content_matrix,
    )
    return finish(
        source, jnp.any(hit, axis=1).astype(jnp.int32), made_out, made_att, made_ffn, returned,
        memory_matrix_store,
    )


def solution(mesh):
    in_specs = (
        P(),
        P("tok", "grp"),
        P("tok", "grp"),
        P("tok", "grp"),
        P(),
        P(),
        P(None, None, "grp"),
        P(),
        P(),
        P(None, "grp"),
        P(),
        P("grp", "tok"),
        P("tok", "grp"),
        P("grp", "tok"),
        P("tok", "grp"),
        P("tok", "grp", None),
        P(),
        P(),
        P("tok"),
    )
    out_specs = (P("tok", "grp"), P("tok", "grp"), P("tok", "grp"), P("tok", "grp", None))
    return jax.shard_map(body, mesh=mesh, in_specs=in_specs, out_specs=out_specs, check_vma=False)
```

```python
import functools

import jax
import jax.numpy as jnp
from jax import lax
from jax.experimental import pallas as pl
from jax.experimental.pallas import tpu as pltpu
from jax.sharding import PartitionSpec as P

HIDDEN = 4096
HEAD = 64
DRAFT = 16
BRANCH = 16
ROWS = BRANCH * DRAFT
WIDTH = 512
TOK = 16
GRP = 8
REQ = 8
PAIRS = 4
KEYS = 896
SPACE = 32
EPSILON = 1e-05
HEAD_EPSILON = 0.00064
F32 = jnp.float32
BF16 = jnp.bfloat16
MESH = pl.DeviceIdType.MESH
ANY = pl.BlockSpec(memory_space=pl.ANY)
VMEM = pl.BlockSpec(memory_space=pltpu.VMEM)


def remote(src, dst, send, recv, device):
    return pltpu.make_async_remote_copy(
        src_ref=src, dst_ref=dst, send_sem=send, recv_sem=recv, device_id=device, device_id_type=MESH
    )


def greet(devices):
    barrier = pltpu.get_barrier_semaphore()
    for device in devices:
        pl.semaphore_signal(barrier, inc=1, device_id=device, device_id_type=MESH)
    pl.semaphore_wait(barrier, len(devices))


def grp_places():
    g = lax.axis_index("grp")
    z, core = g // 2, g % 2
    up = lax.rem(z + 1, 4) * 2 + core
    down = lax.rem(z + 3, 4) * 2 + core
    far = lax.rem(z + 2, 4) * 2 + core
    mate = z * 2 + 1 - core
    return g, up, down, far, mate


def block_of(g):
    return pl.ds(pl.multiple_of(g * WIDTH, WIDTH), WIDTH)


def flip(g):
    return g + 1 - 2 * lax.rem(g, 2)


def gather_grp(own, out, send, recv, local, between=()):
    between = list(between)

    def aside():
        if between:
            between.pop(0)()

    rows = out.shape[0]
    half = rows // 2
    g, up, down, far, mate = grp_places()
    first, last, whole = pl.ds(0, half), pl.ds(half, rows - half), pl.ds(0, rows)
    at = lambda part, g_of: out.at[part, block_of(g_of)]
    keep = pltpu.make_async_copy(own, at(whole, g), local)
    keep.start()
    started = []

    def go(index, src, part, g_of, target):
        copy = remote(src, at(part, g_of), send.at[index], recv.at[index], {"grp": target})
        copy.start()
        started.append(copy)

    def came(index, part, g_of):
        remote(at(part, g_of), at(part, g_of), send.at[index], recv.at[index], {"grp": mate}).wait_recv()

    go(0, own, whole, g, up)
    go(1, own, whole, g, down)
    go(2, own, whole, g, mate)
    aside()
    came(0, whole, down)
    go(3, at(first, down), first, down, up)
    go(5, at(whole, down), whole, down, mate)
    came(1, whole, up)
    go(4, at(last, up), last, up, down)
    go(6, at(whole, up), whole, up, mate)
    aside()
    came(3, first, far)
    go(7, at(first, far), first, far, mate)
    came(4, last, far)
    go(8, at(last, far), last, far, mate)
    came(2, whole, mate)
    came(5, whole, flip(down))
    came(6, whole, flip(up))
    came(7, first, flip(far))
    came(8, last, flip(far))
    while between:
        aside()
    keep.wait()
    for copy in started:
        copy.wait_send()


def reduce_grp(part, mated, sums, halves, full, send, recv, meanwhile=lambda: None):
    g, up, down, far, mate = grp_places()
    half = ROWS // 2
    started = []

    def go(index, src, dst, target):
        copy = remote(src, dst, send.at[index], recv.at[index], {"grp": target})
        copy.start()
        started.append(copy)

    def came(index, dst):
        remote(dst, dst, send.at[index], recv.at[index], {"grp": mate}).wait_recv()

    order = (far, up, down, g)
    for k in range(4):
        go(k, part.at[:, block_of(flip(order[k]))], mated.at[k], mate)

    def own(k):
        return part[:, block_of(order[k])].astype(F32) + mated[k].astype(F32)

    came(0, mated.at[0])
    sums[0] = own(0).astype(BF16)
    go(4, sums.at[0, pl.ds(0, half)], halves.at[0], up)
    go(5, sums.at[0, pl.ds(half, half)], halves.at[1], down)
    came(1, mated.at[1])
    came(4, halves.at[0])
    sums[1, :half] = (own(1)[:half] + halves[0].astype(F32)).astype(BF16)
    sums[1, half:] = own(1)[half:].astype(BF16)
    go(6, sums.at[1], full.at[0], up)
    came(2, mated.at[2])
    came(5, halves.at[1])
    sums[2, :half] = own(2)[:half].astype(BF16)
    sums[2, half:] = (own(2)[half:] + halves[1].astype(F32)).astype(BF16)
    go(7, sums.at[2], full.at[1], down)
    meanwhile()
    came(3, mated.at[3])
    came(6, full.at[0])
    came(7, full.at[1])
    total = own(3) + full[0].astype(F32) + full[1].astype(F32)
    for copy in started:
        copy.wait_send()
    return total


REDUCE_SCRATCH = [
    pltpu.VMEM((4, ROWS, WIDTH), BF16),
    pltpu.VMEM((3, ROWS, WIDTH), BF16),
    pltpu.VMEM((2, ROWS // 2, WIDTH), BF16),
    pltpu.VMEM((2, ROWS, WIDTH), BF16),
    pltpu.SemaphoreType.DMA((8,)),
    pltpu.SemaphoreType.DMA((8,)),
]


def result_views(out):
    cols = lambda x_of: pl.ds(pl.multiple_of(x_of * 256, 256), 256)
    return (
        lambda rows, y_of, x_of: out.at[y_of, rows, cols(x_of)],
        lambda rows, y_of: out.at[y_of, rows],
        lambda rows, x_of: out.at[:, rows, cols(x_of)],
    )


def stack_views(out):
    return (
        lambda rows, y_of, x_of: out.at[y_of, x_of, rows],
        lambda rows, y_of: out.at[y_of, :, rows],
        lambda rows, x_of: out.at[:, x_of, rows],
    )


def gather_tok(own, views, send, recv, local):
    t = lax.axis_index("tok")
    y, x = t // 4, lax.rem(t, 4)
    xu, xd, xf = [lax.rem(x + k, 4) for k in (1, 3, 2)]
    yu, yd, yf = [lax.rem(y + k, 4) for k in (1, 3, 2)]
    along_x = lambda x_of: {"tok": y * 4 + x_of}
    along_y = lambda y_of: {"tok": y_of * 4 + x}
    one, wide, tall = views
    count = own.shape[0]
    f0, f1 = pl.ds(0, count // 2), pl.ds(count // 2, count // 2)
    fa, fb = [pl.ds(f0.start + k * (f0.size // 2), f0.size // 2) for k in (0, 1)]
    la, lb = [pl.ds(f1.start + k * (f1.size // 2), f1.size // 2) for k in (0, 1)]
    started = []

    def go(index, src, dst, target):
        copy = remote(src, dst, send.at[index], recv.at[index], target)
        copy.start()
        started.append(copy)

    def came(index, dst):
        remote(dst, dst, send.at[index], recv.at[index], along_x(xu)).wait_recv()

    keep = pltpu.make_async_copy(own, one(pl.ds(0, count), y, x), local)

    def begin():
        keep.start()
        go(0, own.at[f0], one(f0, y, x), along_x(xu))
        go(1, own.at[f0], one(f0, y, x), along_x(xd))
        go(2, own.at[f1], one(f1, y, x), along_y(yu))
        go(3, own.at[f1], one(f1, y, x), along_y(yd))

    def relay():
        came(0, one(f0, y, xd))
        go(4, one(fa, y, xd), one(fa, y, xd), along_x(xu))
        came(2, one(f1, yd, x))
        go(6, one(la, yd, x), one(la, yd, x), along_y(yu))
        came(1, one(f0, y, xu))
        go(5, one(fb, y, xu), one(fb, y, xu), along_x(xd))
        came(3, one(f1, yu, x))
        go(7, one(lb, yu, x), one(lb, yu, x), along_y(yd))

    def turn():
        keep.wait()
        came(4, one(fa, y, xf))
        came(5, one(fb, y, xf))
        go(8, wide(f0, y), wide(f0, y), along_y(yu))
        go(9, wide(f0, y), wide(f0, y), along_y(yd))
        came(6, one(la, yf, x))
        came(7, one(lb, yf, x))
        go(10, tall(f1, x), tall(f1, x), along_x(xu))
        go(11, tall(f1, x), tall(f1, x), along_x(xd))

    def last():
        came(8, wide(f0, yd))
        go(12, wide(fa, yd), wide(fa, yd), along_y(yu))
        came(10, tall(f1, xd))
        go(14, tall(la, xd), tall(la, xd), along_x(xu))
        came(9, wide(f0, yu))
        go(13, wide(fb, yu), wide(fb, yu), along_y(yd))
        came(11, tall(f1, xu))
        go(15, tall(lb, xu), tall(lb, xu), along_x(xd))

    def end():
        came(12, wide(fa, yf))
        came(13, wide(fb, yf))
        came(14, tall(la, xf))
        came(15, tall(lb, xf))
        for copy in started:
            copy.wait_send()

    return begin, relay, turn, last, end


def grp_peers():
    _, up, down, _, mate = grp_places()
    return [{"grp": up}, {"grp": down}, {"grp": mate}]


def tok_peers():
    t = lax.axis_index("tok")
    return [{"tok": lax.rem(t + k, TOK)} for k in range(1, TOK)]


def page_masks():
    even = lax.rem(lax.broadcasted_iota(jnp.int32, (8, 128), 0), 2) == 0
    left = lax.broadcasted_iota(jnp.int32, (8, 128), 1) < HEAD
    return even, left


def pair_page(page, put):
    even, left = page_masks()
    for block in range(4):
        rows = [[] for _ in range(PAIRS)]
        for group in (2 * block, 2 * block + 1):
            pieces = []
            for m in range(4 * group, 4 * group + 4):
                here = page[:, m * 128 : m * 128 + 128]
                swapped = pltpu.roll(here, HEAD, axis=1)
                pieces += [jnp.where(even, here, swapped), jnp.where(even, swapped, here)]
            turned = jnp.swapaxes(jnp.stack(pieces), 0, 1)
            for pair in range(PAIRS):
                rows[pair].append(jnp.where(left, turned[2 * pair], turned[2 * pair + 1]))
        for pair in range(PAIRS):
            put(pair, 16 * block, jnp.concatenate(rows[pair], axis=0))


def flat_page(page, put):
    even, left = page_masks()
    for group in range(8):
        rows = [page[pair, 8 * group : 8 * group + 8] for pair in range(PAIRS)]
        turned = jnp.swapaxes(jnp.stack([rows[h // 2] for h in range(8)]), 0, 1)
        for m in range(4):
            first, second = turned[2 * m], turned[2 * m + 1]
            swapped_first = pltpu.roll(first, HEAD, axis=1)
            swapped_second = pltpu.roll(second, HEAD, axis=1)
            put(
                (4 * group + m) * 128,
                jnp.where(
                    left,
                    jnp.where(even, first, swapped_first),
                    jnp.where(even, swapped_second, second),
                ),
            )


def trade_start(out_pages, in_pages, send, recv, local):
    t = lax.axis_index("tok")
    keep = pltpu.make_async_copy(out_pages.at[t], in_pages.at[t], local)
    keep.start()
    for k in range(1, TOK):
        peer = lax.rem(t + k, TOK)
        remote(out_pages.at[peer], in_pages.at[t], send.at[k - 1], recv.at[k - 1], {"tok": peer}).start()
    return keep


def trade_end(out_pages, in_pages, send, recv, keep):
    t = lax.axis_index("tok")
    keep.wait()
    for k in range(1, TOK):
        peer = lax.rem(t + k, TOK)
        origin = lax.rem(t + TOK - k, TOK)
        copy = remote(out_pages.at[peer], in_pages.at[origin], send.at[k - 1], recv.at[k - 1], {"tok": peer})
        copy.wait_recv()
        copy.wait_send()


TRADE_SEMAPHORES = [
    pltpu.SemaphoreType.DMA((TOK - 1,)),
    pltpu.SemaphoreType.DMA((TOK - 1,)),
    pltpu.SemaphoreType.DMA,
]


def dense_rows(found, own, begin, a1h, a1s, a1f, b1h, b1s, b1f, a2, a2h, a2s, a2f, b2, b2h, b2s, b2f, xsend, xrecv):
    t = lax.axis_index("tok")
    y, x = t // 4, lax.rem(t, 4)
    xu, xd, xf = [lax.rem(x + k, 4) for k in (1, 3, 2)]
    yu, yd, yf = [lax.rem(y + k, 4) for k in (1, 3, 2)]
    along_x = lambda x_of: {"tok": y * 4 + x_of}
    along_y = lambda y_of: {"tok": y_of * 4 + x}
    started = []

    def go(index, src, dst, target):
        copy = remote(src, dst, xsend.at[index], xrecv.at[index], target)
        copy.start()
        started.append(copy)

    def came(index, dst):
        remote(dst, dst, xsend.at[index], xrecv.at[index], along_x(xu)).wait_recv()

    h = WIDTH // 2
    left, right = pl.ds(0, h), pl.ds(h, h)
    low, high = pl.ds(0, 2), pl.ds(2, 2)
    go(0, found.at[low, xf, :, left], a1h.at[0], along_x(xu))
    go(1, found.at[high, xf, :, left], a1h.at[1], along_x(xd))
    go(2, found.at[yf, low, :, right], b1h.at[0], along_y(yu))
    go(3, found.at[yf, high, :, right], b1h.at[1], along_y(yd))
    begin()
    came(0, a1h.at[0])
    a1s[0, :2] = found[:2, xu, :, :h] + a1h[0]
    a1s[0, 2:] = found[2:, xu, :, :h]
    go(4, a1s.at[0], a1f.at[0], along_x(xu))
    came(1, a1h.at[1])
    a1s[1, :2] = found[:2, xd, :, :h]
    a1s[1, 2:] = found[2:, xd, :, :h] + a1h[1]
    go(5, a1s.at[1], a1f.at[1], along_x(xd))
    came(2, b1h.at[0])
    b1s[0, :2] = found[yu, :2, :, h:] + b1h[0]
    b1s[0, 2:] = found[yu, 2:, :, h:]
    go(6, b1s.at[0], b1f.at[0], along_y(yu))
    came(3, b1h.at[1])
    b1s[1, :2] = found[yd, :2, :, h:]
    b1s[1, 2:] = found[yd, 2:, :, h:] + b1h[1]
    go(7, b1s.at[1], b1f.at[1], along_y(yd))
    m = ROWS // 2
    top, bottom = pl.ds(0, m), pl.ds(m, m)
    came(4, a1f.at[0])
    came(5, a1f.at[1])
    a2[...] = found[:, x, :, :h] + a1f[0] + a1f[1]
    go(8, a2.at[yf, top], a2h.at[0], along_y(yu))
    go(9, a2.at[yf, bottom], a2h.at[1], along_y(yd))
    came(6, b1f.at[0])
    came(7, b1f.at[1])
    b2[...] = found[y, :, :, h:] + b1f[0] + b1f[1]
    go(10, b2.at[xf, top], b2h.at[0], along_x(xu))
    go(11, b2.at[xf, bottom], b2h.at[1], along_x(xd))
    came(8, a2h.at[0])
    a2s[0, :m] = a2[yu, :m] + a2h[0]
    a2s[0, m:] = a2[yu, m:]
    go(12, a2s.at[0], a2f.at[0], along_y(yu))
    came(9, a2h.at[1])
    a2s[1, :m] = a2[yd, :m]
    a2s[1, m:] = a2[yd, m:] + a2h[1]
    go(13, a2s.at[1], a2f.at[1], along_y(yd))
    came(10, b2h.at[0])
    b2s[0, :m] = b2[xu, :m] + b2h[0]
    b2s[0, m:] = b2[xu, m:]
    go(14, b2s.at[0], b2f.at[0], along_x(xu))
    came(11, b2h.at[1])
    b2s[1, :m] = b2[xd, :m]
    b2s[1, m:] = b2[xd, m:] + b2h[1]
    go(15, b2s.at[1], b2f.at[1], along_x(xd))
    came(12, a2f.at[0])
    came(13, a2f.at[1])
    own[:ROWS, :h] = a2[y] + a2f[0] + a2f[1]
    came(14, b2f.at[0])
    came(15, b2f.at[1])
    own[:ROWS, h:] = b2[x] + b2f[0] + b2f[1]
    for copy in started:
        copy.wait_send()


def dense_kernel(found, own, *rest):
    greet(tok_peers())
    dense_rows(found, own, lambda: None, *rest)


def dense_exchange(found):
    h, m = WIDTH // 2, ROWS // 2
    return pl.pallas_call(
        dense_kernel,
        out_shape=jax.ShapeDtypeStruct((ROWS, WIDTH), BF16),
        in_specs=[VMEM],
        out_specs=VMEM,
        scratch_shapes=[
            pltpu.VMEM((2, 2, ROWS, h), BF16),
            pltpu.VMEM((2, 4, ROWS, h), BF16),
            pltpu.VMEM((2, 4, ROWS, h), BF16),
            pltpu.VMEM((2, 2, ROWS, h), BF16),
            pltpu.VMEM((2, 4, ROWS, h), BF16),
            pltpu.VMEM((2, 4, ROWS, h), BF16),
            pltpu.VMEM((4, ROWS, h), BF16),
            pltpu.VMEM((2, m, h), BF16),
            pltpu.VMEM((2, ROWS, h), BF16),
            pltpu.VMEM((2, ROWS, h), BF16),
            pltpu.VMEM((4, ROWS, h), BF16),
            pltpu.VMEM((2, m, h), BF16),
            pltpu.VMEM((2, ROWS, h), BF16),
            pltpu.VMEM((2, ROWS, h), BF16),
            pltpu.SemaphoreType.DMA((16,)),
            pltpu.SemaphoreType.DMA((16,)),
        ],
        compiler_params=pltpu.CompilerParams(
            collective_id=1, has_side_effects=True, vmem_limit_bytes=40 << 20
        ),
        name="dense_exchange",
    )(found)


def pack_rows(ids, table, packed, spot_row, slot_s):
    t_at = lax.axis_index("tok")
    shape = (ROWS, ROWS)
    sub = lax.broadcasted_iota(jnp.int32, shape, 0)
    lane = lax.broadcasted_iota(jnp.int32, shape, 1)
    vocab_rows = table.shape[0]
    base = (t_at * vocab_rows).astype(F32)
    symbols = ids[...]
    owners = symbols // vocab_rows
    values = symbols.astype(F32)
    begins = (owners * vocab_rows).astype(F32)
    columns = jnp.transpose(values)
    slot = lax.broadcasted_iota(jnp.int32, (SPACE, ROWS), 0).astype(F32)
    ones = jnp.ones((8, ROWS), BF16)
    yes = lambda mask: jnp.where(mask, 1.0, 0.0).astype(BF16)
    for t in range(TOK):
        row, begin = values[t : t + 1], begins[t : t + 1]
        col = jnp.broadcast_to(columns[:, t : t + 1], shape)
        earlier = dot(ones, yes((col == row) & (sub < lane)))
        first = jnp.where(earlier < 0.5, 1.0, 0.0)
        rank = dot(first.astype(BF16), yes((col < row) & (col >= begin)))[0:1]
        mine = (first[0:1] > 0.5) & (begin == base)
        found = jnp.where((slot == rank) & mine, row - base + 1.0, 0.0)
        slot_s[t * SPACE : t * SPACE + SPACE] = jnp.sum(found, axis=1, keepdims=True) - 1.0

        @pl.when(t_at == t)
        def _():
            spot_row[...] = jnp.broadcast_to(begin * (SPACE / vocab_rows) + rank, (8, ROWS))

    step = 256
    for k in range(TOK * SPACE // step):
        rows = pl.ds(k * step, step)
        numbers = lax.broadcasted_iota(jnp.int32, (step, vocab_rows), 1).astype(F32)
        value = dot(yes(numbers == slot_s[rows]), table[...]).astype(BF16)
        many = step // SPACE
        packed[k * many : k * many + many] = value.reshape(many, SPACE, WIDTH)
    return jnp.transpose(spot_row[...])[:, 0:1]


def finish_kernel(writes, made_out, made_att, made_ffn, returned, store, out, shift_att, shift_ffn, store_out):
    step = pl.program_id(0)

    @pl.when(step == 0)
    def _():
        out[...] = made_out[...]
        shift_att[...] = made_att[...]
        shift_ffn[...] = made_ffn[...]

    for k in range(4):
        slot = step * 4 + k
        page = returned[writes[slot]].astype(F32)
        taken = writes[TOK + slot] > 0

        def put(column, value):
            columns = slice(column, column + 128)
            store_out[k, :, columns] = jnp.where(taken, value, store[k, :, columns])

        flat_page(page, put)


def finish(writes, made_out, made_att, made_ffn, returned, store):
    full = lambda *shape: pl.BlockSpec(shape, lambda k, *_: (0,) * len(shape))
    slots = pl.BlockSpec((4, REQ, HIDDEN), lambda k, *_: (k, 0, 0))
    return pl.pallas_call(
        finish_kernel,
        out_shape=tuple(jax.ShapeDtypeStruct(v.shape, v.dtype) for v in (made_out, made_att, made_ffn, store)),
        grid_spec=pltpu.PrefetchScalarGridSpec(
            num_scalar_prefetch=1,
            grid=(4,),
            in_specs=[
                full(ROWS, WIDTH), full(BRANCH, WIDTH), full(BRANCH, WIDTH),
                full(TOK, PAIRS, HEAD, 128), slots,
            ],
            out_specs=(full(ROWS, WIDTH), full(BRANCH, WIDTH), full(BRANCH, WIDTH), slots),
        ),
        name="finish",
    )(writes, made_out, made_att, made_ffn, returned, store)


def dot(a, b):
    return jnp.dot(a, b, preferred_element_type=F32)


def normed_and_step(block, prior, mean, scale, gain):
    normed = (block.astype(F32) - mean) * scale * gain
    row = lax.broadcasted_iota(jnp.int32, (ROWS, WIDTH), 0)
    spread = (
        lax.broadcasted_iota(jnp.int32, (ROWS, BRANCH), 0) // DRAFT
        == lax.broadcasted_iota(jnp.int32, (ROWS, BRANCH), 1)
    )
    carried = dot(spread.astype(BF16), prior)
    before = jnp.where(lax.rem(row, DRAFT) == 0, carried, pltpu.roll(normed, 1, axis=0))
    return normed, before - normed


def kept_row(normed, prior, kept_column):
    column = lax.broadcasted_iota(jnp.int32, (BRANCH, ROWS), 1)
    branch = lax.broadcasted_iota(jnp.int32, (BRANCH, ROWS), 0)
    pick = (column == branch * DRAFT + kept_column - 1) & (kept_column > 0)
    picked = dot(pick.astype(BF16), normed.astype(BF16))
    return jnp.where(kept_column > 0, picked, prior.astype(F32)).astype(BF16)


def head_ones(size):
    return (
        lax.broadcasted_iota(jnp.int32, (size, size), 0) // HEAD
        == lax.broadcasted_iota(jnp.int32, (size, size), 1) // HEAD
    ).astype(BF16)


def per_head(value):
    ones = head_ones(256)
    return jnp.concatenate([dot(value[:, :256], ones), dot(value[:, 256:], ones)], axis=1)


def per_head_fine(value):
    top = value.astype(BF16)
    rest = (value - top.astype(F32)).astype(BF16)
    return per_head(top) + per_head(rest)


def two_heads(page):
    side = lax.broadcasted_iota(jnp.int32, (HEAD, 128), 1) < HEAD
    none = jnp.zeros_like(page)
    return jnp.concatenate([jnp.where(side, page, none), jnp.where(side, none, page)], axis=0)


META = ("slots", TOK), ("sent", TOK), ("owner_of", REQ), ("page_of", BRANCH), ("request_of", BRANCH), ("winner", REQ), ("kept", REQ), ("pick", TOK)


def starts():
    at, result = 0, {}
    for name, count in META:
        result[name] = at
        at += count
    return result


def row_stats(value_ref, mean, scale):
    step = 64

    @pl.loop(0, ROWS // step)
    def _(k):
        rows = pl.ds(pl.multiple_of(k * step, step), step)
        value = value_ref[rows].astype(F32)
        middle = jnp.mean(value, axis=-1, keepdims=True)
        centered = value - middle
        spread = jnp.mean(centered * centered, axis=-1, keepdims=True)
        mean[rows] = middle
        scale[rows] = lax.rsqrt(spread + EPSILON)


def layer_kernel(
    page_ids, counts, kept, crowded, ids, dense_own, prior_att, prior_ffn, scales, blends, narrow, widen, baseline, boost,
    store_w, table_w, attention_w, result_w, lookup_w, gating_w, content_w,
    out, shift_att, shift_ffn, returned, writes,
    meta, store, table, packed, spot_row, slot_s, lsem,
    whole, residuals, results, lookups, gatings, contents, wbuf, part,
    mated, sums, halves, full, rsend, rrecv,
    own, residual, parcels, psend, precv, plocal, gsend, grecv, glocal,
    out_pages, in_pages, tsend, trecv, tlocal, made, bsend, brecv, blocal,
    acc, low, w_s, y_s, p_s, ffn, mean, scale, wsend, wrecv, wlocal, wsem,
):
    base = starts()
    word = lambda name, index: meta[base[name] + index]

    def note(name, index, value):
        meta[base[name] + index] = value

    def when(test, value):
        return jnp.where(test, value, 0)

    def note_slots():
        @pl.loop(0, TOK)
        def _(peer):
            slot, sent = 0, 0
            for q in range(REQ):
                page = page_ids[peer * REQ + q]
                here = (page >> 4) == t
                slot = jnp.maximum(slot, when(here, page & 15))
                sent = jnp.maximum(sent, when(here, 1))
            note("slots", peer, slot)
            note("sent", peer, sent)

    def note_rest():
        for q in range(REQ):
            note("owner_of", q, page_ids[t * REQ + q] >> 4)

        @pl.loop(0, TOK)
        def _(peer):
            pick, source, hit = 0, 0, 0
            for q in range(REQ):
                pick = jnp.maximum(pick, when(word("owner_of", q) == peer, q))
            for group in range(TOK):
                match = when(word("slots", group) == peer, word("sent", group))
                source = jnp.maximum(source, match * group)
                hit = jnp.maximum(hit, match)
            note("pick", peer, pick)
            writes[peer] = source
            writes[TOK + peer] = hit

        @pl.loop(0, BRANCH)
        def _(b):
            end, request, owner = 0, 0, 0
            for q in range(REQ):
                end += counts[t, q]
                request += when(end <= b, 1)
            for q in range(REQ):
                owner += when(request == q, word("owner_of", q))
            note("request_of", b, request)
            note("page_of", b, owner)

        @pl.loop(0, REQ)
        def _(q):
            best = 0
            for b in range(BRANCH):
                score = kept[b] * BRANCH + (BRANCH - 1 - b)
                best = jnp.maximum(best, when(word("request_of", b) == q, score))
            note("winner", q, BRANCH - 1 - (best & 15))
            note("kept", q, best >> 4)

    t, g = lax.axis_index("tok"), lax.axis_index("grp")
    mine = block_of(g)
    bring_table = pltpu.make_async_copy(table_w, table, lsem.at[0])
    bring_store = pltpu.make_async_copy(store_w, store, lsem.at[1])
    bring_table.start()
    bring_store.start()
    greet(tok_peers() + grp_peers())

    def load(k):
        rows = pl.ds(pl.multiple_of(k * WIDTH, WIDTH), WIDTH)
        slot = lax.rem(k, 2)
        return pltpu.make_async_copy(attention_w.at[:, rows], wbuf.at[slot], wsem.at[slot])

    res, look, gat, con = [
        gather_tok(w, views(all_of), wsend.at[k], wrecv.at[k], wlocal.at[k])
        for k, (w, views, all_of) in enumerate(
            (
                (result_w, result_views, results),
                (lookup_w, stack_views, lookups),
                (gating_w, stack_views, gatings),
                (content_w, result_views, contents),
            )
        )
    ]
    res[0]()
    look[0]()
    load(0).start()
    load(1).start()
    bring_table.wait()
    spot = pack_rows(ids, table, packed, spot_row, slot_s)
    keep = pltpu.make_async_copy(packed.at[t], parcels.at[t], plocal)
    keep.start()
    copies = []
    for k in range(1, TOK):
        peer = lax.rem(t + k, TOK)
        copy = remote(packed.at[peer], parcels.at[t], psend.at[k - 1], precv.at[k - 1], {"tok": peer})
        copy.start()
        copies.append(copy)
    con[0]()
    gat[0]()
    note_slots()
    bring_store.wait()

    @pl.loop(0, TOK)
    def _(peer):
        page = store[word("slots", peer)]

        def put(pair, row, value):
            out_pages[peer, pair, pl.ds(row, 16)] = value.astype(BF16)

        pair_page(page, put)

    res[1]()
    look[1]()
    own[ROWS : ROWS + BRANCH] = prior_att[...]
    own[ROWS + BRANCH :] = prior_ffn[...]
    note_rest()
    branch = lax.broadcasted_iota(jnp.int32, (BRANCH, 1), 0)
    kept_column = jnp.zeros((BRANCH, 1), jnp.int32)
    for b in range(BRANCH):
        kept_column = jnp.where(branch == b, kept[b], kept_column)
    slots = lax.broadcasted_iota(jnp.int32, (ROWS, TOK * SPACE), 1)
    choice = (slots == spot.astype(jnp.int32)).astype(BF16)
    keep.wait()
    for k in range(1, TOK):
        origin = lax.rem(t + TOK - k, TOK)
        remote(packed.at[t], parcels.at[origin], psend.at[k - 1], precv.at[k - 1], {"tok": origin}).wait_recv()
    picked = dot(choice, parcels[...].reshape(TOK * SPACE, WIDTH)).astype(BF16)
    own[:ROWS] = jnp.where(crowded[0] > 0, dense_own[...], picked)
    trades = []

    def bring():
        res[2]()
        trades.append(trade_start(out_pages, in_pages, tsend, trecv, tlocal))

    gather_grp(own, whole, gsend, grecv, glocal, [bring, look[2]])
    for copy in copies:
        copy.wait_send()

    row_stats(whole, mean, scale)
    acc[...] = jnp.zeros_like(acc)
    low[...] = jnp.zeros_like(low)
    shape3 = (BRANCH, DRAFT, WIDTH)
    flat = lambda value: value.reshape(ROWS, WIDTH)

    def mix(k):
        load(k).wait()
        columns = block_of(k)
        weights = wbuf.at[lax.rem(k, 2)]
        prior = whole[ROWS : ROWS + BRANCH, columns]
        normed, delta = normed_and_step(whole[:ROWS, columns], prior, mean[...], scale[...], scales[0:1, columns])

        @pl.when(k == g)
        def _():
            shift_att[...] = kept_row(normed, prior, kept_column)

        blend = blends[:, columns]
        for c in range(4):
            acc[c] += dot((normed + delta * blend[c : c + 1]).astype(BF16), weights[c]).reshape(shape3)
        low[...] += dot((normed + delta * blend[4:5]).astype(BF16), narrow[columns])

        @pl.when(k < GRP - 2)
        def _():
            load(k + 2).start()

    pl.loop(0, 4)(mix)
    res[3]()
    pl.loop(4, 8)(mix)
    trade_end(out_pages, in_pages, tsend, trecv, trades[0])

    lowrank = jnp.tanh(low[...]).astype(BF16)
    w_s[...] = jnp.exp(-jnp.exp(baseline[:, mine] + dot(lowrank, widen[...]))).reshape(shape3)
    position = lax.broadcasted_iota(jnp.int32, shape3, 1)
    r3, k3, v3, w3 = acc[0], acc[1], acc[2], w_s[...]
    y_s[...] = per_head_fine(flat(r3) * boost[:, mine] * flat(k3)) * flat(v3)
    p_s[...] = jnp.ones_like(p_s)
    for s in range(DRAFT - 2, -1, -1):
        decay = jnp.where(position > s + 1, p_s[...].reshape(shape3) * w3[:, s + 1 : s + 2], 1.0)
        p_s[...] = decay.reshape(ROWS, WIDTH)
        term = jnp.where(position > s, r3 * decay * k3[:, s : s + 1], 0.0)
        score = per_head(term.reshape(ROWS, WIDTH).astype(BF16)).reshape(shape3)
        y_s[...] += (score * v3[:, s : s + 1]).reshape(ROWS, WIDTH)
    decay = jnp.where(position > 0, p_s[...].reshape(shape3) * w3[:, 0:1], 1.0)
    p_s[...] = flat(r3 * decay)

    @pl.loop(0, BRANCH)
    def _(b):
        rows = pl.ds(pl.multiple_of(b * DRAFT, DRAFT), DRAFT)
        page = in_pages[word("page_of", b)]
        for pair in range(PAIRS):
            lanes = pl.ds(pair * 128, 128)
            y_s[rows, lanes] += dot(p_s[rows, lanes].astype(BF16), two_heads(page[pair]))

    look[3]()
    value = y_s[...]
    centered = value - per_head_fine(value) * (1.0 / HEAD)
    spread = per_head_fine(centered * centered) * (1.0 / HEAD)
    gate = flat(acc[3])
    gate = gate * jax.nn.sigmoid(gate)
    attended = (centered * lax.rsqrt(spread + HEAD_EPSILON) * scales[2:3, mine] * gate).astype(BF16)
    res[4]()
    for y_of in range(4):
        part[:, y_of * 1024 : y_of * 1024 + 1024] = dot(attended, results[y_of]).astype(BF16)

    def states():
        con[2]()
        eye = (
            lax.broadcasted_iota(jnp.int32, (128, 128), 0)
            == lax.broadcasted_iota(jnp.int32, (128, 128), 1)
        )
        spot16 = lax.broadcasted_iota(jnp.int32, (DRAFT, WIDTH), 0)
        side = lax.broadcasted_iota(jnp.int32, (HEAD, 128), 1) < HEAD

        @pl.loop(0, REQ)
        def _(q):
            b = word("winner", q)
            count = word("kept", q)
            live = spot16 < count
            tail = jnp.where(live, w_s[b], 1.0)
            for hop in (1, 2, 4, 8):
                later = pltpu.roll(tail, DRAFT - hop, axis=0)
                tail = tail * jnp.where(spot16 < DRAFT - hop, later, 1.0)
            after = jnp.where(spot16 < DRAFT - 1, pltpu.roll(tail, DRAFT - 1, axis=0), 1.0)
            keys = jnp.where(live, acc[1, b], 0.0) * after
            values = acc[2, b].astype(BF16)
            page = in_pages[word("owner_of", q)]
            for pair in range(PAIRS):
                lanes = slice(pair * 128, pair * 128 + 128)
                fade = jnp.where(eye, tail[0:1, lanes], 0.0)
                left = jnp.concatenate([keys[:, lanes], fade], axis=0).astype(BF16)
                right = jnp.concatenate([values[:, lanes], two_heads(page[pair])], axis=0)
                both = lax.dot_general(left, right, (((0,), (0,)), ((), ())), preferred_element_type=F32)
                made[q, pair] = jnp.where(side, both[:HEAD], both[HEAD:]).astype(BF16)

        @pl.loop(0, TOK)
        def _(peer):
            out_pages[peer] = made[word("pick", peer)]

        trades.append(trade_start(out_pages, returned, bsend, brecv, blocal))

    con[1]()
    total = reduce_grp(part, mated, sums, halves, full, rsend, rrecv, states)
    residual[...] = (own[:ROWS].astype(F32) + total).astype(BF16)
    gather_grp(residual, residuals, gsend, grecv, glocal, [look[4], con[3]])
    row_stats(residuals, mean, scale)
    gat[1]()

    ffn[...] = jnp.zeros_like(ffn)
    gat[2]()

    @pl.loop(0, GRP)
    def _(k):
        columns = block_of(k)
        prior = whole[ROWS + BRANCH :, columns]
        normed, delta = normed_and_step(residuals[:, columns], prior, mean[...], scale[...], scales[1:2, columns])

        @pl.when(k == g)
        def _():
            shift_ffn[...] = kept_row(normed, prior, kept_column)

        blend = blends[:, columns]
        y_of, x_of = k // 2, pl.ds(lax.rem(k, 2) * 2, 2)
        ffn[...] += dot(
            (normed + delta * blend[5:6]).astype(BF16), lookups[y_of, x_of].reshape(WIDTH, KEYS)
        )
        residuals[:, columns] = (normed + delta * blend[6:7]).astype(BF16)

    hidden = jnp.square(jnp.maximum(ffn[...], 0.0)).astype(BF16)
    con[4]()
    for y_of in range(4):
        part[:, y_of * 1024 : y_of * 1024 + 1024] = dot(hidden, contents[y_of]).astype(BF16)

    def pages():
        gat[3]()
        trade_end(out_pages, returned, bsend, brecv, trades[1])

    total = reduce_grp(part, mated, sums, halves, full, rsend, rrecv, pages)
    gat[4]()
    received = jnp.zeros((ROWS, WIDTH), F32)
    for k in range(GRP):
        received += dot(
            residuals[:, k * WIDTH : k * WIDTH + WIDTH],
            gatings[k // 2, k % 2 * 2 : k % 2 * 2 + 2].reshape(WIDTH, WIDTH),
        )
    out[...] = (residual[...].astype(F32) + jax.nn.sigmoid(received) * total).astype(BF16)


def layer(page_ids, counts, kept, crowded, ids, dense_own, prior_att, prior_ffn, scales, blends, narrow, widen, baseline, boost, *weights):
    rows = ROWS + 2 * BRANCH
    wide = lambda *shape: pltpu.VMEM(shape, BF16)
    fine = lambda *shape: pltpu.VMEM(shape, F32)
    dma = lambda *shape: pltpu.SemaphoreType.DMA(shape)
    return pl.pallas_call(
        layer_kernel,
        out_shape=(
            jax.ShapeDtypeStruct((ROWS, WIDTH), BF16),
            jax.ShapeDtypeStruct((BRANCH, WIDTH), BF16),
            jax.ShapeDtypeStruct((BRANCH, WIDTH), BF16),
            jax.ShapeDtypeStruct((TOK, PAIRS, HEAD, 128), BF16),
            jax.ShapeDtypeStruct((2 * TOK,), jnp.int32),
        ),
        in_specs=[pl.BlockSpec(memory_space=pltpu.SMEM)] * 4 + [VMEM] * 10 + [ANY] * 7,
        out_specs=(VMEM, VMEM, VMEM, VMEM, pl.BlockSpec(memory_space=pltpu.SMEM)),
        scratch_shapes=[
            pltpu.SMEM((sum(count for _, count in META),), jnp.int32),
            fine(*weights[0].shape),
            wide(*weights[1].shape),
            wide(TOK, SPACE, WIDTH),
            fine(8, ROWS),
            fine(TOK * SPACE, 1),
            dma(2),
            wide(rows, HIDDEN),
            wide(ROWS, HIDDEN),
            wide(4, WIDTH, 1024),
            wide(4, 4, 256, KEYS),
            wide(4, 4, 256, WIDTH),
            wide(4, KEYS, 1024),
            wide(2, 4, WIDTH, WIDTH),
            wide(ROWS, HIDDEN),
            *REDUCE_SCRATCH,
            wide(rows, WIDTH),
            wide(ROWS, WIDTH),
            wide(TOK, SPACE, WIDTH),
            dma(TOK - 1),
            dma(TOK - 1),
            pltpu.SemaphoreType.DMA,
            dma(9),
            dma(9),
            pltpu.SemaphoreType.DMA,
            wide(TOK, PAIRS, HEAD, 128),
            wide(TOK, PAIRS, HEAD, 128),
            *TRADE_SEMAPHORES,
            wide(REQ, PAIRS, HEAD, 128),
            *TRADE_SEMAPHORES,
            fine(4, BRANCH, DRAFT, WIDTH),
            fine(ROWS, 128),
            fine(BRANCH, DRAFT, WIDTH),
            fine(ROWS, WIDTH),
            fine(ROWS, WIDTH),
            fine(ROWS, KEYS),
            fine(ROWS, 1),
            fine(ROWS, 1),
            dma(4, 16),
            dma(4, 16),
            dma(4),
            dma(2),
        ],
        compiler_params=pltpu.CompilerParams(
            collective_id=2, has_side_effects=True, vmem_limit_bytes=60 << 20
        ),
        cost_estimate=pl.CostEstimate(flops=12 << 30, transcendentals=1 << 20, bytes_accessed=60 << 20),
        name="layer",
    )(page_ids, counts, kept, crowded, ids, dense_own, prior_att, prior_ffn, scales, blends, narrow, widen, baseline, boost, *weights)


def body(
    guess_symbol_ids,
    symbol_vector_lookup,
    prior_attention_normed,
    prior_feedforward_normed,
    layernorm_scales,
    lagged_blend_ratios,
    attention_matrices,
    forgetting_baseline_vector,
    forgetting_narrow_matrix,
    forgetting_widen_matrix,
    diagonal_boost,
    attention_result_matrix,
    feedforward_lookup_matrix,
    feedforward_content_matrix,
    feedforward_gating_matrix,
    memory_matrix_store,
    query_memory_slot,
    candidate_tally_each_query,
    kept_guess_tally,
):
    tok_at = lax.axis_index("tok")
    vocab_rows = symbol_vector_lookup.shape[0]

    ids = guess_symbol_ids.reshape(TOK, ROWS)
    order = jnp.arange(ROWS, dtype=jnp.int32)
    again = (ids[:, :, None] == ids[:, None, :]) & (order[:, None] > order[None, :])
    first = ~jnp.any(again, axis=2)
    shard = (ids // vocab_rows)[:, None, :] == jnp.arange(TOK, dtype=jnp.int32)[None, :, None]
    need = jnp.sum((shard & first[:, None, :]).astype(jnp.int32), axis=2)
    crowded = jnp.max(need) > SPACE

    def dense(_):
        wanted = guess_symbol_ids - tok_at * vocab_rows
        inside = (wanted >= 0) & (wanted < vocab_rows)
        found = jnp.take(symbol_vector_lookup, jnp.clip(wanted, 0, vocab_rows - 1), axis=0)
        found = jnp.where(inside[:, None], found, jnp.zeros((), BF16)).reshape(4, 4, ROWS, WIDTH)
        return dense_exchange(found)

    dense_own = lax.cond(crowded, dense, lambda _: jnp.zeros((ROWS, WIDTH), BF16), 0)

    made_out, made_att, made_ffn, returned, writes = layer(
        query_memory_slot, candidate_tally_each_query, kept_guess_tally,
        crowded.astype(jnp.int32).reshape(1), ids, dense_own,
        prior_attention_normed, prior_feedforward_normed,
        layernorm_scales, lagged_blend_ratios, forgetting_narrow_matrix, forgetting_widen_matrix,
        forgetting_baseline_vector.reshape(1, HIDDEN), diagonal_boost.reshape(1, HIDDEN),
        memory_matrix_store, symbol_vector_lookup, attention_matrices,
        attention_result_matrix, feedforward_lookup_matrix, feedforward_gating_matrix,
        feedforward_content_matrix,
    )
    return finish(writes, made_out, made_att, made_ffn, returned, memory_matrix_store)


def solution(mesh):
    in_specs = (
        P(),
        P("tok", "grp"),
        P("tok", "grp"),
        P("tok", "grp"),
        P(),
        P(),
        P(None, None, "grp"),
        P(),
        P(),
        P(None, "grp"),
        P(),
        P("grp", "tok"),
        P("tok", "grp"),
        P("grp", "tok"),
        P("tok", "grp"),
        P("tok", "grp", None),
        P(),
        P(),
        P("tok"),
    )
    out_specs = (P("tok", "grp"), P("tok", "grp"), P("tok", "grp"), P("tok", "grp", None))
    return jax.shard_map(body, mesh=mesh, in_specs=in_specs, out_specs=out_specs, check_vma=False)
```

```python
import functools

import jax
import jax.numpy as jnp
from jax import lax
from jax.experimental import pallas as pl
from jax.experimental.pallas import tpu as pltpu
from jax.sharding import PartitionSpec as P

HIDDEN = 4096
HEAD = 64
DRAFT = 16
BRANCH = 16
ROWS = BRANCH * DRAFT
WIDTH = 512
TOK = 16
GRP = 8
REQ = 8
PAIRS = 4
KEYS = 896
SPACE = 32
EPSILON = 1e-05
HEAD_EPSILON = 0.00064
F32 = jnp.float32
BF16 = jnp.bfloat16
MESH = pl.DeviceIdType.MESH
ANY = pl.BlockSpec(memory_space=pl.ANY)
VMEM = pl.BlockSpec(memory_space=pltpu.VMEM)


def remote(src, dst, send, recv, device):
    return pltpu.make_async_remote_copy(
        src_ref=src, dst_ref=dst, send_sem=send, recv_sem=recv, device_id=device, device_id_type=MESH
    )


def greet(devices):
    barrier = pltpu.get_barrier_semaphore()
    for device in devices:
        pl.semaphore_signal(barrier, inc=1, device_id=device, device_id_type=MESH)
    pl.semaphore_wait(barrier, len(devices))


def grp_places():
    g = lax.axis_index("grp")
    z, core = g // 2, g % 2
    up = lax.rem(z + 1, 4) * 2 + core
    down = lax.rem(z + 3, 4) * 2 + core
    far = lax.rem(z + 2, 4) * 2 + core
    mate = z * 2 + 1 - core
    return g, up, down, far, mate


def block_of(g):
    return pl.ds(pl.multiple_of(g * WIDTH, WIDTH), WIDTH)


def flip(g):
    return g + 1 - 2 * lax.rem(g, 2)


def gather_grp(own, out, send, recv, local, between=()):
    between = list(between)

    def aside():
        if between:
            between.pop(0)()

    rows = out.shape[0]
    half = rows // 2
    g, up, down, far, mate = grp_places()
    first, last, whole = pl.ds(0, half), pl.ds(half, rows - half), pl.ds(0, rows)
    at = lambda part, g_of: out.at[part, block_of(g_of)]
    keep = pltpu.make_async_copy(own, at(whole, g), local)
    keep.start()
    started = []

    def go(index, src, part, g_of, target):
        copy = remote(src, at(part, g_of), send.at[index], recv.at[index], {"grp": target})
        copy.start()
        started.append(copy)

    def came(index, part, g_of):
        remote(at(part, g_of), at(part, g_of), send.at[index], recv.at[index], {"grp": mate}).wait_recv()

    go(0, own, whole, g, up)
    go(1, own, whole, g, down)
    go(2, own, whole, g, mate)
    aside()
    came(0, whole, down)
    go(3, at(first, down), first, down, up)
    go(5, at(whole, down), whole, down, mate)
    came(1, whole, up)
    go(4, at(last, up), last, up, down)
    go(6, at(whole, up), whole, up, mate)
    aside()
    came(3, first, far)
    go(7, at(first, far), first, far, mate)
    came(4, last, far)
    go(8, at(last, far), last, far, mate)
    came(2, whole, mate)
    came(5, whole, flip(down))
    came(6, whole, flip(up))
    came(7, first, flip(far))
    came(8, last, flip(far))
    while between:
        aside()
    keep.wait()
    for copy in started:
        copy.wait_send()


def reduce_grp(part, mated, sums, halves, full, send, recv, meanwhile=lambda: None):
    g, up, down, far, mate = grp_places()
    half = ROWS // 2
    started = []

    def go(index, src, dst, target):
        copy = remote(src, dst, send.at[index], recv.at[index], {"grp": target})
        copy.start()
        started.append(copy)

    def came(index, dst):
        remote(dst, dst, send.at[index], recv.at[index], {"grp": mate}).wait_recv()

    order = (far, up, down, g)
    for k in range(4):
        go(k, part.at[:, block_of(flip(order[k]))], mated.at[k], mate)

    def own(k):
        return part[:, block_of(order[k])].astype(F32) + mated[k].astype(F32)

    came(0, mated.at[0])
    sums[0] = own(0).astype(BF16)
    go(4, sums.at[0, pl.ds(0, half)], halves.at[0], up)
    go(5, sums.at[0, pl.ds(half, half)], halves.at[1], down)
    came(1, mated.at[1])
    came(4, halves.at[0])
    sums[1, :half] = (own(1)[:half] + halves[0].astype(F32)).astype(BF16)
    sums[1, half:] = own(1)[half:].astype(BF16)
    go(6, sums.at[1], full.at[0], up)
    came(2, mated.at[2])
    came(5, halves.at[1])
    sums[2, :half] = own(2)[:half].astype(BF16)
    sums[2, half:] = (own(2)[half:] + halves[1].astype(F32)).astype(BF16)
    go(7, sums.at[2], full.at[1], down)
    meanwhile()
    came(3, mated.at[3])
    came(6, full.at[0])
    came(7, full.at[1])
    total = own(3) + full[0].astype(F32) + full[1].astype(F32)
    for copy in started:
        copy.wait_send()
    return total


REDUCE_SCRATCH = [
    pltpu.VMEM((4, ROWS, WIDTH), BF16),
    pltpu.VMEM((3, ROWS, WIDTH), BF16),
    pltpu.VMEM((2, ROWS // 2, WIDTH), BF16),
    pltpu.VMEM((2, ROWS, WIDTH), BF16),
    pltpu.SemaphoreType.DMA((8,)),
    pltpu.SemaphoreType.DMA((8,)),
]


def result_views(out):
    cols = lambda x_of: pl.ds(pl.multiple_of(x_of * 256, 256), 256)
    return (
        lambda rows, y_of, x_of: out.at[y_of, rows, cols(x_of)],
        lambda rows, y_of: out.at[y_of, rows],
        lambda rows, x_of: out.at[:, rows, cols(x_of)],
    )


def stack_views(out):
    return (
        lambda rows, y_of, x_of: out.at[y_of, x_of, rows],
        lambda rows, y_of: out.at[y_of, :, rows],
        lambda rows, x_of: out.at[:, x_of, rows],
    )


def gather_tok(own, views, send, recv, local):
    t = lax.axis_index("tok")
    y, x = t // 4, lax.rem(t, 4)
    xu, xd, xf = [lax.rem(x + k, 4) for k in (1, 3, 2)]
    yu, yd, yf = [lax.rem(y + k, 4) for k in (1, 3, 2)]
    along_x = lambda x_of: {"tok": y * 4 + x_of}
    along_y = lambda y_of: {"tok": y_of * 4 + x}
    one, wide, tall = views
    count = own.shape[0]
    f0, f1 = pl.ds(0, count // 2), pl.ds(count // 2, count // 2)
    fa, fb = [pl.ds(f0.start + k * (f0.size // 2), f0.size // 2) for k in (0, 1)]
    la, lb = [pl.ds(f1.start + k * (f1.size // 2), f1.size // 2) for k in (0, 1)]
    started = []

    def go(index, src, dst, target):
        copy = remote(src, dst, send.at[index], recv.at[index], target)
        copy.start()
        started.append(copy)

    def came(index, dst):
        remote(dst, dst, send.at[index], recv.at[index], along_x(xu)).wait_recv()

    keep = pltpu.make_async_copy(own, one(pl.ds(0, count), y, x), local)

    def begin():
        keep.start()
        go(0, own.at[f0], one(f0, y, x), along_x(xu))
        go(1, own.at[f0], one(f0, y, x), along_x(xd))
        go(2, own.at[f1], one(f1, y, x), along_y(yu))
        go(3, own.at[f1], one(f1, y, x), along_y(yd))

    def relay():
        came(0, one(f0, y, xd))
        go(4, one(fa, y, xd), one(fa, y, xd), along_x(xu))
        came(2, one(f1, yd, x))
        go(6, one(la, yd, x), one(la, yd, x), along_y(yu))
        came(1, one(f0, y, xu))
        go(5, one(fb, y, xu), one(fb, y, xu), along_x(xd))
        came(3, one(f1, yu, x))
        go(7, one(lb, yu, x), one(lb, yu, x), along_y(yd))

    def turn():
        keep.wait()
        came(4, one(fa, y, xf))
        came(5, one(fb, y, xf))
        go(8, wide(f0, y), wide(f0, y), along_y(yu))
        go(9, wide(f0, y), wide(f0, y), along_y(yd))
        came(6, one(la, yf, x))
        came(7, one(lb, yf, x))
        go(10, tall(f1, x), tall(f1, x), along_x(xu))
        go(11, tall(f1, x), tall(f1, x), along_x(xd))

    def last():
        came(8, wide(f0, yd))
        go(12, wide(fa, yd), wide(fa, yd), along_y(yu))
        came(10, tall(f1, xd))
        go(14, tall(la, xd), tall(la, xd), along_x(xu))
        came(9, wide(f0, yu))
        go(13, wide(fb, yu), wide(fb, yu), along_y(yd))
        came(11, tall(f1, xu))
        go(15, tall(lb, xu), tall(lb, xu), along_x(xd))

    def end():
        came(12, wide(fa, yf))
        came(13, wide(fb, yf))
        came(14, tall(la, xf))
        came(15, tall(lb, xf))
        for copy in started:
            copy.wait_send()

    return begin, relay, turn, last, end


def grp_peers():
    _, up, down, _, mate = grp_places()
    return [{"grp": up}, {"grp": down}, {"grp": mate}]


def tok_peers():
    t = lax.axis_index("tok")
    return [{"tok": lax.rem(t + k, TOK)} for k in range(1, TOK)]


def page_masks():
    even = lax.rem(lax.broadcasted_iota(jnp.int32, (8, 128), 0), 2) == 0
    left = lax.broadcasted_iota(jnp.int32, (8, 128), 1) < HEAD
    return even, left


def pair_page(page, put):
    even, left = page_masks()
    for block in range(4):
        rows = [[] for _ in range(PAIRS)]
        for group in (2 * block, 2 * block + 1):
            pieces = []
            for m in range(4 * group, 4 * group + 4):
                here = page[:, m * 128 : m * 128 + 128]
                swapped = pltpu.roll(here, HEAD, axis=1)
                pieces += [jnp.where(even, here, swapped), jnp.where(even, swapped, here)]
            turned = jnp.swapaxes(jnp.stack(pieces), 0, 1)
            for pair in range(PAIRS):
                rows[pair].append(jnp.where(left, turned[2 * pair], turned[2 * pair + 1]))
        for pair in range(PAIRS):
            put(pair, 16 * block, jnp.concatenate(rows[pair], axis=0))


def flat_page(page, put):
    even, left = page_masks()
    for group in range(8):
        rows = [page[pair, 8 * group : 8 * group + 8] for pair in range(PAIRS)]
        turned = jnp.swapaxes(jnp.stack([rows[h // 2] for h in range(8)]), 0, 1)
        for m in range(4):
            first, second = turned[2 * m], turned[2 * m + 1]
            swapped_first = pltpu.roll(first, HEAD, axis=1)
            swapped_second = pltpu.roll(second, HEAD, axis=1)
            put(
                (4 * group + m) * 128,
                jnp.where(
                    left,
                    jnp.where(even, first, swapped_first),
                    jnp.where(even, swapped_second, second),
                ),
            )


def trade_start(out_pages, in_pages, send, recv, local):
    t = lax.axis_index("tok")
    keep = pltpu.make_async_copy(out_pages.at[t], in_pages.at[t], local)
    keep.start()
    for k in range(1, TOK):
        peer = lax.rem(t + k, TOK)
        remote(out_pages.at[peer], in_pages.at[t], send.at[k - 1], recv.at[k - 1], {"tok": peer}).start()
    return keep


def trade_end(out_pages, in_pages, send, recv, keep):
    t = lax.axis_index("tok")
    keep.wait()
    for k in range(1, TOK):
        peer = lax.rem(t + k, TOK)
        origin = lax.rem(t + TOK - k, TOK)
        copy = remote(out_pages.at[peer], in_pages.at[origin], send.at[k - 1], recv.at[k - 1], {"tok": peer})
        copy.wait_recv()
        copy.wait_send()


TRADE_SEMAPHORES = [
    pltpu.SemaphoreType.DMA((TOK - 1,)),
    pltpu.SemaphoreType.DMA((TOK - 1,)),
    pltpu.SemaphoreType.DMA,
]


def dense_rows(found, own, begin, a1h, a1s, a1f, b1h, b1s, b1f, a2, a2h, a2s, a2f, b2, b2h, b2s, b2f, xsend, xrecv):
    t = lax.axis_index("tok")
    y, x = t // 4, lax.rem(t, 4)
    xu, xd, xf = [lax.rem(x + k, 4) for k in (1, 3, 2)]
    yu, yd, yf = [lax.rem(y + k, 4) for k in (1, 3, 2)]
    along_x = lambda x_of: {"tok": y * 4 + x_of}
    along_y = lambda y_of: {"tok": y_of * 4 + x}
    started = []

    def go(index, src, dst, target):
        copy = remote(src, dst, xsend.at[index], xrecv.at[index], target)
        copy.start()
        started.append(copy)

    def came(index, dst):
        remote(dst, dst, xsend.at[index], xrecv.at[index], along_x(xu)).wait_recv()

    h = WIDTH // 2
    left, right = pl.ds(0, h), pl.ds(h, h)
    low, high = pl.ds(0, 2), pl.ds(2, 2)
    go(0, found.at[low, xf, :, left], a1h.at[0], along_x(xu))
    go(1, found.at[high, xf, :, left], a1h.at[1], along_x(xd))
    go(2, found.at[yf, low, :, right], b1h.at[0], along_y(yu))
    go(3, found.at[yf, high, :, right], b1h.at[1], along_y(yd))
    begin()
    came(0, a1h.at[0])
    a1s[0, :2] = found[:2, xu, :, :h] + a1h[0]
    a1s[0, 2:] = found[2:, xu, :, :h]
    go(4, a1s.at[0], a1f.at[0], along_x(xu))
    came(1, a1h.at[1])
    a1s[1, :2] = found[:2, xd, :, :h]
    a1s[1, 2:] = found[2:, xd, :, :h] + a1h[1]
    go(5, a1s.at[1], a1f.at[1], along_x(xd))
    came(2, b1h.at[0])
    b1s[0, :2] = found[yu, :2, :, h:] + b1h[0]
    b1s[0, 2:] = found[yu, 2:, :, h:]
    go(6, b1s.at[0], b1f.at[0], along_y(yu))
    came(3, b1h.at[1])
    b1s[1, :2] = found[yd, :2, :, h:]
    b1s[1, 2:] = found[yd, 2:, :, h:] + b1h[1]
    go(7, b1s.at[1], b1f.at[1], along_y(yd))
    m = ROWS // 2
    top, bottom = pl.ds(0, m), pl.ds(m, m)
    came(4, a1f.at[0])
    came(5, a1f.at[1])
    a2[...] = found[:, x, :, :h] + a1f[0] + a1f[1]
    go(8, a2.at[yf, top], a2h.at[0], along_y(yu))
    go(9, a2.at[yf, bottom], a2h.at[1], along_y(yd))
    came(6, b1f.at[0])
    came(7, b1f.at[1])
    b2[...] = found[y, :, :, h:] + b1f[0] + b1f[1]
    go(10, b2.at[xf, top], b2h.at[0], along_x(xu))
    go(11, b2.at[xf, bottom], b2h.at[1], along_x(xd))
    came(8, a2h.at[0])
    a2s[0, :m] = a2[yu, :m] + a2h[0]
    a2s[0, m:] = a2[yu, m:]
    go(12, a2s.at[0], a2f.at[0], along_y(yu))
    came(9, a2h.at[1])
    a2s[1, :m] = a2[yd, :m]
    a2s[1, m:] = a2[yd, m:] + a2h[1]
    go(13, a2s.at[1], a2f.at[1], along_y(yd))
    came(10, b2h.at[0])
    b2s[0, :m] = b2[xu, :m] + b2h[0]
    b2s[0, m:] = b2[xu, m:]
    go(14, b2s.at[0], b2f.at[0], along_x(xu))
    came(11, b2h.at[1])
    b2s[1, :m] = b2[xd, :m]
    b2s[1, m:] = b2[xd, m:] + b2h[1]
    go(15, b2s.at[1], b2f.at[1], along_x(xd))
    came(12, a2f.at[0])
    came(13, a2f.at[1])
    own[:ROWS, :h] = a2[y] + a2f[0] + a2f[1]
    came(14, b2f.at[0])
    came(15, b2f.at[1])
    own[:ROWS, h:] = b2[x] + b2f[0] + b2f[1]
    for copy in started:
        copy.wait_send()


def dense_kernel(found, own, *rest):
    greet(tok_peers())
    dense_rows(found, own, lambda: None, *rest)


def dense_exchange(found):
    h, m = WIDTH // 2, ROWS // 2
    return pl.pallas_call(
        dense_kernel,
        out_shape=jax.ShapeDtypeStruct((ROWS, WIDTH), BF16),
        in_specs=[VMEM],
        out_specs=VMEM,
        scratch_shapes=[
            pltpu.VMEM((2, 2, ROWS, h), BF16),
            pltpu.VMEM((2, 4, ROWS, h), BF16),
            pltpu.VMEM((2, 4, ROWS, h), BF16),
            pltpu.VMEM((2, 2, ROWS, h), BF16),
            pltpu.VMEM((2, 4, ROWS, h), BF16),
            pltpu.VMEM((2, 4, ROWS, h), BF16),
            pltpu.VMEM((4, ROWS, h), BF16),
            pltpu.VMEM((2, m, h), BF16),
            pltpu.VMEM((2, ROWS, h), BF16),
            pltpu.VMEM((2, ROWS, h), BF16),
            pltpu.VMEM((4, ROWS, h), BF16),
            pltpu.VMEM((2, m, h), BF16),
            pltpu.VMEM((2, ROWS, h), BF16),
            pltpu.VMEM((2, ROWS, h), BF16),
            pltpu.SemaphoreType.DMA((16,)),
            pltpu.SemaphoreType.DMA((16,)),
        ],
        compiler_params=pltpu.CompilerParams(
            collective_id=1, has_side_effects=True, vmem_limit_bytes=40 << 20
        ),
        name="dense_exchange",
    )(found)


def pack_rows(ids, table, packed, spot_row, slot_s):
    t_at = lax.axis_index("tok")
    shape = (ROWS, ROWS)
    sub = lax.broadcasted_iota(jnp.int32, shape, 0)
    lane = lax.broadcasted_iota(jnp.int32, shape, 1)
    vocab_rows = table.shape[0]
    base = (t_at * vocab_rows).astype(F32)
    symbols = ids[...]
    owners = symbols // vocab_rows
    values = symbols.astype(F32)
    begins = (owners * vocab_rows).astype(F32)
    columns = jnp.transpose(values)
    slot = lax.broadcasted_iota(jnp.int32, (SPACE, ROWS), 0).astype(F32)
    ones = jnp.ones((8, ROWS), BF16)
    yes = lambda mask: jnp.where(mask, 1.0, 0.0).astype(BF16)
    for t in range(TOK):
        row, begin = values[t : t + 1], begins[t : t + 1]
        col = jnp.broadcast_to(columns[:, t : t + 1], shape)
        earlier = dot(ones, yes((col == row) & (sub < lane)))
        first = jnp.where(earlier < 0.5, 1.0, 0.0)
        rank = dot(first.astype(BF16), yes((col < row) & (col >= begin)))[0:1]
        mine = (first[0:1] > 0.5) & (begin == base)
        found = jnp.where((slot == rank) & mine, row - base + 1.0, 0.0)
        slot_s[t * SPACE : t * SPACE + SPACE] = jnp.sum(found, axis=1, keepdims=True) - 1.0

        @pl.when(t_at == t)
        def _():
            spot_row[...] = jnp.broadcast_to(begin * (SPACE / vocab_rows) + rank, (8, ROWS))

    step = 256
    for k in range(TOK * SPACE // step):
        rows = pl.ds(k * step, step)
        numbers = lax.broadcasted_iota(jnp.int32, (step, vocab_rows), 1).astype(F32)
        value = dot(yes(numbers == slot_s[rows]), table[...]).astype(BF16)
        many = step // SPACE
        packed[k * many : k * many + many] = value.reshape(many, SPACE, WIDTH)
    return jnp.transpose(spot_row[...])[:, 0:1]


def finish_kernel(writes, made_out, made_att, made_ffn, pages, store, out, shift_att, shift_ffn, store_out):
    step = pl.program_id(0)

    @pl.when(step == 0)
    def _():
        out[...] = made_out[...]
        shift_att[...] = made_att[...]
        shift_ffn[...] = made_ffn[...]

    for k in range(4):
        slot = step * 4 + k
        store_out[k] = jnp.where(writes[TOK + slot] > 0, pages[k].astype(F32), store[k])


def finish(writes, made_out, made_att, made_ffn, returned, store):
    full = lambda *shape: pl.BlockSpec(shape, lambda k, *_: (0,) * len(shape))
    slots = pl.BlockSpec((4, REQ, HIDDEN), lambda k, *_: (k, 0, 0))
    return pl.pallas_call(
        finish_kernel,
        out_shape=tuple(jax.ShapeDtypeStruct(v.shape, v.dtype) for v in (made_out, made_att, made_ffn, store)),
        grid_spec=pltpu.PrefetchScalarGridSpec(
            num_scalar_prefetch=1,
            grid=(4,),
            in_specs=[
                full(ROWS, WIDTH), full(BRANCH, WIDTH), full(BRANCH, WIDTH),
                slots, slots,
            ],
            out_specs=(full(ROWS, WIDTH), full(BRANCH, WIDTH), full(BRANCH, WIDTH), slots),
        ),
        name="finish",
    )(writes, made_out, made_att, made_ffn, returned, store)


def dot(a, b):
    return jnp.dot(a, b, preferred_element_type=F32)


def normed_and_step(block, prior, mean, scale, gain):
    normed = (block.astype(F32) - mean) * scale * gain
    row = lax.broadcasted_iota(jnp.int32, (ROWS, WIDTH), 0)
    spread = (
        lax.broadcasted_iota(jnp.int32, (ROWS, BRANCH), 0) // DRAFT
        == lax.broadcasted_iota(jnp.int32, (ROWS, BRANCH), 1)
    )
    carried = dot(spread.astype(BF16), prior)
    before = jnp.where(lax.rem(row, DRAFT) == 0, carried, pltpu.roll(normed, 1, axis=0))
    return normed, before - normed


def kept_row(normed, prior, kept_column):
    column = lax.broadcasted_iota(jnp.int32, (BRANCH, ROWS), 1)
    branch = lax.broadcasted_iota(jnp.int32, (BRANCH, ROWS), 0)
    pick = (column == branch * DRAFT + kept_column - 1) & (kept_column > 0)
    picked = dot(pick.astype(BF16), normed.astype(BF16))
    return jnp.where(kept_column > 0, picked, prior.astype(F32)).astype(BF16)


def head_ones(size):
    return (
        lax.broadcasted_iota(jnp.int32, (size, size), 0) // HEAD
        == lax.broadcasted_iota(jnp.int32, (size, size), 1) // HEAD
    ).astype(BF16)


def per_head(value):
    ones = head_ones(256)
    return jnp.concatenate([dot(value[:, :256], ones), dot(value[:, 256:], ones)], axis=1)


def per_head_fine(value):
    top = value.astype(BF16)
    rest = (value - top.astype(F32)).astype(BF16)
    return per_head(top) + per_head(rest)


def two_heads(page):
    side = lax.broadcasted_iota(jnp.int32, (HEAD, 128), 1) < HEAD
    none = jnp.zeros_like(page)
    return jnp.concatenate([jnp.where(side, page, none), jnp.where(side, none, page)], axis=0)


META = ("slots", TOK), ("sent", TOK), ("owner_of", REQ), ("page_of", BRANCH), ("request_of", BRANCH), ("winner", REQ), ("kept", REQ), ("pick", TOK)


def starts():
    at, result = 0, {}
    for name, count in META:
        result[name] = at
        at += count
    return result


def row_stats(value_ref, mean, scale):
    step = 64

    @pl.loop(0, ROWS // step)
    def _(k):
        rows = pl.ds(pl.multiple_of(k * step, step), step)
        value = value_ref[rows].astype(F32)
        middle = jnp.mean(value, axis=-1, keepdims=True)
        centered = value - middle
        spread = jnp.mean(centered * centered, axis=-1, keepdims=True)
        mean[rows] = middle
        scale[rows] = lax.rsqrt(spread + EPSILON)


def layer_kernel(
    page_ids, counts, kept, crowded, ids, dense_own, prior_att, prior_ffn, scales, blends, narrow, widen, baseline, boost,
    store_w, table_w, attention_w, result_w, lookup_w, gating_w, content_w,
    out, shift_att, shift_ffn, flat_pages, writes,
    returned, meta, store, table, packed, spot_row, slot_s, lsem,
    whole, residuals, results, lookups, gatings, contents, wbuf, part,
    mated, sums, halves, full, rsend, rrecv,
    own, residual, parcels, psend, precv, plocal, gsend, grecv, glocal,
    out_pages, in_pages, tsend, trecv, tlocal, made, bsend, brecv, blocal,
    acc, low, w_s, y_s, p_s, ffn, mean, scale, wsend, wrecv, wlocal, wsem,
):
    base = starts()
    word = lambda name, index: meta[base[name] + index]

    def note(name, index, value):
        meta[base[name] + index] = value

    def when(test, value):
        return jnp.where(test, value, 0)

    def note_slots():
        @pl.loop(0, TOK)
        def _(peer):
            slot, sent = 0, 0
            for q in range(REQ):
                page = page_ids[peer * REQ + q]
                here = (page >> 4) == t
                slot = jnp.maximum(slot, when(here, page & 15))
                sent = jnp.maximum(sent, when(here, 1))
            note("slots", peer, slot)
            note("sent", peer, sent)

    def note_rest():
        for q in range(REQ):
            note("owner_of", q, page_ids[t * REQ + q] >> 4)

        @pl.loop(0, TOK)
        def _(peer):
            pick, source, hit = 0, 0, 0
            for q in range(REQ):
                pick = jnp.maximum(pick, when(word("owner_of", q) == peer, q))
            for group in range(TOK):
                match = when(word("slots", group) == peer, word("sent", group))
                source = jnp.maximum(source, match * group)
                hit = jnp.maximum(hit, match)
            note("pick", peer, pick)
            writes[peer] = source
            writes[TOK + peer] = hit

        @pl.loop(0, BRANCH)
        def _(b):
            end, request, owner = 0, 0, 0
            for q in range(REQ):
                end += counts[t, q]
                request += when(end <= b, 1)
            for q in range(REQ):
                owner += when(request == q, word("owner_of", q))
            note("request_of", b, request)
            note("page_of", b, owner)

        @pl.loop(0, REQ)
        def _(q):
            best = 0
            for b in range(BRANCH):
                score = kept[b] * BRANCH + (BRANCH - 1 - b)
                best = jnp.maximum(best, when(word("request_of", b) == q, score))
            note("winner", q, BRANCH - 1 - (best & 15))
            note("kept", q, best >> 4)

    t, g = lax.axis_index("tok"), lax.axis_index("grp")
    mine = block_of(g)
    bring_table = pltpu.make_async_copy(table_w, table, lsem.at[0])
    bring_store = pltpu.make_async_copy(store_w, store, lsem.at[1])
    bring_table.start()
    bring_store.start()
    greet(tok_peers() + grp_peers())

    def load(k):
        rows = pl.ds(pl.multiple_of(k * WIDTH, WIDTH), WIDTH)
        slot = lax.rem(k, 2)
        return pltpu.make_async_copy(attention_w.at[:, rows], wbuf.at[slot], wsem.at[slot])

    res, look, gat, con = [
        gather_tok(w, views(all_of), wsend.at[k], wrecv.at[k], wlocal.at[k])
        for k, (w, views, all_of) in enumerate(
            (
                (result_w, result_views, results),
                (lookup_w, stack_views, lookups),
                (gating_w, stack_views, gatings),
                (content_w, result_views, contents),
            )
        )
    ]
    res[0]()
    look[0]()
    load(0).start()
    load(1).start()
    bring_table.wait()
    spot = pack_rows(ids, table, packed, spot_row, slot_s)
    keep = pltpu.make_async_copy(packed.at[t], parcels.at[t], plocal)
    keep.start()
    copies = []
    for k in range(1, TOK):
        peer = lax.rem(t + k, TOK)
        copy = remote(packed.at[peer], parcels.at[t], psend.at[k - 1], precv.at[k - 1], {"tok": peer})
        copy.start()
        copies.append(copy)
    con[0]()
    gat[0]()
    note_slots()
    bring_store.wait()

    @pl.loop(0, TOK)
    def _(peer):
        page = store[word("slots", peer)]

        def put(pair, row, value):
            out_pages[peer, pair, pl.ds(row, 16)] = value.astype(BF16)

        pair_page(page, put)

    res[1]()
    look[1]()
    own[ROWS : ROWS + BRANCH] = prior_att[...]
    own[ROWS + BRANCH :] = prior_ffn[...]
    note_rest()
    branch = lax.broadcasted_iota(jnp.int32, (BRANCH, 1), 0)
    kept_column = jnp.zeros((BRANCH, 1), jnp.int32)
    for b in range(BRANCH):
        kept_column = jnp.where(branch == b, kept[b], kept_column)
    slots = lax.broadcasted_iota(jnp.int32, (ROWS, TOK * SPACE), 1)
    choice = (slots == spot.astype(jnp.int32)).astype(BF16)
    keep.wait()
    for k in range(1, TOK):
        origin = lax.rem(t + TOK - k, TOK)
        remote(packed.at[t], parcels.at[origin], psend.at[k - 1], precv.at[k - 1], {"tok": origin}).wait_recv()
    picked = dot(choice, parcels[...].reshape(TOK * SPACE, WIDTH)).astype(BF16)
    own[:ROWS] = jnp.where(crowded[0] > 0, dense_own[...], picked)
    trades = []

    def bring():
        res[2]()
        trades.append(trade_start(out_pages, in_pages, tsend, trecv, tlocal))

    gather_grp(own, whole, gsend, grecv, glocal, [bring, look[2]])
    for copy in copies:
        copy.wait_send()

    row_stats(whole, mean, scale)
    acc[...] = jnp.zeros_like(acc)
    low[...] = jnp.zeros_like(low)
    shape3 = (BRANCH, DRAFT, WIDTH)
    flat = lambda value: value.reshape(ROWS, WIDTH)

    def mix(k):
        load(k).wait()
        columns = block_of(k)
        weights = wbuf.at[lax.rem(k, 2)]
        prior = whole[ROWS : ROWS + BRANCH, columns]
        normed, delta = normed_and_step(whole[:ROWS, columns], prior, mean[...], scale[...], scales[0:1, columns])

        @pl.when(k == g)
        def _():
            shift_att[...] = kept_row(normed, prior, kept_column)

        blend = blends[:, columns]
        for c in range(4):
            acc[c] += dot((normed + delta * blend[c : c + 1]).astype(BF16), weights[c]).reshape(shape3)
        low[...] += dot((normed + delta * blend[4:5]).astype(BF16), narrow[columns])

        @pl.when(k < GRP - 2)
        def _():
            load(k + 2).start()

    pl.loop(0, 4)(mix)
    res[3]()
    pl.loop(4, 8)(mix)
    trade_end(out_pages, in_pages, tsend, trecv, trades[0])

    lowrank = jnp.tanh(low[...]).astype(BF16)
    w_s[...] = jnp.exp(-jnp.exp(baseline[:, mine] + dot(lowrank, widen[...]))).reshape(shape3)
    position = lax.broadcasted_iota(jnp.int32, shape3, 1)
    r3, k3, v3, w3 = acc[0], acc[1], acc[2], w_s[...]
    y_s[...] = per_head_fine(flat(r3) * boost[:, mine] * flat(k3)) * flat(v3)
    p_s[...] = jnp.ones_like(p_s)
    for s in range(DRAFT - 2, -1, -1):
        decay = jnp.where(position > s + 1, p_s[...].reshape(shape3) * w3[:, s + 1 : s + 2], 1.0)
        p_s[...] = decay.reshape(ROWS, WIDTH)
        term = jnp.where(position > s, r3 * decay * k3[:, s : s + 1], 0.0)
        score = per_head(term.reshape(ROWS, WIDTH).astype(BF16)).reshape(shape3)
        y_s[...] += (score * v3[:, s : s + 1]).reshape(ROWS, WIDTH)
    decay = jnp.where(position > 0, p_s[...].reshape(shape3) * w3[:, 0:1], 1.0)
    p_s[...] = flat(r3 * decay)

    @pl.loop(0, BRANCH)
    def _(b):
        rows = pl.ds(pl.multiple_of(b * DRAFT, DRAFT), DRAFT)
        page = in_pages[word("page_of", b)]
        for pair in range(PAIRS):
            lanes = pl.ds(pair * 128, 128)
            y_s[rows, lanes] += dot(p_s[rows, lanes].astype(BF16), two_heads(page[pair]))

    look[3]()
    value = y_s[...]
    centered = value - per_head_fine(value) * (1.0 / HEAD)
    spread = per_head_fine(centered * centered) * (1.0 / HEAD)
    gate = flat(acc[3])
    gate = gate * jax.nn.sigmoid(gate)
    attended = (centered * lax.rsqrt(spread + HEAD_EPSILON) * scales[2:3, mine] * gate).astype(BF16)
    res[4]()
    for y_of in range(4):
        part[:, y_of * 1024 : y_of * 1024 + 1024] = dot(attended, results[y_of]).astype(BF16)

    def states():
        con[2]()
        eye = (
            lax.broadcasted_iota(jnp.int32, (128, 128), 0)
            == lax.broadcasted_iota(jnp.int32, (128, 128), 1)
        )
        spot16 = lax.broadcasted_iota(jnp.int32, (DRAFT, WIDTH), 0)
        side = lax.broadcasted_iota(jnp.int32, (HEAD, 128), 1) < HEAD

        @pl.loop(0, REQ)
        def _(q):
            b = word("winner", q)
            count = word("kept", q)
            live = spot16 < count
            tail = jnp.where(live, w_s[b], 1.0)
            for hop in (1, 2, 4, 8):
                later = pltpu.roll(tail, DRAFT - hop, axis=0)
                tail = tail * jnp.where(spot16 < DRAFT - hop, later, 1.0)
            after = jnp.where(spot16 < DRAFT - 1, pltpu.roll(tail, DRAFT - 1, axis=0), 1.0)
            keys = jnp.where(live, acc[1, b], 0.0) * after
            values = acc[2, b].astype(BF16)
            page = in_pages[word("owner_of", q)]
            for pair in range(PAIRS):
                lanes = slice(pair * 128, pair * 128 + 128)
                fade = jnp.where(eye, tail[0:1, lanes], 0.0)
                left = jnp.concatenate([keys[:, lanes], fade], axis=0).astype(BF16)
                right = jnp.concatenate([values[:, lanes], two_heads(page[pair])], axis=0)
                both = lax.dot_general(left, right, (((0,), (0,)), ((), ())), preferred_element_type=F32)
                made[q, pair] = jnp.where(side, both[:HEAD], both[HEAD:]).astype(BF16)

        @pl.loop(0, TOK)
        def _(peer):
            out_pages[peer] = made[word("pick", peer)]

        trades.append(trade_start(out_pages, returned, bsend, brecv, blocal))

    con[1]()
    total = reduce_grp(part, mated, sums, halves, full, rsend, rrecv, states)
    residual[...] = (own[:ROWS].astype(F32) + total).astype(BF16)
    gather_grp(residual, residuals, gsend, grecv, glocal, [look[4], con[3]])
    row_stats(residuals, mean, scale)
    gat[1]()

    ffn[...] = jnp.zeros_like(ffn)
    gat[2]()

    @pl.loop(0, GRP)
    def _(k):
        columns = block_of(k)
        prior = whole[ROWS + BRANCH :, columns]
        normed, delta = normed_and_step(residuals[:, columns], prior, mean[...], scale[...], scales[1:2, columns])

        @pl.when(k == g)
        def _():
            shift_ffn[...] = kept_row(normed, prior, kept_column)

        blend = blends[:, columns]
        y_of, x_of = k // 2, pl.ds(lax.rem(k, 2) * 2, 2)
        ffn[...] += dot(
            (normed + delta * blend[5:6]).astype(BF16), lookups[y_of, x_of].reshape(WIDTH, KEYS)
        )
        residuals[:, columns] = (normed + delta * blend[6:7]).astype(BF16)

    hidden = jnp.square(jnp.maximum(ffn[...], 0.0)).astype(BF16)
    con[4]()
    for y_of in range(4):
        part[:, y_of * 1024 : y_of * 1024 + 1024] = dot(hidden, contents[y_of]).astype(BF16)

    def pages():
        gat[3]()
        trade_end(out_pages, returned, bsend, brecv, trades[1])

        @pl.loop(0, TOK)
        def _(slot):
            page = returned[writes[slot]].astype(F32)

            def put(column, value):
                flat_pages[slot, :, pl.ds(column, 128)] = value.astype(BF16)

            flat_page(page, put)

    total = reduce_grp(part, mated, sums, halves, full, rsend, rrecv, pages)
    gat[4]()
    received = jnp.zeros((ROWS, WIDTH), F32)
    for k in range(GRP):
        received += dot(
            residuals[:, k * WIDTH : k * WIDTH + WIDTH],
            gatings[k // 2, k % 2 * 2 : k % 2 * 2 + 2].reshape(WIDTH, WIDTH),
        )
    out[...] = (residual[...].astype(F32) + jax.nn.sigmoid(received) * total).astype(BF16)


def layer(page_ids, counts, kept, crowded, ids, dense_own, prior_att, prior_ffn, scales, blends, narrow, widen, baseline, boost, *weights):
    rows = ROWS + 2 * BRANCH
    wide = lambda *shape: pltpu.VMEM(shape, BF16)
    fine = lambda *shape: pltpu.VMEM(shape, F32)
    dma = lambda *shape: pltpu.SemaphoreType.DMA(shape)
    return pl.pallas_call(
        layer_kernel,
        out_shape=(
            jax.ShapeDtypeStruct((ROWS, WIDTH), BF16),
            jax.ShapeDtypeStruct((BRANCH, WIDTH), BF16),
            jax.ShapeDtypeStruct((BRANCH, WIDTH), BF16),
            jax.ShapeDtypeStruct((TOK, REQ, HIDDEN), BF16),
            jax.ShapeDtypeStruct((2 * TOK,), jnp.int32),
        ),
        in_specs=[pl.BlockSpec(memory_space=pltpu.SMEM)] * 4 + [VMEM] * 10 + [ANY] * 7,
        out_specs=(VMEM, VMEM, VMEM, VMEM, pl.BlockSpec(memory_space=pltpu.SMEM)),
        scratch_shapes=[
            wide(TOK, PAIRS, HEAD, 128),
            pltpu.SMEM((sum(count for _, count in META),), jnp.int32),
            fine(*weights[0].shape),
            wide(*weights[1].shape),
            wide(TOK, SPACE, WIDTH),
            fine(8, ROWS),
            fine(TOK * SPACE, 1),
            dma(2),
            wide(rows, HIDDEN),
            wide(ROWS, HIDDEN),
            wide(4, WIDTH, 1024),
            wide(4, 4, 256, KEYS),
            wide(4, 4, 256, WIDTH),
            wide(4, KEYS, 1024),
            wide(2, 4, WIDTH, WIDTH),
            wide(ROWS, HIDDEN),
            *REDUCE_SCRATCH,
            wide(rows, WIDTH),
            wide(ROWS, WIDTH),
            wide(TOK, SPACE, WIDTH),
            dma(TOK - 1),
            dma(TOK - 1),
            pltpu.SemaphoreType.DMA,
            dma(9),
            dma(9),
            pltpu.SemaphoreType.DMA,
            wide(TOK, PAIRS, HEAD, 128),
            wide(TOK, PAIRS, HEAD, 128),
            *TRADE_SEMAPHORES,
            wide(REQ, PAIRS, HEAD, 128),
            *TRADE_SEMAPHORES,
            fine(4, BRANCH, DRAFT, WIDTH),
            fine(ROWS, 128),
            fine(BRANCH, DRAFT, WIDTH),
            fine(ROWS, WIDTH),
            fine(ROWS, WIDTH),
            fine(ROWS, KEYS),
            fine(ROWS, 1),
            fine(ROWS, 1),
            dma(4, 16),
            dma(4, 16),
            dma(4),
            dma(2),
        ],
        compiler_params=pltpu.CompilerParams(
            collective_id=2, has_side_effects=True, vmem_limit_bytes=60 << 20
        ),
        cost_estimate=pl.CostEstimate(flops=12 << 30, transcendentals=1 << 20, bytes_accessed=60 << 20),
        name="layer",
    )(page_ids, counts, kept, crowded, ids, dense_own, prior_att, prior_ffn, scales, blends, narrow, widen, baseline, boost, *weights)


def body(
    guess_symbol_ids,
    symbol_vector_lookup,
    prior_attention_normed,
    prior_feedforward_normed,
    layernorm_scales,
    lagged_blend_ratios,
    attention_matrices,
    forgetting_baseline_vector,
    forgetting_narrow_matrix,
    forgetting_widen_matrix,
    diagonal_boost,
    attention_result_matrix,
    feedforward_lookup_matrix,
    feedforward_content_matrix,
    feedforward_gating_matrix,
    memory_matrix_store,
    query_memory_slot,
    candidate_tally_each_query,
    kept_guess_tally,
):
    tok_at = lax.axis_index("tok")
    vocab_rows = symbol_vector_lookup.shape[0]

    ids = guess_symbol_ids.reshape(TOK, ROWS)
    order = jnp.arange(ROWS, dtype=jnp.int32)
    again = (ids[:, :, None] == ids[:, None, :]) & (order[:, None] > order[None, :])
    first = ~jnp.any(again, axis=2)
    shard = (ids // vocab_rows)[:, None, :] == jnp.arange(TOK, dtype=jnp.int32)[None, :, None]
    need = jnp.sum((shard & first[:, None, :]).astype(jnp.int32), axis=2)
    crowded = jnp.max(need) > SPACE

    def dense(_):
        wanted = guess_symbol_ids - tok_at * vocab_rows
        inside = (wanted >= 0) & (wanted < vocab_rows)
        found = jnp.take(symbol_vector_lookup, jnp.clip(wanted, 0, vocab_rows - 1), axis=0)
        found = jnp.where(inside[:, None], found, jnp.zeros((), BF16)).reshape(4, 4, ROWS, WIDTH)
        return dense_exchange(found)

    dense_own = lax.cond(crowded, dense, lambda _: jnp.zeros((ROWS, WIDTH), BF16), 0)

    made_out, made_att, made_ffn, returned, writes = layer(
        query_memory_slot, candidate_tally_each_query, kept_guess_tally,
        crowded.astype(jnp.int32).reshape(1), ids, dense_own,
        prior_attention_normed, prior_feedforward_normed,
        layernorm_scales, lagged_blend_ratios, forgetting_narrow_matrix, forgetting_widen_matrix,
        forgetting_baseline_vector.reshape(1, HIDDEN), diagonal_boost.reshape(1, HIDDEN),
        memory_matrix_store, symbol_vector_lookup, attention_matrices,
        attention_result_matrix, feedforward_lookup_matrix, feedforward_gating_matrix,
        feedforward_content_matrix,
    )
    return finish(writes, made_out, made_att, made_ffn, returned, memory_matrix_store)


def solution(mesh):
    in_specs = (
        P(),
        P("tok", "grp"),
        P("tok", "grp"),
        P("tok", "grp"),
        P(),
        P(),
        P(None, None, "grp"),
        P(),
        P(),
        P(None, "grp"),
        P(),
        P("grp", "tok"),
        P("tok", "grp"),
        P("grp", "tok"),
        P("tok", "grp"),
        P("tok", "grp", None),
        P(),
        P(),
        P("tok"),
    )
    out_specs = (P("tok", "grp"), P("tok", "grp"), P("tok", "grp"), P("tok", "grp", None))
    return jax.shard_map(body, mesh=mesh, in_specs=in_specs, out_specs=out_specs, check_vma=False)
```
